128 devices in a mesh: map: 32 (over y, x, core), row: 4 (over z).
Axes of the slice: x: 4, y: 4, z: 4, core: 2. Of those that a mesh axis runs over, the one named last changes fastest.
Arguments:
- block_list: int32 [1024, 3], P(('map', 'row')), may hold values from 0 to 47, as said below
- block_values: bfloat16 [1024, 6, 6, 128], P(('map', 'row')), may hold values from -1.25 to 1.25
- atom_offsets: int32 [32], replicated, may hold values from 0 to 186, as said below
- density: bfloat16 [192, 192], P('row'), may hold values from -2.5 to 2.5
- metric_inverse: bfloat16 [6144, 6144], P('map', 'row'), may hold values from -0.078125 to 0.078125
Outputs:
- exchange_matrix: float32 [192, 192], P('map', 'row')
The draws below stay inside these ranges and needn't reach their ends.
Inputs may be any that keep to these rules, and one draw needn't show every extreme that they name: `block_list`: each row is (mu atom, lambda atom, auxiliary block); no row appears twice. The 8 rows of the device at index r of row name auxiliary blocks r * 12 to (r + 1) * 12 - 1. atom_offsets is 6 times a permutation of the atoms: the atoms' functions tile 0 to 191.
All inputs are finite; a program needn't handle non-finite values.
Results may differ from the reference program's by a relative error of at most 0.0085.
Values may be sent and summed in bfloat16 or wider, within the bound.
A program may use at most 128 MiB of HBM per device.

```python
import jax
import jax.numpy as jnp
from jax import lax

BA = 6
PB = 128
PBLK = 48
ATOM_DEV = 1
BLK_DEV = 8
NATOM = 32
AO = 192
AUX = 6144
PQ = 12
NBLK = 1024
N_ROW = 4


def draw_atom_offsets(key, part):
    shuffled = jax.random.permutation(jax.random.fold_in(key, 11), NATOM)
    return (shuffled * BA).astype(jnp.int32)


def draw_block_list(key, part):
    row_count = PBLK // PQ
    map_count = NBLK // (BLK_DEV * row_count)
    per_row = map_count * BLK_DEV
    combos = NATOM * NATOM * PQ

    def one_row(row_number):
        picked = jax.random.permutation(jax.random.fold_in(key, 100 + row_number), combos)[:per_row]
        local_block = picked // (NATOM * NATOM)
        remain = picked % (NATOM * NATOM)
        first_atom = remain // NATOM
        second_atom = remain % NATOM
        return jnp.stack([first_atom, second_atom, row_number * PQ + local_block], axis=1)
    stacked = jax.vmap(one_row)(jnp.arange(row_count, dtype=jnp.int32))
    arranged = stacked.reshape(row_count, map_count, BLK_DEV, 3).transpose(1, 0, 2, 3).reshape(NBLK, 3)
    return arranged.astype(jnp.int32)


def level_of(stream_key, shape, shards, smallest, high):
    loudness = 1.0
    for position, parts in shards:
        draws = jax.random.uniform(jax.random.fold_in(jax.random.fold_in(stream_key, 6), position), (parts,), jnp.float32, smallest / len(shards), high / len(shards))
        loudness = loudness * jnp.repeat(jnp.exp(draws), shape[position] // parts).reshape((-1,) + (1,) * (len(shape) - 1 - position))
    return loudness


def scatter_about(stream_key, shape, width, most, cuts=(), kind=jnp.bfloat16):
    level = level_of(stream_key, shape, cuts, -0.22, 0.18) if cuts else 1.0
    values = jax.random.normal(stream_key, shape, jnp.float32) * width * level
    return jnp.minimum(jnp.maximum(values, -most), most).astype(kind)


def setup_inputs(seed: int = 0) -> dict:
    keys = jax.random.split(jax.random.key(seed), 6)
    block_list = draw_block_list(jax.random.fold_in(keys[5], 71), 0)
    block_values = scatter_about(keys[1], (NBLK, BA, BA, PB), (1.0 / (BA * PB * BLK_DEV * N_ROW // ATOM_DEV) ** 0.25), 1.25, ((0, 128),))
    atom_offsets = draw_atom_offsets(jax.random.fold_in(keys[5], 71), 0)
    density = scatter_about(keys[3], (AO, AO), BA ** -0.5, 2.5, ((0, 4),))
    metric_inverse = scatter_about(keys[4], (AUX, AUX), AUX ** -0.5, 0.078125, ((0, 32), (1, 4)))
    return {"block_list": block_list, "block_values": block_values, "atom_offsets": atom_offsets, "density": density, "metric_inverse": metric_inverse}


def reference(block_list, block_values, atom_offsets, density, metric_inverse):
    orbitals = NATOM * BA
    aux_total = PBLK * PB
    atom_slots = atom_offsets // BA
    first_slot = jnp.take(atom_slots, block_list[:, 0])
    second_slot = jnp.take(atom_slots, block_list[:, 1])
    target_key = first_slot * PBLK + block_list[:, 2]
    density_rows = jnp.take(density.reshape(NATOM, BA, orbitals), second_slot, axis=0)
    values_wide = block_values.astype(jnp.float32)

    def one_atom(running, column_atom):
        columns = lax.dynamic_slice_in_dim(density_rows, column_atom * BA, BA, 2).astype(jnp.float32)
        partial_value = jnp.einsum("bijc,bjn->binc", values_wide, columns).astype(jnp.bfloat16)
        summed = jax.ops.segment_sum(partial_value.astype(jnp.float32), target_key, NATOM * PBLK)
        half_tensor = summed.reshape(NATOM, PBLK, BA, BA, PB).transpose(0, 2, 3, 1, 4)
        half_tensor = half_tensor.reshape(orbitals * BA, aux_total).astype(jnp.bfloat16)
        fitted = jnp.dot(half_tensor, metric_inverse, preferred_element_type=jnp.float32).astype(jnp.bfloat16)
        chosen = jnp.where((second_slot == column_atom)[:, None, None, None], block_values, jnp.zeros_like(block_values))
        placed = jax.ops.segment_sum(chosen, target_key, NATOM * PBLK)
        tensor_slice = placed.reshape(NATOM, PBLK, BA, BA, PB).transpose(0, 2, 3, 1, 4).reshape(orbitals, BA * aux_total)
        product = lax.dot_general(fitted.reshape(orbitals, BA * aux_total), tensor_slice, (((1,), (1,)), ((), ())), preferred_element_type=jnp.float32)
        return running + product, None

    running, unused = lax.scan(one_atom, jnp.zeros((orbitals, orbitals), jnp.float32), jnp.arange(NATOM, dtype=jnp.int32))
    return running
```

```python
import jax
import jax.numpy as jnp
from jax import lax
from jax.experimental import pallas as pl
from jax.experimental.pallas import tpu as pltpu
from jax.sharding import PartitionSpec as P

HI = lax.Precision.HIGHEST
F32, BF16, I32 = jnp.float32, jnp.bfloat16, jnp.int32
NT = (((1,), (1,)), ((), ()))
GROUP = 32
CHUNK = 16
UNROLL = 8


def iota(shape, axis):
    return lax.broadcasted_iota(I32, shape, axis)


def contract_kernel(codeq, codep, meta, bq, bp, v, dt, out, vp, xbuf, hbuf, dexp, rbuf, ebuf, kbuf):
    parity = meta[35]
    vp[...] = jnp.zeros_like(vp)
    vp[pl.ds(pl.multiple_of(parity * 64, 64), 192), :] = v[...]
    r48, c36 = iota((48, 36), 0), iota((48, 36), 1)
    spread = ((c36 // 6 == r48 % 8) & (c36 % 6 == r48 // 8)).astype(F32).astype(BF16)

    def x_step(step, carry):
        for u in range(UNROLL):
            t = step * UNROLL + u
            code = codeq[t]
            k = code & 255
            q = (code >> 8) & 15
            padded = jnp.dot(spread, bq[k], preferred_element_type=F32).astype(BF16)
            w = vp[:, pl.ds(pl.multiple_of(q * 128, 128), 128)]
            x = lax.dot_general(padded, w, NT, preferred_element_type=F32)
            for j in range(6):
                xbuf[j, t] = x[8 * j:8 * j + 8, :]
        return carry

    lax.fori_loop(0, 256 // UNROLL, x_step, 0)
    kbuf[...] = jnp.zeros_like(kbuf)

    mask = (iota((8, 128), 1) // 6 == iota((8, 128), 0)) & (iota((8, 128), 0) < 6)
    lam, lane = iota((192, 128), 0), iota((192, 128), 1)
    lane_j = lane % 6

    def group(e, base, cnt):
        ebuf[...] = jnp.zeros_like(ebuf)
        rbuf[...] = jnp.zeros_like(rbuf)

        def h_step(t, carry):
            code = codep[base + t]
            k = code & 255
            l = (code >> 8) & 31
            a = (code >> 13) & 31
            sel = (lam == 6 * l + lane_j).astype(F32).astype(BF16)
            dexp[...] = jnp.dot(dt[...], sel, preferred_element_type=F32)
            b = bp[k]
            for c in range(6):
                d = dexp[32 * c:32 * c + 32, :]
                w = jnp.where(mask[None], d[:, None, :], 0.0).reshape(256, 128).astype(BF16)
                h = jnp.dot(w[:, :36], b, preferred_element_type=F32)
                hbuf[32 * c:32 * c + 32, t] = h.reshape(32, 8, 128)
            row, col = iota((8, 256), 0), iota((8, 256), 1)
            ebuf[pl.ds(pl.multiple_of(8 * t, 8), 8), :] = ((col == 6 * a + row) & (row < 6)).astype(F32)
            return carry

        lax.fori_loop(0, cnt, h_step, 0)

        def n_step(n, carry):
            s0, s1 = meta[n], meta[n + 1]

            def c_step(c, carry):
                k0 = s0 + CHUNK * c
                xs, hs = [], []
                for j in range(6):
                    xs.append(xbuf[j, pl.ds(k0, CHUNK), :, pl.ds(pl.multiple_of(e * 128, 128), 128)].reshape(CHUNK * 8, 128).astype(BF16))
                    hs.append(hbuf[n * 6 + j].reshape(GROUP * 8, 128).astype(BF16))
                o = lax.dot_general(jnp.concatenate(xs, axis=1), jnp.concatenate(hs, axis=1), NT, preferred_element_type=F32)
                for t in range(CHUNK):
                    s = jnp.where(k0 + t < s1, (codeq[k0 + t] >> 12) & 31, 32)
                    at = pl.ds(pl.multiple_of(8 * s, 8), 8)
                    rbuf[at, :] += o[8 * t:8 * t + 8, :]
                return carry

            return lax.fori_loop(0, (s1 - s0 + CHUNK - 1) // CHUNK, c_step, carry)

        lax.fori_loop(0, 32, n_step, 0)
        r = jnp.where(iota((256, 256), 1) < 8 * cnt, rbuf[0:256, :], 0.0)
        kbuf[...] += jnp.dot(r, ebuf[...], preferred_element_type=F32, precision=HI)

    n0, n1 = meta[33], meta[34]

    def g_step(g, carry):
        g0 = (n0 + GROUP - 1) // GROUP
        e = (g >= g0).astype(I32)
        first = jnp.where(e == 1, n0, 0)
        left = jnp.where(e == 1, n1, n0) - GROUP * (g - e * g0)
        group(e, first + GROUP * (g - e * g0), jnp.minimum(left, GROUP))
        return carry

    lax.fori_loop(0, (n0 + GROUP - 1) // GROUP + (n1 + GROUP - 1) // GROUP, g_step, 0)
    r, c = iota((256, 192), 0), iota((256, 192), 1)
    squeeze = ((r // 8 == c // 6) & (r % 8 == c % 6)).astype(F32)
    out[...] = jnp.dot(kbuf[...].T, squeeze, preferred_element_type=F32, precision=HI)[:192, :]


def contract(codeq, codep, meta, bq, bp, v, dt):
    smem = pl.BlockSpec(memory_space=pltpu.SMEM)
    vmem = pl.BlockSpec(memory_space=pltpu.VMEM)
    return pl.pallas_call(
        contract_kernel,
        out_shape=jax.ShapeDtypeStruct((192, 192), F32),
        in_specs=[smem] * 3 + [vmem] * 4,
        out_specs=vmem,
        scratch_shapes=[
            pltpu.VMEM((256, 1536), BF16),
            pltpu.VMEM((6, 256 + CHUNK, 8, 256), F32),
            pltpu.VMEM((192, GROUP, 8, 128), F32),
            pltpu.VMEM((192, 128), F32),
            pltpu.VMEM((264, 256), F32),
            pltpu.VMEM((256, 256), F32),
            pltpu.VMEM((256, 256), F32),
        ],
        compiler_params=pltpu.CompilerParams(vmem_limit_bytes=60 << 20),
        name="contract",
    )(codeq, codep, meta, bq, bp, v, dt)


def ranks(key):
    n = key.shape[-1]
    mine, other = key[..., :, None], key[..., None, :]
    at = jnp.arange(n, dtype=I32)
    before = (other < mine) | ((other == mine) & (at[None, :] < at[:, None]))
    return jnp.sum(before.astype(I32), axis=-1)


def tables(listq, listp, slots, first_block, row_start):
    def slot(x):
        return jnp.sum(jnp.where(x[:, None] == jnp.arange(32, dtype=I32), slots, 0), axis=1)
    at = jnp.arange(256, dtype=I32)
    keyq = slot(listq[:, 1])
    codeq = at + ((listq[:, 2] - row_start) << 8) + (slot(listq[:, 0]) << 12)
    p = listp[:, 2] - first_block
    keyp = jnp.where((p == 0) | (p == 1), p, 2)
    codep = at + (slot(listp[:, 1]) << 8) + (slot(listp[:, 0]) << 13)
    key = jnp.stack([keyq, keyp])
    code = jnp.stack([codeq, codep])
    rank = ranks(key)
    ordered = jnp.sum(jnp.where(rank[:, None, :] == at[None, :, None], code[:, None, :], 0), axis=2)
    starts = jnp.sum((keyq[None, :] < jnp.arange(33, dtype=I32)[:, None]).astype(I32), axis=1)
    counts = jnp.sum((keyp[None, :] == jnp.arange(2, dtype=I32)[:, None]).astype(I32), axis=1)
    return jnp.pad(ordered[0], (0, CHUNK)), ordered[1], starts, counts


def body(block_list, block_values, atom_offsets, density, metric_inverse):
    m, r = lax.axis_index("map"), lax.axis_index("row")
    row = m // 8
    lists = lax.all_gather(block_list, ("map", "row"), axis=0).reshape(32, 4, 8, 3)
    values = lax.all_gather(block_values.reshape(8, 36, 128), ("map", "row"), axis=0).reshape(32, 4, 8, 36, 128)
    full = lax.all_gather(density, "row", axis=0, tiled=True)

    def pick(x, at):
        return lax.dynamic_index_in_dim(x, at, 1, keepdims=False).reshape((256,) + x.shape[3:])
    parity = m % 2
    codeq, codep, starts, counts = tables(pick(lists, r), pick(lists, row), atom_offsets // 6, 3 * (m // 2) + parity, r * 12)
    meta = jnp.concatenate([starts, counts, jnp.stack([parity, parity, parity, parity, parity]).astype(I32)])
    part = contract(codeq, codep, meta, pick(values, r), pick(values, row), metric_inverse, full.T)
    by_column = lax.psum_scatter(part, "row", scatter_dimension=1, tiled=True)
    return lax.psum_scatter(by_column, "map", scatter_dimension=0, tiled=True)


def solution(mesh):
    placed = (
        P(("map", "row"), None),
        P(("map", "row"), None, None, None),
        P(),
        P("row", None),
        P("map", "row"),
    )
    return jax.shard_map(
        body, mesh=mesh, in_specs=placed, out_specs=P("map", "row"), check_vma=False
    )
```

```python
import jax
import jax.numpy as jnp
from jax import lax
from jax.experimental import pallas as pl
from jax.experimental.pallas import tpu as pltpu
from jax.sharding import PartitionSpec as P

HI = lax.Precision.HIGHEST
F32, BF16, I32 = jnp.float32, jnp.bfloat16, jnp.int32
NT = (((1,), (1,)), ((), ()))
MESH = pl.DeviceIdType.MESH
GROUP = 32
CHUNK = 16
UNROLL = 8


def iota(shape, axis):
    return lax.broadcasted_iota(I32, shape, axis)


def contract_kernel(codeq, codep, meta, bq, bp, v, dt, out, vp, xbuf, hbuf, dexp, rbuf, ebuf, kbuf):
    parity = meta[35]
    vp[...] = jnp.zeros_like(vp)
    vp[pl.ds(pl.multiple_of(parity * 64, 64), 192), :] = v[...]
    r48, c36 = iota((48, 36), 0), iota((48, 36), 1)
    spread = ((c36 // 6 == r48 % 8) & (c36 % 6 == r48 // 8)).astype(F32).astype(BF16)

    def x_step(step, carry):
        for u in range(UNROLL):
            t = step * UNROLL + u
            code = codeq[t]
            k = code & 255
            q = (code >> 8) & 15
            padded = jnp.dot(spread, bq[k], preferred_element_type=F32).astype(BF16)
            w = vp[:, pl.ds(pl.multiple_of(q * 128, 128), 128)]
            x = lax.dot_general(padded, w, NT, preferred_element_type=F32)
            for j in range(6):
                xbuf[j, t] = x[8 * j:8 * j + 8, :]
        return carry

    lax.fori_loop(0, 256 // UNROLL, x_step, 0)
    kbuf[...] = jnp.zeros_like(kbuf)

    mask = (iota((8, 128), 1) // 6 == iota((8, 128), 0)) & (iota((8, 128), 0) < 6)
    lam, lane = iota((192, 128), 0), iota((192, 128), 1)
    lane_j = lane % 6

    def group(e, base, cnt):
        ebuf[...] = jnp.zeros_like(ebuf)
        rbuf[...] = jnp.zeros_like(rbuf)

        def h_step(t, carry):
            code = codep[base + t]
            k = code & 255
            l = (code >> 8) & 31
            a = (code >> 13) & 31
            sel = (lam == 6 * l + lane_j).astype(F32).astype(BF16)
            dexp[...] = jnp.dot(dt[...], sel, preferred_element_type=F32)
            b = bp[k]
            for c in range(6):
                d = dexp[32 * c:32 * c + 32, :]
                w = jnp.where(mask[None], d[:, None, :], 0.0).reshape(256, 128).astype(BF16)
                h = jnp.dot(w[:, :36], b, preferred_element_type=F32)
                hbuf[32 * c:32 * c + 32, t] = h.reshape(32, 8, 128)
            row, col = iota((8, 256), 0), iota((8, 256), 1)
            ebuf[pl.ds(pl.multiple_of(8 * t, 8), 8), :] = (col == 8 * a + row).astype(F32)
            return carry

        lax.fori_loop(0, cnt, h_step, 0)

        def n_step(n, carry):
            s0, s1 = meta[n], meta[n + 1]

            def c_step(c, carry):
                k0 = s0 + CHUNK * c
                xs, hs = [], []
                for j in range(6):
                    xs.append(xbuf[j, pl.ds(k0, CHUNK), :, pl.ds(pl.multiple_of(e * 128, 128), 128)].reshape(CHUNK * 8, 128).astype(BF16))
                    hs.append(hbuf[n * 6 + j].reshape(GROUP * 8, 128).astype(BF16))
                o = lax.dot_general(jnp.concatenate(xs, axis=1), jnp.concatenate(hs, axis=1), NT, preferred_element_type=F32)
                for t in range(CHUNK):
                    s = jnp.where(k0 + t < s1, (codeq[k0 + t] >> 12) & 31, 32)
                    at = pl.ds(pl.multiple_of(8 * s, 8), 8)
                    rbuf[at, :] += o[8 * t:8 * t + 8, :]
                return carry

            return lax.fori_loop(0, (s1 - s0 + CHUNK - 1) // CHUNK, c_step, carry)

        lax.fori_loop(0, 32, n_step, 0)
        r = jnp.where(iota((256, 256), 1) < 8 * cnt, rbuf[0:256, :], 0.0)
        kbuf[...] += jnp.dot(r, ebuf[...], preferred_element_type=F32, precision=HI)

    n0, n1 = meta[33], meta[34]

    def g_step(g, carry):
        g0 = (n0 + GROUP - 1) // GROUP
        e = (g >= g0).astype(I32)
        first = jnp.where(e == 1, n0, 0)
        left = jnp.where(e == 1, n1, n0) - GROUP * (g - e * g0)
        group(e, first + GROUP * (g - e * g0), jnp.minimum(left, GROUP))
        return carry

    lax.fori_loop(0, (n0 + GROUP - 1) // GROUP + (n1 + GROUP - 1) // GROUP, g_step, 0)
    r, c = iota((256, 256), 0), iota((256, 256), 1)
    squeeze = ((r // 8 == c // 6) & (r % 8 == c % 6)).astype(F32)
    out[...] = jnp.dot(kbuf[...].T, squeeze, preferred_element_type=F32, precision=HI)


def contract(codeq, codep, meta, bq, bp, v, dt):
    smem = pl.BlockSpec(memory_space=pltpu.SMEM)
    vmem = pl.BlockSpec(memory_space=pltpu.VMEM)
    return pl.pallas_call(
        contract_kernel,
        out_shape=jax.ShapeDtypeStruct((256, 256), F32),
        in_specs=[smem] * 3 + [vmem] * 4,
        out_specs=vmem,
        scratch_shapes=[
            pltpu.VMEM((256, 1536), BF16),
            pltpu.VMEM((6, 256 + CHUNK, 8, 256), F32),
            pltpu.VMEM((192, GROUP, 8, 128), F32),
            pltpu.VMEM((192, 128), F32),
            pltpu.VMEM((264, 256), F32),
            pltpu.VMEM((256, 256), F32),
            pltpu.VMEM((256, 256), F32),
        ],
        compiler_params=pltpu.CompilerParams(vmem_limit_bytes=60 << 20),
        name="contract",
    )(codeq, codep, meta, bq, bp, v, dt)


def ranks(key):
    n = key.shape[-1]
    mine, other = key[..., :, None], key[..., None, :]
    at = jnp.arange(n, dtype=I32)
    before = (other < mine) | ((other == mine) & (at[None, :] < at[:, None]))
    return jnp.sum(before.astype(I32), axis=-1)


def tables(listq, listp, slots, first_block, row_start):
    def slot(x):
        return jnp.sum(jnp.where(x[:, None] == jnp.arange(32, dtype=I32), slots, 0), axis=1)
    at = jnp.arange(256, dtype=I32)
    keyq = slot(listq[:, 1])
    codeq = at + ((listq[:, 2] - row_start) << 8) + (slot(listq[:, 0]) << 12)
    p = listp[:, 2] - first_block
    keyp = jnp.where((p == 0) | (p == 1), p, 2)
    codep = at + (slot(listp[:, 1]) << 8) + (slot(listp[:, 0]) << 13)
    key = jnp.stack([keyq, keyp])
    code = jnp.stack([codeq, codep])
    rank = ranks(key)
    ordered = jnp.sum(jnp.where(rank[:, None, :] == at[None, :, None], code[:, None, :], 0), axis=2)
    starts = jnp.sum((keyq[None, :] < jnp.arange(33, dtype=I32)[:, None]).astype(I32), axis=1)
    counts = jnp.sum((keyp[None, :] == jnp.arange(2, dtype=I32)[:, None]).astype(I32), axis=1)
    return jnp.pad(ordered[0], (0, CHUNK)), ordered[1], starts, counts


def place():
    m, z = lax.axis_index("map"), lax.axis_index("row")
    return m, (m // 2) % 4, m // 8, z, m % 2


def at_map(x, y, c):
    return (y * 4 + x) * 2 + c


def greet(devices):
    barrier = pltpu.get_barrier_semaphore()
    for d in devices:
        pl.semaphore_signal(barrier, inc=1, device_id=d, device_id_type=MESH)
    pl.semaphore_wait(barrier, len(devices))


def gather_kernel(own, dens, bq, bp, dout, stage, s_send, s_z, s_d, s_ax, s_ay, s_as, s_by, s_bx, s_bs, s_loc):
    m, x, y, z, c = place()
    way = 1 - 2 * c
    o = 1 - c

    def dev(xx, yy, zz, cc):
        return (at_map(lax.rem(xx + 4, 4), lax.rem(yy + 4, 4), cc), lax.rem(zz + 4, 4))

    def r4(v):
        return lax.rem(v + 8, 4)

    sib = dev(x, y, z, o)
    greet([dev(x + 1, y, z, c), dev(x + 3, y, z, c), dev(x, y + 1, z, c), dev(x, y + 3, z, c), dev(x, y + 2, z, c), dev(x, y, z + 1, c), dev(x, y, z + 3, c), sib])
    sends = []

    def send(src, dst, recv, device):
        n = len(sends)
        d = pltpu.make_async_remote_copy(src_ref=src, dst_ref=dst, send_sem=s_send.at[n], recv_sem=recv, device_id=device, device_id_type=MESH)
        d.start()
        sends.append(d)

    def arrive(dst, recv):
        pltpu.make_async_remote_copy(src_ref=dst, dst_ref=dst, send_sem=s_send.at[0], recv_sem=recv, device_id=sib, device_id_type=MESH).wait_recv()

    def slot(ref, xx, yy, cc=None):
        return ref.at[at_map(r4(xx), r4(yy), c if cc is None else cc)]

    drows = pl.ds(pl.multiple_of(z * 48, 16), 48)
    for s in (1, 3):
        send(own, stage.at[z], s_z.at[z], dev(x, y, z + s, c))
        send(dens, dout.at[z], s_d.at[z], dev(x, y, z + s, c))
    for s in (1, 3):
        send(own, slot(bq, x, y), s_ax.at[x], dev(x + s, y, z, c))
    for s in (1, 3):
        send(own, slot(bq, x, y), s_ay.at[x, y], dev(x, y + s, z, c))
    send(own, slot(bq, x, y), s_as.at[x, y], sib)
    local = [
        pltpu.make_async_copy(own, slot(bq, x, y), s_loc.at[0]),
        pltpu.make_async_copy(own, stage.at[z], s_loc.at[1]),
        pltpu.make_async_copy(dens, dout.at[z], s_loc.at[2]),
    ]
    for d in local:
        d.start()
    zf = r4(z - way)
    arrive(stage.at[zf], s_z.at[zf])
    send(stage.at[zf], stage.at[zf], s_z.at[zf], dev(x, y, z + way, c))
    arrive(dout.at[zf], s_d.at[zf])
    send(dout.at[zf], dout.at[zf], s_d.at[zf], dev(x, y, z + way, c))
    def spread_y(xx):
        for s in (1, 3):
            send(slot(bq, xx, y), slot(bq, xx, y), s_ay.at[r4(xx), y], dev(x, y + s, z, c))
        send(slot(bq, xx, y), slot(bq, xx, y), s_as.at[r4(xx), y], sib)

    xf, xb = r4(x - way), r4(x + way)
    arrive(slot(bq, xf, y), s_ax.at[xf])
    send(slot(bq, xf, y), slot(bq, xf, y), s_ax.at[xf], dev(x + way, y, z, c))
    spread_y(xf)
    arrive(slot(bq, xb, y), s_ax.at[xb])
    spread_y(xb)
    for zz in (r4(z + way), r4(z + 2)):
        arrive(stage.at[zz], s_z.at[zz])
        arrive(dout.at[zz], s_d.at[zz])
    for d in local:
        d.wait()
    for s in (1, 3, 2):
        yt = r4(y + s)
        send(stage.at[yt], slot(bp, x, y), s_by.at[y], dev(x, yt, z, c))
    mine = pltpu.make_async_copy(stage.at[y], slot(bp, x, y), s_loc.at[3])
    mine.start()

    def spread_x(src, yy):
        for s in (1, 3):
            send(src, slot(bp, x, yy), s_bx.at[x, r4(yy)], dev(x + s, y, z, c))
        send(src, slot(bp, x, yy), s_bs.at[x, r4(yy)], sib)

    spread_x(stage.at[y], y)
    x2 = r4(x + 2)
    arrive(slot(bq, x2, y), s_ax.at[x2])
    spread_y(x2)
    for s in (1, 3, 2):
        yy = r4(y + s)
        arrive(slot(bp, x, yy), s_by.at[yy])
        spread_x(slot(bp, x, yy), yy)
    yf = r4(y - way)
    for s, yy in ((0, y), (1, r4(y + 1)), (3, r4(y + 3)), (2, r4(y + 2))):
        xx = r4((x, xf, xb, x2)[(0, 1, 3, 2).index(s)])
        arrive(slot(bq, xx, yf), s_ay.at[xx, yf])
        send(slot(bq, xx, yf), slot(bq, xx, yf), s_ay.at[xx, yf], dev(x, y + way, z, c))
        send(slot(bq, xx, yf), slot(bq, xx, yf), s_as.at[xx, yf], sib)
        arrive(slot(bp, xf, yy), s_bx.at[xf, yy])
        send(slot(bp, xf, yy), slot(bp, xf, yy), s_bx.at[xf, yy], dev(x + way, y, z, c))
        send(slot(bp, xf, yy), slot(bp, xf, yy), s_bs.at[xf, yy], sib)
    yb, y2 = r4(y + way), r4(y + 2)
    for ya, xa in ((yb, xb), (y2, x2)):
        for s in range(4):
            xx, yy = r4(x + s), r4(y + s)
            arrive(slot(bq, xx, ya), s_ay.at[xx, ya])
            send(slot(bq, xx, ya), slot(bq, xx, ya), s_as.at[xx, ya], sib)
            arrive(slot(bp, xa, yy), s_bx.at[xa, yy])
            send(slot(bp, xa, yy), slot(bp, xa, yy), s_bs.at[xa, yy], sib)
    mine.wait()
    for xx in range(4):
        for yy in range(4):
            arrive(slot(bq, xx, yy, o), s_as.at[xx, yy])
            arrive(slot(bp, xx, yy, o), s_bs.at[xx, yy])
    for d in sends:
        d.wait_send()


def gather(own, dens):
    hbm = pl.BlockSpec(memory_space=pl.ANY)
    n, dma = own.shape, pltpu.SemaphoreType.DMA
    return pl.pallas_call(
        gather_kernel,
        out_shape=[
            jax.ShapeDtypeStruct((32,) + n, own.dtype),
            jax.ShapeDtypeStruct((32,) + n, own.dtype),
            jax.ShapeDtypeStruct((4,) + dens.shape, dens.dtype),
            jax.ShapeDtypeStruct((4,) + n, own.dtype),
        ],
        in_specs=[hbm] * 2,
        out_specs=[hbm] * 4,
        scratch_shapes=[dma((72,)), dma((4,)), dma((4,)), dma((4,)), dma((4, 4)), dma((4, 4)), dma((4,)), dma((4, 4)), dma((4, 4)), dma((4,))],
        compiler_params=pltpu.CompilerParams(collective_id=0, has_side_effects=True),
        name="gather",
    )(own, dens)[:3]


def reduce_kernel(part, out, got, cut, got2, send1, recv1, send2, recv2):
    m, x, y, z, c = place()
    g = lax.rem(m, 8)
    near = [(y * 8 + lax.rem(g + d, 8), z) for d in range(1, 8)]
    far = []
    for d in range(1, 16):
        h = lax.rem(y * 4 + z + d, 16)
        far.append((h // 4, lax.rem(h, 4)))
    greet(near + [((yy * 8 + g), zz) for yy, zz in far])
    first = []
    for d in range(1, 8):
        gg = lax.rem(g + d, 8)
        cp = pltpu.make_async_remote_copy(src_ref=part.at[:, gg], dst_ref=got.at[g], send_sem=send1.at[d], recv_sem=recv1.at[g], device_id=near[d - 1], device_id_type=MESH)
        cp.start()
        first.append(cp)
    got[g] = part[:, g]
    cut[...] = jnp.zeros_like(cut)
    for d in range(1, 8):
        gg = lax.rem(g + d, 8)
        pltpu.make_async_remote_copy(src_ref=part.at[:, gg], dst_ref=got.at[gg], send_sem=send1.at[d], recv_sem=recv1.at[gg], device_id=near[0], device_id_type=MESH).wait_recv()
    total = got[0]
    for k in range(1, 8):
        total = total + got[k]
    for zz in range(4):
        cut[:, zz, :, 0:48] = total[:, :, 48 * zz:48 * zz + 48]
    second = []
    for d, (yy, zz) in enumerate(far):
        cp = pltpu.make_async_remote_copy(src_ref=cut.at[yy, zz], dst_ref=got2.at[y, z], send_sem=send2.at[d], recv_sem=recv2.at[y, z], device_id=(yy * 8 + g, zz), device_id_type=MESH)
        cp.start()
        second.append(cp)
    got2[y, z] = cut[y, z]
    for yy, zz in far:
        pltpu.make_async_remote_copy(src_ref=cut.at[yy, zz], dst_ref=got2.at[yy, zz], send_sem=send2.at[0], recv_sem=recv2.at[yy, zz], device_id=(yy * 8 + g, zz), device_id_type=MESH).wait_recv()
    result = got2[0, 0]
    for k in range(1, 16):
        result = result + got2[k // 4, k % 4]
    out[...] = result
    for cp in first + second:
        cp.wait_send()


def reduce(part):
    vmem = pl.BlockSpec(memory_space=pltpu.VMEM)
    dma = pltpu.SemaphoreType.DMA
    return pl.pallas_call(
        reduce_kernel,
        out_shape=jax.ShapeDtypeStruct((8, 128), F32),
        in_specs=[vmem],
        out_specs=vmem,
        scratch_shapes=[
            pltpu.VMEM((8, 4, 8, 256), F32),
            pltpu.VMEM((4, 4, 8, 128), F32),
            pltpu.VMEM((4, 4, 8, 128), F32),
            dma((8,)), dma((8,)), dma((16,)), dma((4, 4)),
        ],
        compiler_params=pltpu.CompilerParams(collective_id=1, has_side_effects=True),
        name="reduce",
    )(part)


def body(block_list, block_values, atom_offsets, density, metric_inverse):
    m, r = lax.axis_index("map"), lax.axis_index("row")
    parity = m % 2
    names = jnp.pad(block_list.astype(BF16), ((0, 0), (0, 125)))
    own = jnp.concatenate([block_values.transpose(1, 2, 0, 3).reshape(36, 8, 128), names[None]], axis=0)
    bq, bp, dens = gather(own, density)

    def lists(b):
        return b[:, 36, :, :3].reshape(256, 3).astype(I32)

    def blocks(b):
        return b[:, :36].transpose(0, 2, 1, 3).reshape(256, 36, 128)
    codeq, codep, starts, counts = tables(lists(bq), lists(bp), atom_offsets // 6, 3 * (m // 2) + parity, r * 12)
    meta = jnp.concatenate([starts, counts, jnp.stack([parity, parity, parity, parity, parity]).astype(I32)])
    part = contract(codeq, codep, meta, blocks(bq), blocks(bp), metric_inverse, dens.reshape(192, 192).T)
    return reduce(part.reshape(4, 8, 8, 256))[:6, :48]


def solution(mesh):
    placed = (
        P(("map", "row"), None),
        P(("map", "row"), None, None, None),
        P(),
        P("row", None),
        P("map", "row"),
    )
    return jax.shard_map(
        body, mesh=mesh, in_specs=placed, out_specs=P("map", "row"), check_vma=False
    )
```

```python
import jax
import jax.numpy as jnp
from jax import lax
from jax.experimental import pallas as pl
from jax.experimental.pallas import tpu as pltpu
from jax.sharding import PartitionSpec as P

HI = lax.Precision.HIGHEST
F32, BF16, I32 = jnp.float32, jnp.bfloat16, jnp.int32
NT = (((1,), (1,)), ((), ()))
MESH = pl.DeviceIdType.MESH
GROUP = 32
CHUNK = 16
XROWS = 44
XUN = 4
HN = 48
NB = 16


def iota(shape, axis):
    return lax.broadcasted_iota(I32, shape, axis)


def contract_kernel(codex, codep, meta, sig, bq, bp_hbm, vt, dexp_hbm, out, xbuf, hbuf, obuf, sbuf, ebuf, kbuf, bp, dexp, s_b, s_d):
    nf, nh = meta[33], meta[34]
    table = pltpu.make_async_copy(dexp_hbm, dexp, s_d.at[0])
    table.start()

    def fetch(t):
        return pltpu.make_async_copy(bp_hbm.at[codep[t] & 255], bp.at[t, 0:48], s_b.at[t])

    def f_step(t, carry):
        fetch(t).start()
        bp[t, 48:64] = jnp.zeros((16, 128), BF16)
        return carry

    lax.fori_loop(0, nf + nh, f_step, 0)
    low_half = iota((8, 128), 1) < 64

    def x_step(step, carry):
        for w in range(XUN):
            ch = XUN * step + w
            src = [codex[8 * ch + u] for u in range(8)]
            rows = jnp.concatenate([bq[s & 255] for s in src], axis=0)
            x = jnp.dot(rows, vt[meta[40 + ch]], preferred_element_type=F32)
            for u in range(8):
                tiles = [x[48 * u + 8 * j:48 * u + 8 * j + 8] for j in range(6)]
                whole = [t[:, :128] for t in tiles]
                half = [jnp.where(low_half, tiles[2 * j][:, 128:], tiles[2 * j + 1][:, 128:]) for j in range(3)]
                xbuf[src[u] >> 8] = jnp.stack(whole + half)
        return carry

    lax.fori_loop(0, (meta[35] + XUN - 1) // XUN, x_step, 0)
    kbuf[...] = jnp.zeros_like(kbuf)
    ebuf[...] = jnp.zeros_like(ebuf)
    sbuf[...] = (iota((256, 2048), 0) == sig[...]).astype(F32).astype(BF16)
    lane, sub = iota((8, 128), 1), iota((8, 128), 0)
    low_mask = (lane % 8 == sub) & (lane < 64)
    high_mask = (lane % 8 == sub) & (lane >= 64)
    row, col = iota((8, 256), 0), iota((8, 256), 1)
    even_device = (iota((64, 128), 0) * 0 + meta[36]) == 0
    left_lanes = iota((64, 128), 1) < 64
    none = jnp.zeros((64, 128), BF16)
    table.wait()

    def w_step(t, carry):
        fetch(t).wait()
        return carry

    lax.fori_loop(0, nf + nh, w_step, 0)

    def spread(ld, nu_a, lb, nu_b):
        a = dexp[ld, pl.ds(nu_a, 8, stride=0), :]
        b = dexp[lb, pl.ds(nu_b, 8, stride=0), :]
        return jnp.where(low_mask, a, jnp.where(high_mask, b, 0.0))

    def pair(h):
        n = h.shape[0] // 8
        both = jnp.concatenate([h[:, :128].reshape(n, 8, 128), h[:, 128:].reshape(n, 8, 128)], axis=1)
        return both.astype(BF16)

    def group(half, base, cnt):
        def h_step(t2, carry):
            at, ls = [], []
            for u in range(2):
                t = base + jnp.minimum(2 * t2 + u, cnt - 1)
                code = codep[t]
                at.append(t)
                ls.append((code >> 8) & 31)
                ebuf[pl.ds(pl.multiple_of(16 * t2 + 8 * u, 8), 8), :] = (col == 8 * (code >> 13) + row).astype(F32)
            b0, b1 = bp[at[0]], bp[at[1]]
            if not half:
                rhs = jnp.concatenate([jnp.concatenate([b0, none], axis=1), jnp.concatenate([none, b1], axis=1)], axis=0)
                for c in range(0, 192, HN):
                    w = jnp.concatenate([spread(ls[0], nu, ls[1], nu) for nu in range(c, c + HN)], axis=0).astype(BF16)
                    hbuf[c:c + HN, t2] = pair(jnp.dot(w, rhs, preferred_element_type=F32))
            else:
                quads = []
                for b in (b0, b1):
                    wide = b.astype(F32)
                    turned = pltpu.roll(wide, 64, 1)
                    first = jnp.where(even_device, wide, turned)
                    second = jnp.where(even_device, turned, wide)
                    quads.append((jnp.where(left_lanes, first, 0.0).astype(BF16), jnp.where(left_lanes, 0.0, second).astype(BF16)))
                (e0, o0), (e1, o1) = quads
                rhs = jnp.concatenate([jnp.concatenate([p, q], axis=1) for p, q in ((e0, none), (o0, none), (none, e1), (none, o1))], axis=0)
                for c in range(0, 96, HN):
                    w = jnp.concatenate([
                        jnp.concatenate([spread(l, 2 * r, l, 2 * r + 1) for r in range(c, c + HN)], axis=0).astype(BF16)
                        for l in ls], axis=1)
                    hbuf[c:c + HN, t2] = pair(jnp.dot(w, rhs, preferred_element_type=F32))
            return carry

        lax.fori_loop(0, (cnt + 1) // 2, h_step, 0)
        depth, first = (3, 6) if half else (6, 0)

        def chunk(n, k0):
            xs = jnp.concatenate([xbuf[pl.ds(k0, CHUNK), first + j].reshape(CHUNK * 8, 128).astype(BF16) for j in range(depth)], axis=1)
            hs = jnp.concatenate([hbuf[n * depth + j].reshape(GROUP * 8, 128) for j in range(depth)], axis=1)
            o = lax.dot_general(xs, hs, NT, preferred_element_type=F32)
            obuf[pl.ds(pl.multiple_of(8 * k0, 8), CHUNK * 8), :] = o

        def n_step(i, carry):
            ends = [meta[NB * i + u] for u in range(NB + 1)]
            for u in range(NB):
                chunk(NB * i + u, ends[u])
            longest = ends[1] - ends[0]
            for u in range(1, NB):
                longest = jnp.maximum(longest, ends[u + 1] - ends[u])

            @pl.when(longest > CHUNK)
            def _():
                def again(n, carry):
                    s0, s1 = meta[n], meta[n + 1]

                    def c_step(c, carry):
                        chunk(n, s0 + CHUNK * c)
                        return carry

                    return lax.fori_loop(0, (s1 - s0 + CHUNK - 1) // CHUNK, c_step, carry)

                lax.fori_loop(NB * i, NB * i + NB, again, 0)
            return carry

        lax.fori_loop(0, 32 // NB, n_step, 0)
        r = jnp.zeros((256, 256), F32)
        for k in range(8):
            o = obuf[256 * k:256 * k + 256, :]
            high = o.astype(BF16)
            low = (o - high.astype(F32)).astype(BF16)
            s = sbuf[:, 256 * k:256 * k + 256]
            r += jnp.dot(s, high, preferred_element_type=F32) + jnp.dot(s, low, preferred_element_type=F32)
        r = jnp.where(iota((256, 256), 1) < 8 * cnt, r, 0.0)
        kbuf[...] += jnp.dot(r, ebuf[...], preferred_element_type=F32, precision=HI)

    for half, base, total in ((False, 0, nf), (True, nf, nh)):
        def g_step(g, carry, half=half, base=base, total=total):
            group(half, base + GROUP * g, jnp.minimum(total - GROUP * g, GROUP))
            return carry

        lax.fori_loop(0, (total + GROUP - 1) // GROUP, g_step, 0)
    out[...] = kbuf[...].T


def contract(codex, codep, meta, sig, bq, bp, vt, dexp):
    smem = pl.BlockSpec(memory_space=pltpu.SMEM)
    vmem = pl.BlockSpec(memory_space=pltpu.VMEM)
    hbm = pl.BlockSpec(memory_space=pl.ANY)
    return pl.pallas_call(
        contract_kernel,
        out_shape=jax.ShapeDtypeStruct((256, 256), F32),
        in_specs=[smem] * 3 + [vmem, vmem, hbm, vmem, hbm],
        out_specs=vmem,
        scratch_shapes=[
            pltpu.VMEM((256 + CHUNK, 9, 8, 128), F32),
            pltpu.VMEM((192, GROUP // 2, 16, 128), BF16),
            pltpu.VMEM(((256 + CHUNK) * 8, 256), F32),
            pltpu.VMEM((256, 2048), BF16),
            pltpu.VMEM((256, 256), F32),
            pltpu.VMEM((256, 256), F32),
            pltpu.VMEM((256, 64, 128), BF16),
            pltpu.VMEM((32, 192, 128), F32),
            pltpu.SemaphoreType.DMA((256,)),
            pltpu.SemaphoreType.DMA((1,)),
        ],
        compiler_params=pltpu.CompilerParams(vmem_limit_bytes=60 << 20),
        name="contract",
    )(codex, codep, meta, sig, bq, bp, vt, dexp)


def tables(listq, listp, slots, whole_block, half_block, row_start, parity):
    at = jnp.arange(256, dtype=I32)

    def slot(x):
        return jnp.sum(jnp.where(x[:, None] == jnp.arange(32, dtype=I32), slots, 0), axis=1)

    def count(keys, upto):
        return jnp.sum((keys[None, :] < upto[:, None]).astype(I32), axis=1)

    def rank(key):
        before = (key[None, :] < key[:, None]) | ((key[None, :] == key[:, None]) & (at[None, :] < at[:, None]))
        return jnp.sum(before.astype(I32), axis=1)

    def place(where, n, code, rest):
        hit = where[None, :] == jnp.arange(n, dtype=I32)[:, None]
        return rest + jnp.sum(jnp.where(hit, code[None, :] - rest, 0), axis=1)

    q = listq[:, 2] - row_start
    by_n = rank(slot(listq[:, 1]))
    starts = count(slot(listq[:, 1]), jnp.arange(33, dtype=I32))
    sig = 6 * place(by_n, 256, slot(listq[:, 0]), 0)[:, None] + jnp.arange(8, dtype=I32)
    sig = jnp.where(jnp.arange(8) < 6, sig, -1).reshape(1, 2048)
    ends = jnp.cumsum((count(q, jnp.arange(1, 13, dtype=I32)) - count(q, jnp.arange(12, dtype=I32)) + 7) // 8)
    lead = 8 * jnp.sum(jnp.where(q[:, None] > jnp.arange(12, dtype=I32), (ends - jnp.concatenate([ends[:1] * 0, ends[:-1]]))[None, :], 0), axis=1)
    within = rank(q) - jnp.sum((q[None, :] < q[:, None]).astype(I32), axis=1)
    codex = place(lead + within, 8 * XROWS, at + (by_n << 8), 256 << 8)
    chunk_q = jnp.minimum(jnp.sum((ends[None, :] <= jnp.arange(XROWS, dtype=I32)[:, None]).astype(I32), axis=1), 11)
    p = listp[:, 2]
    keyp = jnp.where(p == whole_block, 0, jnp.where(p == half_block, 1, 2))
    codep = place(rank(keyp), 256, at + (slot(listp[:, 1]) << 8) + (slot(listp[:, 0]) << 13), 0)
    counts = jnp.stack([jnp.sum((keyp == 0).astype(I32)), jnp.sum((keyp == 1).astype(I32))])
    meta = jnp.concatenate([starts, counts, ends[11:], jnp.stack([parity] * 4).astype(I32), chunk_q])
    return codex, codep, meta, sig


def place():
    m, z = lax.axis_index("map"), lax.axis_index("row")
    return m, (m // 2) % 4, m // 8, z, m % 2


def at_map(x, y, c):
    return (y * 4 + x) * 2 + c


def greet(devices, between=None):
    barrier = pltpu.get_barrier_semaphore()
    for d in devices:
        pl.semaphore_signal(barrier, inc=1, device_id=d, device_id_type=MESH)
    if between is not None:
        between()
    pl.semaphore_wait(barrier, len(devices))


ROWS = 304


def gather_kernel(own, names, dens, v, wide_q, wide_p, names_q, names_p, vt_out, dexp_out, bq, bp, stage, dall, held, vbuf, vt, dexp, wq, wp, spread, s_send, s_z, s_d, s_ax, s_ay, s_as, s_by, s_bx, s_bs, s_loc, s_wq, s_wp):
    m, x, y, z, c = place()
    way = 1 - 2 * c
    o = 1 - c

    def dev(xx, yy, zz, cc):
        return (at_map(lax.rem(xx + 4, 4), lax.rem(yy + 4, 4), cc), lax.rem(zz + 4, 4))

    def r4(v):
        return lax.rem(v + 8, 4)

    def index(xx, yy, cc=None):
        return at_map(r4(xx), r4(yy), c if cc is None else cc)

    sib = dev(x, y, z, o)
    mine_at = index(x, y)
    first = [
        pltpu.make_async_copy(own, bq.at[mine_at, 0:288], s_loc.at[0]),
        pltpu.make_async_copy(names, bq.at[mine_at, 288:304], s_loc.at[1]),
        pltpu.make_async_copy(dens, dall.at[z], s_loc.at[2]),
        pltpu.make_async_copy(v, held, s_loc.at[3]),
    ]
    for d in first:
        d.start()

    def between():
        r, k = iota((384, 288), 0), iota((384, 288), 1)
        block, j, i = r // 48, (r % 48) // 8, r % 8
        spread[...] = ((k % 8 == block) & (k // 8 == i * 6 + j) & (i < 6)).astype(F32).astype(BF16)
        for d in first[:3]:
            d.wait()

    greet([dev(x + 1, y, z, c), dev(x + 3, y, z, c), dev(x, y + 1, z, c), dev(x, y + 3, z, c), dev(x, y + 2, z, c), dev(x, y, z + 1, c), dev(x, y, z + 3, c), sib], between)
    sends = []

    def send(src, dst, recv, device):
        n = len(sends)
        d = pltpu.make_async_remote_copy(src_ref=src, dst_ref=dst, send_sem=s_send.at[n], recv_sem=recv, device_id=device, device_id_type=MESH)
        d.start()
        sends.append(d)

    def arrive(dst, recv):
        pltpu.make_async_remote_copy(src_ref=dst, dst_ref=dst, send_sem=s_send.at[0], recv_sem=recv, device_id=sib, device_id_type=MESH).wait_recv()

    def slot(ref, xx, yy, cc=None):
        return ref.at[index(xx, yy, cc)]

    written = []

    def widen(ref, at, buf, out, sem):
        got = ref[at]
        buf[at] = jnp.dot(spread[...], got[0:288], preferred_element_type=F32).astype(BF16)
        d = pltpu.make_async_copy(buf.at[at], out.at[at], sem.at[at])
        d.start()
        written.append(d)

    def wide_of_q(xx, yy, cc=None):
        widen(bq, index(xx, yy, cc), wq, wide_q, s_wq)

    def wide_of_p(xx, yy, cc=None):
        widen(bp, index(xx, yy, cc), wp, wide_p, s_wp)

    own_piece = slot(bq, x, y)
    for s in (1, 3):
        send(own_piece, stage.at[z], s_z.at[z], dev(x, y, z + s, c))
        send(dall.at[z], dall.at[z], s_d.at[z], dev(x, y, z + s, c))
    for s in (1, 3):
        send(own_piece, own_piece, s_ax.at[x], dev(x + s, y, z, c))
    for s in (1, 3):
        send(own_piece, own_piece, s_ay.at[x, y], dev(x, y + s, z, c))
    send(own_piece, own_piece, s_as.at[x, y], sib)
    keep = pltpu.make_async_copy(own_piece, stage.at[z], s_loc.at[0])
    keep.start()
    wide_of_q(x, y)
    zf = r4(z - way)
    arrive(stage.at[zf], s_z.at[zf])
    send(stage.at[zf], stage.at[zf], s_z.at[zf], dev(x, y, z + way, c))
    arrive(dall.at[zf], s_d.at[zf])
    send(dall.at[zf], dall.at[zf], s_d.at[zf], dev(x, y, z + way, c))

    def spread_y(xx):
        for s in (1, 3):
            send(slot(bq, xx, y), slot(bq, xx, y), s_ay.at[r4(xx), y], dev(x, y + s, z, c))
        send(slot(bq, xx, y), slot(bq, xx, y), s_as.at[r4(xx), y], sib)

    xf, xb = r4(x - way), r4(x + way)
    arrive(slot(bq, xf, y), s_ax.at[xf])
    send(slot(bq, xf, y), slot(bq, xf, y), s_ax.at[xf], dev(x + way, y, z, c))
    spread_y(xf)
    arrive(slot(bq, xb, y), s_ax.at[xb])
    spread_y(xb)
    for zz in (r4(z + way), r4(z + 2)):
        arrive(stage.at[zz], s_z.at[zz])
        arrive(dall.at[zz], s_d.at[zz])
    keep.wait()
    for s in (1, 3, 2):
        yt = r4(y + s)
        send(stage.at[yt], slot(bp, x, y), s_by.at[y], dev(x, yt, z, c))
    mine = pltpu.make_async_copy(stage.at[y], slot(bp, x, y), s_loc.at[1])
    mine.start()

    def spread_x(src, yy):
        for s in (1, 3):
            send(src, slot(bp, x, yy), s_bx.at[x, r4(yy)], dev(x + s, y, z, c))
        send(src, slot(bp, x, yy), s_bs.at[x, r4(yy)], sib)

    spread_x(stage.at[y], y)
    x2 = r4(x + 2)
    arrive(slot(bq, x2, y), s_ax.at[x2])
    spread_y(x2)
    first[3].wait()
    parity = lax.rem(m, 2)
    vbuf[0:128] = held[pl.ds(pl.multiple_of(64 * parity, 64), 128), :]
    half = held[pl.ds(pl.multiple_of(128 * (1 - parity), 64), 64), :]
    vbuf[128:192] = half
    vbuf[192:256] = half
    same = (iota((128, 128), 0) == iota((128, 128), 1)).astype(F32).astype(BF16)
    for q in range(12):
        vt[q] = lax.dot_general(same, vbuf[:, 128 * q:128 * q + 128], NT, preferred_element_type=F32).astype(BF16)
    vt_copy = pltpu.make_async_copy(vt, vt_out, s_loc.at[2])
    vt_copy.start()
    for s in (1, 3, 2):
        yy = r4(y + s)
        arrive(slot(bp, x, yy), s_by.at[yy])
        spread_x(slot(bp, x, yy), yy)
    mine.wait()
    same = (iota((192, 192), 0) == iota((192, 192), 1)).astype(F32).astype(BF16)
    full = jnp.concatenate([dall[k] for k in range(4)], axis=0)
    turned = lax.dot_general(same, full, NT, preferred_element_type=F32).astype(BF16)
    lam, lane = iota((192, 128), 0), iota((192, 128), 1)
    part = (lane % 64) // 8
    for l in range(32):
        sel = ((lam == 6 * l + part) & (part < 6)).astype(F32).astype(BF16)
        dexp[l] = jnp.dot(turned, sel, preferred_element_type=F32)
    dexp_copy = pltpu.make_async_copy(dexp, dexp_out, s_loc.at[0])
    dexp_copy.start()
    for xx in (xf, xb, x2):
        wide_of_q(xx, y)
    yf = r4(y - way)
    for xx, yy in ((x, y), (xf, r4(y + 1)), (xb, r4(y + 3)), (x2, r4(y + 2))):
        arrive(slot(bq, xx, yf), s_ay.at[xx, yf])
        send(slot(bq, xx, yf), slot(bq, xx, yf), s_ay.at[xx, yf], dev(x, y + way, z, c))
        send(slot(bq, xx, yf), slot(bq, xx, yf), s_as.at[xx, yf], sib)
        arrive(slot(bp, xf, yy), s_bx.at[xf, yy])
        send(slot(bp, xf, yy), slot(bp, xf, yy), s_bx.at[xf, yy], dev(x + way, y, z, c))
        send(slot(bp, xf, yy), slot(bp, xf, yy), s_bs.at[xf, yy], sib)
        wide_of_p(x, yy)
        wide_of_q(xx, yf)
        wide_of_p(xf, yy)
    yb, y2 = r4(y + way), r4(y + 2)
    for ya, xa in ((yb, xb), (y2, x2)):
        for s in range(4):
            xx, yy = r4(x + s), r4(y + s)
            arrive(slot(bq, xx, ya), s_ay.at[xx, ya])
            send(slot(bq, xx, ya), slot(bq, xx, ya), s_as.at[xx, ya], sib)
            arrive(slot(bp, xa, yy), s_bx.at[xa, yy])
            send(slot(bp, xa, yy), slot(bp, xa, yy), s_bs.at[xa, yy], sib)
            wide_of_q(xx, ya)
            wide_of_p(xa, yy)
    for xx, xp in ((x, x), (xf, xf), (xb, xb), (x2, x2)):
        for yy in (y, yf, yb, y2):
            arrive(slot(bq, xx, yy, o), s_as.at[xx, yy])
            wide_of_q(xx, yy, o)
            arrive(slot(bp, xx, yy, o), s_bs.at[xx, yy])
            wide_of_p(xx, yy, o)
    last = [
        pltpu.make_async_copy(bq.at[:, 288:304], names_q, s_loc.at[1]),
        pltpu.make_async_copy(bp.at[:, 288:304], names_p, s_loc.at[3]),
    ]
    for d in last:
        d.start()
    for d in written + last + [vt_copy, dexp_copy]:
        d.wait()
    for d in sends:
        d.wait_send()


def gather(own, names, dens, v):
    hbm = pl.BlockSpec(memory_space=pl.ANY)
    dma = pltpu.SemaphoreType.DMA
    return pl.pallas_call(
        gather_kernel,
        out_shape=[
            jax.ShapeDtypeStruct((32, 384, 128), BF16),
            jax.ShapeDtypeStruct((32, 384, 128), BF16),
            jax.ShapeDtypeStruct((32, 16, 128), BF16),
            jax.ShapeDtypeStruct((32, 16, 128), BF16),
            jax.ShapeDtypeStruct((12, 128, 256), BF16),
            jax.ShapeDtypeStruct((32, 192, 128), F32),
        ],
        in_specs=[hbm] * 4,
        out_specs=[hbm] * 6,
        scratch_shapes=[
            pltpu.VMEM((32, ROWS, 128), BF16),
            pltpu.VMEM((32, ROWS, 128), BF16),
            pltpu.VMEM((4, ROWS, 128), BF16),
            pltpu.VMEM((4, 48, 192), BF16),
            pltpu.VMEM((192, 1536), BF16),
            pltpu.VMEM((256, 1536), BF16),
            pltpu.VMEM((12, 128, 256), BF16),
            pltpu.VMEM((32, 192, 128), F32),
            pltpu.VMEM((32, 384, 128), BF16),
            pltpu.VMEM((32, 384, 128), BF16),
            pltpu.VMEM((384, 288), BF16),
            dma((72,)), dma((4,)), dma((4,)), dma((4,)), dma((4, 4)), dma((4, 4)), dma((4,)), dma((4, 4)), dma((4, 4)), dma((4,)), dma((32,)), dma((32,)),
        ],
        compiler_params=pltpu.CompilerParams(collective_id=0, has_side_effects=True, vmem_limit_bytes=48 << 20),
        name="gather",
    )(own, names, dens, v)


def reduce_kernel(part, out, got, cut, got2, send1, recv1, send2, recv2):
    m, x, y, z, c = place()
    g = lax.rem(m, 8)
    near = [(y * 8 + lax.rem(g + d, 8), z) for d in range(1, 8)]
    far = []
    for d in range(1, 16):
        h = lax.rem(y * 4 + z + d, 16)
        far.append((h // 4, lax.rem(h, 4)))
    greet(near + [((yy * 8 + g), zz) for yy, zz in far])
    first = []
    for d in range(1, 8):
        gg = lax.rem(g + d, 8)
        cp = pltpu.make_async_remote_copy(src_ref=part.at[:, gg], dst_ref=got.at[g], send_sem=send1.at[d], recv_sem=recv1.at[g], device_id=near[d - 1], device_id_type=MESH)
        cp.start()
        first.append(cp)
    got[g] = part[:, g]
    cut[...] = jnp.zeros_like(cut)
    for d in range(1, 8):
        gg = lax.rem(g + d, 8)
        pltpu.make_async_remote_copy(src_ref=part.at[:, gg], dst_ref=got.at[gg], send_sem=send1.at[d], recv_sem=recv1.at[gg], device_id=near[0], device_id_type=MESH).wait_recv()
    total = got[0]
    for k in range(1, 8):
        total = total + got[k]
    for zz in range(4):
        cut[:, zz, :, 0:48] = total[:, :, 48 * zz:48 * zz + 48]
    second = []
    for d, (yy, zz) in enumerate(far):
        cp = pltpu.make_async_remote_copy(src_ref=cut.at[yy, zz], dst_ref=got2.at[y, z], send_sem=send2.at[d], recv_sem=recv2.at[y, z], device_id=(yy * 8 + g, zz), device_id_type=MESH)
        cp.start()
        second.append(cp)
    got2[y, z] = cut[y, z]
    for yy, zz in far:
        pltpu.make_async_remote_copy(src_ref=cut.at[yy, zz], dst_ref=got2.at[yy, zz], send_sem=send2.at[0], recv_sem=recv2.at[yy, zz], device_id=(yy * 8 + g, zz), device_id_type=MESH).wait_recv()
    result = got2[0, 0]
    for k in range(1, 16):
        result = result + got2[k // 4, k % 4]
    out[...] = result
    for cp in first + second:
        cp.wait_send()


def reduce(part):
    vmem = pl.BlockSpec(memory_space=pltpu.VMEM)
    dma = pltpu.SemaphoreType.DMA
    return pl.pallas_call(
        reduce_kernel,
        out_shape=jax.ShapeDtypeStruct((8, 128), F32),
        in_specs=[vmem],
        out_specs=vmem,
        scratch_shapes=[
            pltpu.VMEM((8, 4, 8, 256), F32),
            pltpu.VMEM((4, 4, 8, 128), F32),
            pltpu.VMEM((4, 4, 8, 128), F32),
            dma((8,)), dma((8,)), dma((16,)), dma((4, 4)),
        ],
        compiler_params=pltpu.CompilerParams(collective_id=1, has_side_effects=True),
        name="reduce",
    )(part)


def body(block_list, block_values, atom_offsets, density, metric_inverse):
    m, r = lax.axis_index("map"), lax.axis_index("row")
    parity, chip = m % 2, m // 2
    names = jnp.pad(block_list.astype(BF16), ((0, 8), (0, 125)))
    own = block_values.transpose(1, 2, 0, 3).reshape(288, 128)
    bq, bp, names_q, names_p, vt, dexp = gather(own, names, density, metric_inverse)

    def lists(b):
        return b[:, :8, :3].reshape(256, 3).astype(I32)
    codex, codep, meta, sig = tables(lists(names_q), lists(names_p), atom_offsets // 6, 3 * chip + 2 * parity, 3 * chip + 1, r * 12, parity)
    part = contract(codex, codep, meta, sig, bq.reshape(256, 48, 128), bp.reshape(256, 48, 128), vt, dexp)
    return reduce(part.reshape(4, 8, 8, 256))[:6, :48]


def solution(mesh):
    placed = (
        P(("map", "row"), None),
        P(("map", "row"), None, None, None),
        P(),
        P("row", None),
        P("map", "row"),
    )
    return jax.shard_map(
        body, mesh=mesh, in_specs=placed, out_specs=P("map", "row"), check_vma=False
    )
```

```python
import jax
import jax.numpy as jnp
from jax import lax
from jax.experimental import pallas as pl
from jax.experimental.pallas import tpu as pltpu
from jax.sharding import PartitionSpec as P

HI = lax.Precision.HIGHEST
F32, BF16, I32 = jnp.float32, jnp.bfloat16, jnp.int32
NT = (((1,), (1,)), ((), ()))
MESH = pl.DeviceIdType.MESH
GROUP = 32
CHUNK = 16
XROWS = 44
XUN = 4
HN = 48
NB = 16


def iota(shape, axis):
    return lax.broadcasted_iota(I32, shape, axis)


def contract_kernel(codex, codep, meta, sig, bq, bp_hbm, vt, dexp_hbm, out, xbuf, hbuf, obuf, sbuf, ebuf, kbuf, bp, dexp, s_b, s_d):
    nf, nh = meta[33], meta[34]
    table = pltpu.make_async_copy(dexp_hbm, dexp, s_d.at[0])
    table.start()

    def fetch(t):
        return pltpu.make_async_copy(bp_hbm.at[codep[t] & 255], bp.at[t, 0:48], s_b.at[t])

    def f_step(t, carry):
        fetch(t).start()
        bp[t, 48:64] = jnp.zeros((16, 128), BF16)
        return carry

    lax.fori_loop(0, nf + nh, f_step, 0)
    low_half = iota((8, 128), 1) < 64

    def x_step(step, carry):
        for w in range(XUN):
            ch = XUN * step + w
            src = [codex[8 * ch + u] for u in range(8)]
            rows = jnp.concatenate([bq[s & 255] for s in src], axis=0)
            x = jnp.dot(rows, vt[meta[40 + ch]], preferred_element_type=F32)
            for u in range(8):
                tiles = [x[48 * u + 8 * j:48 * u + 8 * j + 8] for j in range(6)]
                whole = [t[:, :128] for t in tiles]
                half = [jnp.where(low_half, tiles[2 * j][:, 128:], tiles[2 * j + 1][:, 128:]) for j in range(3)]
                xbuf[src[u] >> 8] = jnp.stack(whole + half)
        return carry

    lax.fori_loop(0, (meta[35] + XUN - 1) // XUN, x_step, 0)
    kbuf[...] = jnp.zeros_like(kbuf)
    ebuf[...] = jnp.zeros_like(ebuf)
    sbuf[...] = (iota((256, 2048), 0) == sig[...]).astype(F32).astype(BF16)
    lane, sub = iota((8, 128), 1), iota((8, 128), 0)
    low_mask = (lane % 8 == sub) & (lane < 64)
    high_mask = (lane % 8 == sub) & (lane >= 64)
    row, col = iota((8, 256), 0), iota((8, 256), 1)
    even_device = (iota((64, 128), 0) * 0 + meta[36]) == 0
    left_lanes = iota((64, 128), 1) < 64
    none = jnp.zeros((64, 128), BF16)
    table.wait()

    def w_step(t, carry):
        fetch(t).wait()
        return carry

    lax.fori_loop(0, nf + nh, w_step, 0)

    def spread(ld, nu_a, lb, nu_b):
        a = dexp[ld, pl.ds(nu_a, 8, stride=0), :]
        b = dexp[lb, pl.ds(nu_b, 8, stride=0), :]
        return jnp.where(low_mask, a, jnp.where(high_mask, b, 0.0))

    def pair(h):
        n = h.shape[0] // 8
        both = jnp.concatenate([h[:, :128].reshape(n, 8, 128), h[:, 128:].reshape(n, 8, 128)], axis=1)
        return both.astype(BF16)

    def group(half, base, cnt):
        def h_step(t2, carry):
            at, ls = [], []
            for u in range(2):
                t = base + jnp.minimum(2 * t2 + u, cnt - 1)
                code = codep[t]
                at.append(t)
                ls.append((code >> 8) & 31)
                ebuf[pl.ds(pl.multiple_of(16 * t2 + 8 * u, 8), 8), :] = (col == 8 * (code >> 13) + row).astype(F32)
            b0, b1 = bp[at[0]], bp[at[1]]
            if not half:
                rhs = jnp.concatenate([jnp.concatenate([b0, none], axis=1), jnp.concatenate([none, b1], axis=1)], axis=0)
                for c in range(0, 192, HN):
                    w = jnp.concatenate([spread(ls[0], nu, ls[1], nu) for nu in range(c, c + HN)], axis=0).astype(BF16)
                    hbuf[c:c + HN, t2] = pair(jnp.dot(w, rhs, preferred_element_type=F32))
            else:
                quads = []
                for b in (b0, b1):
                    wide = b.astype(F32)
                    turned = pltpu.roll(wide, 64, 1)
                    first = jnp.where(even_device, wide, turned)
                    second = jnp.where(even_device, turned, wide)
                    quads.append((jnp.where(left_lanes, first, 0.0).astype(BF16), jnp.where(left_lanes, 0.0, second).astype(BF16)))
                (e0, o0), (e1, o1) = quads
                rhs = jnp.concatenate([jnp.concatenate([p, q], axis=1) for p, q in ((e0, none), (o0, none), (none, e1), (none, o1))], axis=0)
                for c in range(0, 96, HN):
                    w = jnp.concatenate([
                        jnp.concatenate([spread(l, 2 * r, l, 2 * r + 1) for r in range(c, c + HN)], axis=0).astype(BF16)
                        for l in ls], axis=1)
                    hbuf[c:c + HN, t2] = pair(jnp.dot(w, rhs, preferred_element_type=F32))
            return carry

        lax.fori_loop(0, (cnt + 1) // 2, h_step, 0)
        depth, first = (3, 6) if half else (6, 0)

        def chunk(n, k0):
            xs = jnp.concatenate([xbuf[pl.ds(k0, CHUNK), first + j].reshape(CHUNK * 8, 128).astype(BF16) for j in range(depth)], axis=1)
            hs = jnp.concatenate([hbuf[n * depth + j].reshape(GROUP * 8, 128) for j in range(depth)], axis=1)
            o = lax.dot_general(xs, hs, NT, preferred_element_type=F32)
            obuf[pl.ds(pl.multiple_of(8 * k0, 8), CHUNK * 8), :] = o

        def n_step(i, carry):
            ends = [meta[NB * i + u] for u in range(NB + 1)]
            for u in range(NB):
                chunk(NB * i + u, ends[u])
            longest = ends[1] - ends[0]
            for u in range(1, NB):
                longest = jnp.maximum(longest, ends[u + 1] - ends[u])

            @pl.when(longest > CHUNK)
            def _():
                def again(n, carry):
                    s0, s1 = meta[n], meta[n + 1]

                    def c_step(c, carry):
                        chunk(n, s0 + CHUNK * c)
                        return carry

                    return lax.fori_loop(0, (s1 - s0 + CHUNK - 1) // CHUNK, c_step, carry)

                lax.fori_loop(NB * i, NB * i + NB, again, 0)
            return carry

        lax.fori_loop(0, 32 // NB, n_step, 0)
        r = jnp.zeros((256, 256), F32)
        for k in range(8):
            o = obuf[256 * k:256 * k + 256, :]
            high = o.astype(BF16)
            low = (o - high.astype(F32)).astype(BF16)
            s = sbuf[:, 256 * k:256 * k + 256]
            r += jnp.dot(s, high, preferred_element_type=F32) + jnp.dot(s, low, preferred_element_type=F32)
        r = jnp.where(iota((256, 256), 1) < 8 * cnt, r, 0.0)
        kbuf[...] += jnp.dot(r, ebuf[...], preferred_element_type=F32, precision=HI)

    for half, base, total in ((False, 0, nf), (True, nf, nh)):
        def g_step(g, carry, half=half, base=base, total=total):
            group(half, base + GROUP * g, jnp.minimum(total - GROUP * g, GROUP))
            return carry

        lax.fori_loop(0, (total + GROUP - 1) // GROUP, g_step, 0)
    out[...] = kbuf[...].T


def contract(codex, codep, meta, sig, bq, bp, vt, dexp):
    smem = pl.BlockSpec(memory_space=pltpu.SMEM)
    vmem = pl.BlockSpec(memory_space=pltpu.VMEM)
    hbm = pl.BlockSpec(memory_space=pl.ANY)
    return pl.pallas_call(
        contract_kernel,
        out_shape=jax.ShapeDtypeStruct((256, 256), F32),
        in_specs=[smem] * 3 + [vmem, vmem, hbm, vmem, hbm],
        out_specs=vmem,
        scratch_shapes=[
            pltpu.VMEM((256 + CHUNK, 9, 8, 128), F32),
            pltpu.VMEM((192, GROUP // 2, 16, 128), BF16),
            pltpu.VMEM(((256 + CHUNK) * 8, 256), F32),
            pltpu.VMEM((256, 2048), BF16),
            pltpu.VMEM((256, 256), F32),
            pltpu.VMEM((256, 256), F32),
            pltpu.VMEM((256, 64, 128), BF16),
            pltpu.VMEM((32, 192, 128), F32),
            pltpu.SemaphoreType.DMA((256,)),
            pltpu.SemaphoreType.DMA((1,)),
        ],
        compiler_params=pltpu.CompilerParams(vmem_limit_bytes=60 << 20),
        name="contract",
    )(codex, codep, meta, sig, bq, bp, vt, dexp)


def tables(listq, listp, slots, whole_block, half_block, row_start, parity):
    at = jnp.arange(256, dtype=I32)

    def slot(x):
        return jnp.sum(jnp.where(x[:, None] == jnp.arange(32, dtype=I32), slots, 0), axis=1)

    def count(keys, upto):
        return jnp.sum((keys[None, :] < upto[:, None]).astype(I32), axis=1)

    def rank(key):
        before = (key[None, :] < key[:, None]) | ((key[None, :] == key[:, None]) & (at[None, :] < at[:, None]))
        return jnp.sum(before.astype(I32), axis=1)

    def place(where, n, code, rest):
        hit = where[None, :] == jnp.arange(n, dtype=I32)[:, None]
        return rest + jnp.sum(jnp.where(hit, code[None, :] - rest, 0), axis=1)

    q = listq[:, 2] - row_start
    by_n = rank(slot(listq[:, 1]))
    starts = count(slot(listq[:, 1]), jnp.arange(33, dtype=I32))
    sig = 6 * place(by_n, 256, slot(listq[:, 0]), 0)[:, None] + jnp.arange(8, dtype=I32)
    sig = jnp.where(jnp.arange(8) < 6, sig, -1).reshape(1, 2048)
    ends = jnp.cumsum((count(q, jnp.arange(1, 13, dtype=I32)) - count(q, jnp.arange(12, dtype=I32)) + 7) // 8)
    lead = 8 * jnp.sum(jnp.where(q[:, None] > jnp.arange(12, dtype=I32), (ends - jnp.concatenate([ends[:1] * 0, ends[:-1]]))[None, :], 0), axis=1)
    within = rank(q) - jnp.sum((q[None, :] < q[:, None]).astype(I32), axis=1)
    codex = place(lead + within, 8 * XROWS, at + (by_n << 8), 256 << 8)
    chunk_q = jnp.minimum(jnp.sum((ends[None, :] <= jnp.arange(XROWS, dtype=I32)[:, None]).astype(I32), axis=1), 11)
    p = listp[:, 2]
    keyp = jnp.where(p == whole_block, 0, jnp.where(p == half_block, 1, 2))
    codep = place(rank(keyp), 256, at + (slot(listp[:, 1]) << 8) + (slot(listp[:, 0]) << 13), 0)
    counts = jnp.stack([jnp.sum((keyp == 0).astype(I32)), jnp.sum((keyp == 1).astype(I32))])
    meta = jnp.concatenate([starts, counts, ends[11:], jnp.stack([parity] * 4).astype(I32), chunk_q])
    return codex, codep, meta, sig


ROWS = 304
XDIRECT = True


def place():
    m, z = lax.axis_index("map"), lax.axis_index("row")
    return m, (m // 2) % 4, m // 8, z, m % 2


def at_map(x, y, c):
    return (y * 4 + x) * 2 + c


def greet(devices, between=None):
    barrier = pltpu.get_barrier_semaphore()
    for d in devices:
        pl.semaphore_signal(barrier, inc=1, device_id=d, device_id_type=MESH)
    if between is not None:
        between()
    pl.semaphore_wait(barrier, len(devices))


def gather_kernel(own, names, dens, v, wide_q, wide_p, vt_out, dexp_out, bq, bp, stage, dall, held, vbuf, vt, dexp, wq, wp, spread, s_send, s_z, s_d, s_ax, s_ay, s_as, s_by, s_bx, s_bs, s_loc, s_wq, s_wp):
    m, x, y, z, c = place()
    way = 1 - 2 * c
    o = 1 - c

    def r4(v):
        return lax.rem(v + 8, 4)

    def dev(xx, yy, zz, cc):
        return (at_map(r4(xx), r4(yy), cc), r4(zz))

    sib = dev(x, y, z, o)
    own_piece = bq.at[y, x]
    first = [
        pltpu.make_async_copy(own, bq.at[y, x, 0:288], s_loc.at[0]),
        pltpu.make_async_copy(names, bq.at[y, x, 288:304], s_loc.at[1]),
        pltpu.make_async_copy(dens, dall.at[z], s_loc.at[2]),
        pltpu.make_async_copy(v, held, s_loc.at[3]),
    ]
    for d in first:
        d.start()

    def between():
        r, k = iota((384, 304), 0), iota((384, 304), 1)
        block, j, i = r // 48, (r % 48) // 8, r % 8
        source = jnp.where(i < 6, (i * 6 + j) * 8 + block, jnp.where((i == 6) & (j == 0), 288 + block, -1))
        spread[...] = (k == source).astype(F32).astype(BF16)
        for d in first[:3]:
            d.wait()

    greet([dev(x + s, y, z, c) for s in (1, 2, 3)] + [dev(x, y + s, z, c) for s in (1, 2, 3)] + [dev(x, y, z + s, c) for s in (1, 2, 3)] + [sib], between)
    sends = []

    def send(src, dst, recv, device):
        n = len(sends)
        d = pltpu.make_async_remote_copy(src_ref=src, dst_ref=dst, send_sem=s_send.at[n], recv_sem=recv, device_id=device, device_id_type=MESH)
        d.start()
        sends.append(d)

    def arrive(dst, recv):
        pltpu.make_async_remote_copy(src_ref=dst, dst_ref=dst, send_sem=s_send.at[0], recv_sem=recv, device_id=sib, device_id_type=MESH).wait_recv()

    written = []

    def across(buf, out, sem, over, yy, xx):
        send(buf.at[yy, xx], out.at[c, yy, xx], over.at[yy, xx], sib)
        d = pltpu.make_async_copy(buf.at[yy, xx], out.at[c, yy, xx], sem.at[yy, xx])
        d.start()
        written.append(d)

    def widen(yq, xq, yp, xp):
        two = jnp.concatenate([bq[yq, xq], bp[yp, xp]], axis=1)
        got = jnp.dot(spread[...], two, preferred_element_type=F32).astype(BF16)
        wq[yq, xq] = got[:, :128]
        wp[yp, xp] = got[:, 128:]
        across(wq, wide_q, s_wq, s_as, yq, xq)
        across(wp, wide_p, s_wp, s_bs, yp, xp)

    peers = (1, 3, 2)
    for s in peers:
        send(own_piece, stage.at[z], s_z.at[z], dev(x, y, z + s, c))
    for s in peers if XDIRECT else (1, 3):
        send(own_piece, own_piece, s_ax.at[x], dev(x + s, y, z, c))
    for s in (1, 3):
        send(own_piece, own_piece, s_ay.at[y, x], dev(x, y + s, z, c))
    for s in peers:
        send(dall.at[z], dall.at[z], s_d.at[z], dev(x, y, z + s, c))
    keep = pltpu.make_async_copy(own_piece, stage.at[z], s_loc.at[0])
    keep.start()
    for s in peers:
        arrive(stage.at[r4(z + s)], s_z.at[r4(z + s)])
    keep.wait()
    for s in peers:
        yt = r4(y + s)
        send(stage.at[yt], bp.at[y, x], s_by.at[y], dev(x, yt, z, c))
    mine = pltpu.make_async_copy(stage.at[y], bp.at[y, x], s_loc.at[1])
    mine.start()
    for s in (1, 3):
        send(stage.at[y], bp.at[y, x], s_bx.at[y, x], dev(x + s, y, z, c))

    xf, xb, x2 = r4(x - way), r4(x + way), r4(x + 2)
    yf, yb, y2 = r4(y - way), r4(y + way), r4(y + 2)
    for xx in (xf, xb, x2):
        arrive(bq.at[y, xx], s_ax.at[xx])
        if not XDIRECT and xx is xf:
            send(bq.at[y, xx], bq.at[y, xx], s_ax.at[xx], dev(x + way, y, z, c))
        for s in (1, 3):
            send(bq.at[y, xx], bq.at[y, xx], s_ay.at[y, xx], dev(x, y + s, z, c))
    for yy in (yf, yb, y2):
        arrive(bp.at[yy, x], s_by.at[yy])
        for s in (1, 3):
            send(bp.at[yy, x], bp.at[yy, x], s_bx.at[yy, x], dev(x + s, y, z, c))
    mine.wait()
    widen(y, x, y, x)
    for xx, yy in ((x, y), (xf, yf), (xb, yb), (x2, y2)):
        arrive(bq.at[yf, xx], s_ay.at[yf, xx])
        send(bq.at[yf, xx], bq.at[yf, xx], s_ay.at[yf, xx], dev(x, y + way, z, c))
        arrive(bp.at[yy, xf], s_bx.at[yy, xf])
        send(bp.at[yy, xf], bp.at[yy, xf], s_bx.at[yy, xf], dev(x + way, y, z, c))
        if xx is not x:
            widen(y, xx, yy, x)
        widen(yf, xx, yy, xf)
    first[3].wait()
    parity = lax.rem(m, 2)
    vbuf[0:128] = held[pl.ds(pl.multiple_of(64 * parity, 64), 128), :]
    half = held[pl.ds(pl.multiple_of(128 * (1 - parity), 64), 64), :]
    vbuf[128:192] = half
    vbuf[192:256] = half
    same = (iota((128, 128), 0) == iota((128, 128), 1)).astype(F32).astype(BF16)
    for q in range(12):
        vt[q] = lax.dot_general(same, vbuf[:, 128 * q:128 * q + 128], NT, preferred_element_type=F32).astype(BF16)
    vt_copy = pltpu.make_async_copy(vt, vt_out, s_loc.at[2])
    vt_copy.start()
    for s in peers:
        arrive(dall.at[r4(z + s)], s_d.at[r4(z + s)])
    same = (iota((192, 192), 0) == iota((192, 192), 1)).astype(F32).astype(BF16)
    full = jnp.concatenate([dall[k] for k in range(4)], axis=0)
    turned = lax.dot_general(same, full, NT, preferred_element_type=F32).astype(BF16)
    lam, lane = iota((192, 128), 0), iota((192, 128), 1)
    part = (lane % 64) // 8
    for l in range(32):
        sel = ((lam == 6 * l + part) & (part < 6)).astype(F32).astype(BF16)
        dexp[l] = jnp.dot(turned, sel, preferred_element_type=F32)
    dexp_copy = pltpu.make_async_copy(dexp, dexp_out, s_loc.at[0])
    dexp_copy.start()
    for ya, xa in ((yb, xb), (y2, x2)):
        for xx, yy in ((x, y), (xf, yf), (xb, yb), (x2, y2)):
            arrive(bq.at[ya, xx], s_ay.at[ya, xx])
            arrive(bp.at[yy, xa], s_bx.at[yy, xa])
            widen(ya, xx, yy, xa)
    for yy in (y, yf, yb, y2):
        for xx in (x, xf, xb, x2):
            arrive(wide_q.at[o, yy, xx], s_as.at[yy, xx])
            arrive(wide_p.at[o, yy, xx], s_bs.at[yy, xx])
    for d in written + [vt_copy, dexp_copy]:
        d.wait()
    for d in sends:
        d.wait_send()


def gather(own, names, dens, v):
    hbm = pl.BlockSpec(memory_space=pl.ANY)
    dma = pltpu.SemaphoreType.DMA
    return pl.pallas_call(
        gather_kernel,
        out_shape=[
            jax.ShapeDtypeStruct((2, 4, 4, 384, 128), BF16),
            jax.ShapeDtypeStruct((2, 4, 4, 384, 128), BF16),
            jax.ShapeDtypeStruct((12, 128, 256), BF16),
            jax.ShapeDtypeStruct((32, 192, 128), F32),
        ],
        in_specs=[hbm] * 4,
        out_specs=[hbm] * 4,
        scratch_shapes=[
            pltpu.VMEM((4, 4, ROWS, 128), BF16),
            pltpu.VMEM((4, 4, ROWS, 128), BF16),
            pltpu.VMEM((4, ROWS, 128), BF16),
            pltpu.VMEM((4, 48, 192), BF16),
            pltpu.VMEM((192, 1536), BF16),
            pltpu.VMEM((256, 1536), BF16),
            pltpu.VMEM((12, 128, 256), BF16),
            pltpu.VMEM((32, 192, 128), F32),
            pltpu.VMEM((4, 4, 384, 128), BF16),
            pltpu.VMEM((4, 4, 384, 128), BF16),
            pltpu.VMEM((384, 304), BF16),
            dma((80,)), dma((4,)), dma((4,)), dma((4,)), dma((4, 4)), dma((4, 4)), dma((4,)), dma((4, 4)), dma((4, 4)), dma((4,)), dma((4, 4)), dma((4, 4)),
        ],
        compiler_params=pltpu.CompilerParams(collective_id=0, has_side_effects=True, vmem_limit_bytes=48 << 20),
        name="gather",
    )(own, names, dens, v)


def reduce_kernel(part, out, got, cut, got2, send1, recv1, send2, recv2):
    m, x, y, z, c = place()
    g = lax.rem(m, 8)
    near = [(y * 8 + lax.rem(g + d, 8), z) for d in range(1, 8)]
    far = []
    for d in range(1, 16):
        h = lax.rem(y * 4 + z + d, 16)
        far.append((h // 4, lax.rem(h, 4)))
    greet(near + [((yy * 8 + g), zz) for yy, zz in far])
    first = []
    for d in range(1, 8):
        gg = lax.rem(g + d, 8)
        cp = pltpu.make_async_remote_copy(src_ref=part.at[:, gg], dst_ref=got.at[g], send_sem=send1.at[d], recv_sem=recv1.at[g], device_id=near[d - 1], device_id_type=MESH)
        cp.start()
        first.append(cp)
    got[g] = part[:, g]
    cut[...] = jnp.zeros_like(cut)
    for d in range(1, 8):
        gg = lax.rem(g + d, 8)
        pltpu.make_async_remote_copy(src_ref=part.at[:, gg], dst_ref=got.at[gg], send_sem=send1.at[d], recv_sem=recv1.at[gg], device_id=near[0], device_id_type=MESH).wait_recv()
    total = got[0]
    for k in range(1, 8):
        total = total + got[k]
    for zz in range(4):
        cut[:, zz, :, 0:48] = total[:, :, 48 * zz:48 * zz + 48]
    second = []
    for d, (yy, zz) in enumerate(far):
        cp = pltpu.make_async_remote_copy(src_ref=cut.at[yy, zz], dst_ref=got2.at[y, z], send_sem=send2.at[d], recv_sem=recv2.at[y, z], device_id=(yy * 8 + g, zz), device_id_type=MESH)
        cp.start()
        second.append(cp)
    got2[y, z] = cut[y, z]
    for yy, zz in far:
        pltpu.make_async_remote_copy(src_ref=cut.at[yy, zz], dst_ref=got2.at[yy, zz], send_sem=send2.at[0], recv_sem=recv2.at[yy, zz], device_id=(yy * 8 + g, zz), device_id_type=MESH).wait_recv()
    result = got2[0, 0]
    for k in range(1, 16):
        result = result + got2[k // 4, k % 4]
    out[...] = result
    for cp in first + second:
        cp.wait_send()


def reduce(part):
    vmem = pl.BlockSpec(memory_space=pltpu.VMEM)
    dma = pltpu.SemaphoreType.DMA
    return pl.pallas_call(
        reduce_kernel,
        out_shape=jax.ShapeDtypeStruct((8, 128), F32),
        in_specs=[vmem],
        out_specs=vmem,
        scratch_shapes=[
            pltpu.VMEM((8, 4, 8, 256), F32),
            pltpu.VMEM((4, 4, 8, 128), F32),
            pltpu.VMEM((4, 4, 8, 128), F32),
            dma((8,)), dma((8,)), dma((16,)), dma((4, 4)),
        ],
        compiler_params=pltpu.CompilerParams(collective_id=1, has_side_effects=True),
        name="reduce",
    )(part)


def body(block_list, block_values, atom_offsets, density, metric_inverse):
    m, r = lax.axis_index("map"), lax.axis_index("row")
    parity, chip = m % 2, m // 2
    names = jnp.pad(block_list.astype(BF16), ((0, 8), (0, 125)))
    own = block_values.transpose(1, 2, 0, 3).reshape(288, 128)
    bq, bp, vt, dexp = gather(own, names, density, metric_inverse)
    bq, bp = bq.reshape(256, 48, 128), bp.reshape(256, 48, 128)

    def lists(b):
        return b[:, 6, :3].astype(I32)
    codex, codep, meta, sig = tables(lists(bq), lists(bp), atom_offsets // 6, 3 * chip + 2 * parity, 3 * chip + 1, r * 12, parity)
    part = contract(codex, codep, meta, sig, bq, bp, vt, dexp)
    return reduce(part.reshape(4, 8, 8, 256))[:6, :48]


def solution(mesh):
    placed = (
        P(("map", "row"), None),
        P(("map", "row"), None, None, None),
        P(),
        P("row", None),
        P("map", "row"),
    )
    return jax.shard_map(
        body, mesh=mesh, in_specs=placed, out_specs=P("map", "row"), check_vma=False
    )
```

```python
import jax
import jax.numpy as jnp
from jax import lax
from jax.experimental import pallas as pl
from jax.experimental.pallas import tpu as pltpu
from jax.sharding import PartitionSpec as P

HI = lax.Precision.HIGHEST
F32, BF16, I32 = jnp.float32, jnp.bfloat16, jnp.int32
NT = (((1,), (1,)), ((), ()))
MESH = pl.DeviceIdType.MESH
GROUP = 32
CHUNK = 16
XROWS = 44
XUN = 4
HN = 48
NB = 16


def iota(shape, axis):
    return lax.broadcasted_iota(I32, shape, axis)


def contract_kernel(codex, codep, meta, sig, bq, bp_hbm, vt, dexp_hbm, out, xbuf, hbuf, obuf, sbuf, ebuf, kbuf, bp, dexp, s_b, s_d):
    nf, nh = meta[0, 33], meta[0, 34]
    table = pltpu.make_async_copy(dexp_hbm, dexp, s_d.at[0])
    table.start()

    def fetch(t):
        return pltpu.make_async_copy(bp_hbm.at[codep[0, t] & 255], bp.at[t, 0:48], s_b.at[t])

    def f_step(t, carry):
        fetch(t).start()
        bp[t, 48:64] = jnp.zeros((16, 128), BF16)
        return carry

    lax.fori_loop(0, nf + nh, f_step, 0)
    low_half = iota((8, 128), 1) < 64

    def x_step(step, carry):
        for w in range(XUN):
            ch = XUN * step + w
            src = [codex[0, 8 * ch + u] for u in range(8)]
            rows = jnp.concatenate([bq[s & 255] for s in src], axis=0)
            x = jnp.dot(rows, vt[meta[0, 40 + ch]], preferred_element_type=F32)
            for u in range(8):
                tiles = [x[48 * u + 8 * j:48 * u + 8 * j + 8] for j in range(6)]
                whole = [t[:, :128] for t in tiles]
                half = [jnp.where(low_half, tiles[2 * j][:, 128:], tiles[2 * j + 1][:, 128:]) for j in range(3)]
                xbuf[src[u] >> 8] = jnp.stack(whole + half)
        return carry

    lax.fori_loop(0, (meta[0, 35] + XUN - 1) // XUN, x_step, 0)
    kbuf[...] = jnp.zeros_like(kbuf)
    ebuf[...] = jnp.zeros_like(ebuf)
    sbuf[...] = (iota((256, 2048), 0) == sig[...]).astype(F32).astype(BF16)
    lane, sub = iota((8, 128), 1), iota((8, 128), 0)
    low_mask = (lane % 8 == sub) & (lane < 64)
    high_mask = (lane % 8 == sub) & (lane >= 64)
    row, col = iota((8, 256), 0), iota((8, 256), 1)
    even_device = (iota((64, 128), 0) * 0 + meta[0, 36]) == 0
    left_lanes = iota((64, 128), 1) < 64
    none = jnp.zeros((64, 128), BF16)
    table.wait()

    def w_step(t, carry):
        fetch(t).wait()
        return carry

    lax.fori_loop(0, nf + nh, w_step, 0)

    def spread(ld, nu_a, lb, nu_b):
        a = dexp[ld, pl.ds(nu_a, 8, stride=0), :]
        b = dexp[lb, pl.ds(nu_b, 8, stride=0), :]
        return jnp.where(low_mask, a, jnp.where(high_mask, b, 0.0))

    def pair(h):
        n = h.shape[0] // 8
        both = jnp.concatenate([h[:, :128].reshape(n, 8, 128), h[:, 128:].reshape(n, 8, 128)], axis=1)
        return both.astype(BF16)

    def group(half, base, cnt):
        def h_step(t2, carry):
            at, ls = [], []
            for u in range(2):
                t = base + jnp.minimum(2 * t2 + u, cnt - 1)
                code = codep[0, t]
                at.append(t)
                ls.append((code >> 8) & 31)
                ebuf[pl.ds(pl.multiple_of(16 * t2 + 8 * u, 8), 8), :] = (col == 8 * (code >> 13) + row).astype(F32)
            b0, b1 = bp[at[0]], bp[at[1]]
            if not half:
                rhs = jnp.concatenate([jnp.concatenate([b0, none], axis=1), jnp.concatenate([none, b1], axis=1)], axis=0)
                for c in range(0, 192, HN):
                    w = jnp.concatenate([spread(ls[0], nu, ls[1], nu) for nu in range(c, c + HN)], axis=0).astype(BF16)
                    hbuf[c:c + HN, t2] = pair(jnp.dot(w, rhs, preferred_element_type=F32))
            else:
                quads = []
                for b in (b0, b1):
                    wide = b.astype(F32)
                    turned = pltpu.roll(wide, 64, 1)
                    first = jnp.where(even_device, wide, turned)
                    second = jnp.where(even_device, turned, wide)
                    quads.append((jnp.where(left_lanes, first, 0.0).astype(BF16), jnp.where(left_lanes, 0.0, second).astype(BF16)))
                (e0, o0), (e1, o1) = quads
                rhs = jnp.concatenate([jnp.concatenate([p, q], axis=1) for p, q in ((e0, none), (o0, none), (none, e1), (none, o1))], axis=0)
                for c in range(0, 96, HN):
                    w = jnp.concatenate([
                        jnp.concatenate([spread(l, 2 * r, l, 2 * r + 1) for r in range(c, c + HN)], axis=0).astype(BF16)
                        for l in ls], axis=1)
                    hbuf[c:c + HN, t2] = pair(jnp.dot(w, rhs, preferred_element_type=F32))
            return carry

        lax.fori_loop(0, (cnt + 1) // 2, h_step, 0)
        depth, first = (3, 6) if half else (6, 0)

        def chunk(n, k0):
            xs = jnp.concatenate([xbuf[pl.ds(k0, CHUNK), first + j].reshape(CHUNK * 8, 128).astype(BF16) for j in range(depth)], axis=1)
            hs = jnp.concatenate([hbuf[n * depth + j].reshape(GROUP * 8, 128) for j in range(depth)], axis=1)
            o = lax.dot_general(xs, hs, NT, preferred_element_type=F32)
            obuf[pl.ds(pl.multiple_of(8 * k0, 8), CHUNK * 8), :] = o

        def n_step(i, carry):
            ends = [meta[0, NB * i + u] for u in range(NB + 1)]
            for u in range(NB):
                chunk(NB * i + u, ends[u])
            longest = ends[1] - ends[0]
            for u in range(1, NB):
                longest = jnp.maximum(longest, ends[u + 1] - ends[u])

            @pl.when(longest > CHUNK)
            def _():
                def again(n, carry):
                    s0, s1 = meta[0, n], meta[0, n + 1]

                    def c_step(c, carry):
                        chunk(n, s0 + CHUNK * c)
                        return carry

                    return lax.fori_loop(0, (s1 - s0 + CHUNK - 1) // CHUNK, c_step, carry)

                lax.fori_loop(NB * i, NB * i + NB, again, 0)
            return carry

        lax.fori_loop(0, 32 // NB, n_step, 0)
        r = jnp.zeros((256, 256), F32)
        for k in range(8):
            o = obuf[256 * k:256 * k + 256, :]
            high = o.astype(BF16)
            low = (o - high.astype(F32)).astype(BF16)
            s = sbuf[:, 256 * k:256 * k + 256]
            r += jnp.dot(s, high, preferred_element_type=F32) + jnp.dot(s, low, preferred_element_type=F32)
        r = jnp.where(iota((256, 256), 1) < 8 * cnt, r, 0.0)
        kbuf[...] += jnp.dot(r, ebuf[...], preferred_element_type=F32, precision=HI)

    for half, base, total in ((False, 0, nf), (True, nf, nh)):
        def g_step(g, carry, half=half, base=base, total=total):
            group(half, base + GROUP * g, jnp.minimum(total - GROUP * g, GROUP))
            return carry

        lax.fori_loop(0, (total + GROUP - 1) // GROUP, g_step, 0)
    out[...] = kbuf[...].T


def contract(codex, codep, meta, sig, bq, bp, vt, dexp):
    smem = pl.BlockSpec(memory_space=pltpu.SMEM)
    vmem = pl.BlockSpec(memory_space=pltpu.VMEM)
    hbm = pl.BlockSpec(memory_space=pl.ANY)
    return pl.pallas_call(
        contract_kernel,
        out_shape=jax.ShapeDtypeStruct((256, 256), F32),
        in_specs=[smem] * 3 + [vmem, vmem, hbm, vmem, hbm],
        out_specs=vmem,
        scratch_shapes=[
            pltpu.VMEM((256 + CHUNK, 9, 8, 128), F32),
            pltpu.VMEM((192, GROUP // 2, 16, 128), BF16),
            pltpu.VMEM(((256 + CHUNK) * 8, 256), F32),
            pltpu.VMEM((256, 2048), BF16),
            pltpu.VMEM((256, 256), F32),
            pltpu.VMEM((256, 256), F32),
            pltpu.VMEM((256, 64, 128), BF16),
            pltpu.VMEM((32, 192, 128), F32),
            pltpu.SemaphoreType.DMA((256,)),
            pltpu.SemaphoreType.DMA((1,)),
        ],
        compiler_params=pltpu.CompilerParams(vmem_limit_bytes=62 << 20),
        name="contract",
    )(codex, codep, meta, sig, bq, bp, vt, dexp)


ROWS = 288
XDIRECT = True


def place():
    m, z = lax.axis_index("map"), lax.axis_index("row")
    return m, (m // 2) % 4, m // 8, z, m % 2


def at_map(x, y, c):
    return (y * 4 + x) * 2 + c


def greet(devices, between=None):
    barrier = pltpu.get_barrier_semaphore()
    for d in devices:
        pl.semaphore_signal(barrier, inc=1, device_id=d, device_id_type=MESH)
    if between is not None:
        between()
    pl.semaphore_wait(barrier, len(devices))


def tables(nq, nn, whole_block, half_block, row_start, parity, codex, codep, meta, sig):
    g = iota((256, 1), 0)
    wide = iota((256, 256), 1)
    lane = iota((256, 128), 1)

    def column(ref, field):
        rows = []
        for t in range(32):
            c, s, u = t // 16, (t // 4) % 4, t % 4
            rows.append(ref[c, s, u, pl.ds(field, 8, stride=0), :])
        spread = jnp.concatenate(rows, axis=0)
        return jnp.sum(jnp.where(lane == g % 8, spread, 0.0), axis=1, keepdims=True).astype(I32)

    def across(col):
        return jnp.sum(jnp.where(wide == g, col.astype(F32), 0.0), axis=0, keepdims=True).astype(I32)

    def lanes(hit):
        return jnp.sum(hit.astype(F32), axis=1, keepdims=True).astype(I32)

    def rows(hit):
        return jnp.sum(hit.astype(F32), axis=0, keepdims=True).astype(I32)

    def rank(col):
        other = across(col)
        return lanes((other < col) | ((other == col) & (wide < g)))

    def put(where, at, code, rest):
        return rest + jnp.sum(jnp.where(where == at, (code - rest).astype(F32), 0.0), axis=0, keepdims=True).astype(I32)

    first, second, q = column(nq, 0), column(nq, 1), column(nq, 2) - row_start
    by_n = rank(second)
    starts = rows(second < lane)
    sig_at = iota((256, 2048), 1)
    where = jnp.sum(jnp.where(by_n == sig_at // 8, first.astype(F32), 0.0), axis=0, keepdims=True).astype(I32)
    inner = iota((1, 2048), 1) % 8
    sig[...] = jnp.where(inner < 6, 6 * where + inner, -1)
    other = across(q)
    within = lanes((other == q) & (wide < g))
    chunks_row = (rows(q == lane) + 7) // 8
    n16, l16 = iota((16, 128), 0), iota((16, 128), 1)
    ends_col = jnp.sum(jnp.where(l16 <= n16, chunks_row.astype(F32), 0.0), axis=1, keepdims=True).astype(I32)
    lead = jnp.sum(jnp.where(lane < q, chunks_row.astype(F32), 0.0), axis=1, keepdims=True).astype(I32)
    codex[...] = put(8 * lead + within, iota((256, 512), 1), g + by_n * 256, 256 * 256)
    at128 = iota((1, 128), 1)
    chunk_q = jnp.minimum(rows((ends_col <= l16 - 40) & (n16 < 12)), 11)
    total = jnp.sum(chunks_row.astype(F32), axis=1, keepdims=True).astype(I32)
    p = column(nn, 2)
    key = jnp.where(p == whole_block, 0, jnp.where(p == half_block, 1, 2))
    piece = g // 8
    place_of = ((piece // 16) * 16 + (piece % 4) * 4 + (piece // 4) % 4) * 8 + g % 8
    codep[...] = put(rank(key), wide, place_of + column(nn, 1) * 256 + column(nn, 0) * 8192, 0)
    n0, n1 = rows(key == 0), rows(key == 1)
    meta[...] = jnp.where(at128 < 33, starts, jnp.where(at128 == 33, n0, jnp.where(at128 == 34, n1, jnp.where(at128 == 35, total, jnp.where(at128 == 36, parity, jnp.where(at128 < 40, 0, chunk_q))))))


def gather_kernel(own, triples, offsets, dens, v, wide_q, wide_p, vt_out, dexp_out, codex, codep, meta, sig, bq, bp, stage, dall, held, vbuf, vt, dexp, wq, wp, spread, s_send, s_z, s_d, s_ax, s_ay, s_as, s_by, s_bx, s_bs, s_loc, s_wq, s_wp, nq, nn, nz, s_nz, s_nx, s_ny, s_my, s_mx, s_ns):
    m, x, y, z, c = place()
    way = 1 - 2 * c
    o = 1 - c

    def r4(v):
        return lax.rem(v + 8, 4)

    def dev(xx, yy, zz, cc):
        return (at_map(r4(xx), r4(yy), cc), r4(zz))

    sib = dev(x, y, z, o)
    own_piece = bq.at[y, x]
    first = [
        pltpu.make_async_copy(own, bq.at[y, x], s_loc.at[0]),
        pltpu.make_async_copy(dens, dall.at[z], s_loc.at[2]),
        pltpu.make_async_copy(v, held, s_loc.at[3]),
    ]
    for d in first:
        d.start()

    def between():
        r, k = iota((384, 288), 0), iota((384, 288), 1)
        block, j, i = r // 48, (r % 48) // 8, r % 8
        source = jnp.where(i < 6, (i * 6 + j) * 8 + block, -1)
        spread[...] = (k == source).astype(F32).astype(BF16)
        row, lane = iota((8, 128), 0), iota((8, 128), 1)
        tile = jnp.zeros((8, 128), F32)
        for k in range(8):
            a, l, p = offsets[triples[0, k]] // 6, offsets[triples[1, k]] // 6, triples[2, k]
            tile = jnp.where(lane == k, jnp.where(row == 0, a, jnp.where(row == 1, l, p)).astype(F32), tile)
        nq[c, y, x] = tile
        nz[z] = tile
        for d in first[:2]:
            d.wait()

    greet([dev(x + s, y, z, c) for s in (1, 2, 3)] + [dev(x, y + s, z, c) for s in (1, 2, 3)] + [dev(x, y, z + s, c) for s in (1, 2, 3)] + [sib], between)
    sends = []

    def send(src, dst, recv, device):
        n = len(sends)
        d = pltpu.make_async_remote_copy(src_ref=src, dst_ref=dst, send_sem=s_send.at[n], recv_sem=recv, device_id=device, device_id_type=MESH)
        d.start()
        sends.append(d)

    def arrive(dst, recv):
        pltpu.make_async_remote_copy(src_ref=dst, dst_ref=dst, send_sem=s_send.at[0], recv_sem=recv, device_id=sib, device_id_type=MESH).wait_recv()

    written = []

    def across(buf, out, sem, over, yy, xx):
        send(buf.at[yy, xx], out.at[c, yy, xx], over.at[yy, xx], sib)
        d = pltpu.make_async_copy(buf.at[yy, xx], out.at[c, yy, xx], sem.at[yy, xx])
        d.start()
        written.append(d)

    def widen(yq, xq, yp, xp):
        two = jnp.concatenate([bq[yq, xq], bp[yp, xp]], axis=1)
        got = jnp.dot(spread[...], two, preferred_element_type=F32).astype(BF16)
        wq[yq, xq] = got[:, :128]
        wp[yp, xp] = got[:, 128:]
        across(wq, wide_q, s_wq, s_as, yq, xq)
        across(wp, wide_p, s_wp, s_bs, yp, xp)

    peers = (1, 3, 2)
    for s in peers:
        send(own_piece, stage.at[z], s_z.at[z], dev(x, y, z + s, c))
    for s in peers if XDIRECT else (1, 3):
        send(own_piece, own_piece, s_ax.at[x], dev(x + s, y, z, c))
    for s in (1, 3):
        send(own_piece, own_piece, s_ay.at[y, x], dev(x, y + s, z, c))
    for s in peers:
        send(nz.at[z], nz.at[z], s_nz.at[z], dev(x, y, z + s, c))
        send(nq.at[c, y, x], nq.at[c, y, x], s_nx.at[x], dev(x + s, y, z, c))
    for s in peers:
        send(dall.at[z], dall.at[z], s_d.at[z], dev(x, y, z + s, c))
    keep = pltpu.make_async_copy(own_piece, stage.at[z], s_loc.at[0])
    keep.start()
    for s in peers:
        arrive(stage.at[r4(z + s)], s_z.at[r4(z + s)])
    keep.wait()
    for s in peers:
        yt = r4(y + s)
        send(stage.at[yt], bp.at[y, x], s_by.at[y], dev(x, yt, z, c))
    for s in peers:
        arrive(nz.at[r4(z + s)], s_nz.at[r4(z + s)])
    nn[c, x, y] = nz[y]
    for s in peers:
        yt = r4(y + s)
        send(nz.at[yt], nn.at[c, x, y], s_my.at[y], dev(x, yt, z, c))
    mine = pltpu.make_async_copy(stage.at[y], bp.at[y, x], s_loc.at[1])
    mine.start()
    for s in (1, 3):
        send(stage.at[y], bp.at[y, x], s_bx.at[y, x], dev(x + s, y, z, c))

    xf, xb, x2 = r4(x - way), r4(x + way), r4(x + 2)
    yf, yb, y2 = r4(y - way), r4(y + way), r4(y + 2)
    for xx in (xf, xb, x2):
        arrive(bq.at[y, xx], s_ax.at[xx])
        if not XDIRECT and xx is xf:
            send(bq.at[y, xx], bq.at[y, xx], s_ax.at[xx], dev(x + way, y, z, c))
        for s in (1, 3):
            send(bq.at[y, xx], bq.at[y, xx], s_ay.at[y, xx], dev(x, y + s, z, c))
    for xx in (xf, xb, x2):
        arrive(nq.at[c, y, xx], s_nx.at[xx])
    for s in peers:
        send(nq.at[c, y], nq.at[c, y], s_ny.at[y], dev(x, y + s, z, c))
    for yy in (yf, yb, y2):
        arrive(bp.at[yy, x], s_by.at[yy])
        for s in (1, 3):
            send(bp.at[yy, x], bp.at[yy, x], s_bx.at[yy, x], dev(x + s, y, z, c))
    for yy in (yf, yb, y2):
        arrive(nn.at[c, x, yy], s_my.at[yy])
    for s in peers:
        send(nn.at[c, x], nn.at[c, x], s_mx.at[x], dev(x + s, y, z, c))
    mine.wait()
    widen(y, x, y, x)
    for xx, yy in ((x, y), (xf, yf), (xb, yb), (x2, y2)):
        arrive(bq.at[yf, xx], s_ay.at[yf, xx])
        send(bq.at[yf, xx], bq.at[yf, xx], s_ay.at[yf, xx], dev(x, y + way, z, c))
        arrive(bp.at[yy, xf], s_bx.at[yy, xf])
        send(bp.at[yy, xf], bp.at[yy, xf], s_bx.at[yy, xf], dev(x + way, y, z, c))
        if xx is not x:
            widen(y, xx, yy, x)
        widen(yf, xx, yy, xf)
    for s in peers:
        arrive(nq.at[c, r4(y + s)], s_ny.at[r4(y + s)])
        arrive(nn.at[c, r4(x + s)], s_mx.at[r4(x + s)])
    send(nq.at[c], nq.at[c], s_ns.at[0], sib)
    send(nn.at[c], nn.at[c], s_ns.at[1], sib)
    first[2].wait()
    parity = lax.rem(m, 2)
    vbuf[0:128] = held[pl.ds(pl.multiple_of(64 * parity, 64), 128), :]
    half = held[pl.ds(pl.multiple_of(128 * (1 - parity), 64), 64), :]
    vbuf[128:192] = half
    vbuf[192:256] = half
    same = (iota((128, 128), 0) == iota((128, 128), 1)).astype(F32).astype(BF16)
    for q in range(12):
        vt[q] = lax.dot_general(same, vbuf[:, 128 * q:128 * q + 128], NT, preferred_element_type=F32).astype(BF16)
    vt_copy = pltpu.make_async_copy(vt, vt_out, s_loc.at[2])
    vt_copy.start()
    for s in peers:
        arrive(dall.at[r4(z + s)], s_d.at[r4(z + s)])
    same = (iota((192, 192), 0) == iota((192, 192), 1)).astype(F32).astype(BF16)
    full = jnp.concatenate([dall[k] for k in range(4)], axis=0)
    turned = lax.dot_general(same, full, NT, preferred_element_type=F32).astype(BF16)
    lam, lane = iota((192, 128), 0), iota((192, 128), 1)
    part = (lane % 64) // 8
    for l in range(32):
        sel = ((lam == 6 * l + part) & (part < 6)).astype(F32).astype(BF16)
        dexp[l] = jnp.dot(turned, sel, preferred_element_type=F32)
    dexp_copy = pltpu.make_async_copy(dexp, dexp_out, s_loc.at[0])
    dexp_copy.start()
    arrive(nq.at[o], s_ns.at[0])
    arrive(nn.at[o], s_ns.at[1])
    chip = m // 2
    tables(nq, nn, 3 * chip + 2 * parity, 3 * chip + 1, z * 12, parity, codex, codep, meta, sig)
    for ya, xa in ((yb, xb), (y2, x2)):
        for xx, yy in ((x, y), (xf, yf), (xb, yb), (x2, y2)):
            arrive(bq.at[ya, xx], s_ay.at[ya, xx])
            arrive(bp.at[yy, xa], s_bx.at[yy, xa])
            widen(ya, xx, yy, xa)
    for yy in (y, yf, yb, y2):
        for xx in (x, xf, xb, x2):
            arrive(wide_q.at[o, yy, xx], s_as.at[yy, xx])
            arrive(wide_p.at[o, yy, xx], s_bs.at[yy, xx])
    for d in written + [vt_copy, dexp_copy]:
        d.wait()
    for d in sends:
        d.wait_send()


def gather(own, triples, offsets, dens, v):
    hbm = pl.BlockSpec(memory_space=pl.ANY)
    smem = pl.BlockSpec(memory_space=pltpu.SMEM)
    vmem = pl.BlockSpec(memory_space=pltpu.VMEM)
    dma = pltpu.SemaphoreType.DMA
    return pl.pallas_call(
        gather_kernel,
        out_shape=[
            jax.ShapeDtypeStruct((2, 4, 4, 384, 128), BF16),
            jax.ShapeDtypeStruct((2, 4, 4, 384, 128), BF16),
            jax.ShapeDtypeStruct((12, 128, 256), BF16),
            jax.ShapeDtypeStruct((32, 192, 128), F32),
            jax.ShapeDtypeStruct((1, 512), I32),
            jax.ShapeDtypeStruct((1, 256), I32),
            jax.ShapeDtypeStruct((1, 128), I32),
            jax.ShapeDtypeStruct((1, 2048), I32),
        ],
        in_specs=[hbm, smem, smem, hbm, hbm],
        out_specs=[hbm] * 4 + [vmem] * 4,
        scratch_shapes=[
            pltpu.VMEM((4, 4, ROWS, 128), BF16),
            pltpu.VMEM((4, 4, ROWS, 128), BF16),
            pltpu.VMEM((4, ROWS, 128), BF16),
            pltpu.VMEM((4, 48, 192), BF16),
            pltpu.VMEM((192, 1536), BF16),
            pltpu.VMEM((256, 1536), BF16),
            pltpu.VMEM((12, 128, 256), BF16),
            pltpu.VMEM((32, 192, 128), F32),
            pltpu.VMEM((4, 4, 384, 128), BF16),
            pltpu.VMEM((4, 4, 384, 128), BF16),
            pltpu.VMEM((384, 288), BF16),
            dma((104,)), dma((4,)), dma((4,)), dma((4,)), dma((4, 4)), dma((4, 4)), dma((4,)), dma((4, 4)), dma((4, 4)), dma((4,)), dma((4, 4)), dma((4, 4)),
            pltpu.VMEM((2, 4, 4, 8, 128), F32),
            pltpu.VMEM((2, 4, 4, 8, 128), F32),
            pltpu.VMEM((4, 8, 128), F32),
            dma((4,)), dma((4,)), dma((4,)), dma((4,)), dma((4,)), dma((2,)),
        ],
        compiler_params=pltpu.CompilerParams(collective_id=0, has_side_effects=True, vmem_limit_bytes=62 << 20),
        name="gather",
    )(own, triples, offsets, dens, v)


def reduce_kernel(part, out, got, cut, got2, send1, recv1, send2, recv2):
    m, x, y, z, c = place()
    g = lax.rem(m, 8)
    near = [(y * 8 + lax.rem(g + d, 8), z) for d in range(1, 8)]
    far = []
    for d in range(1, 16):
        h = lax.rem(y * 4 + z + d, 16)
        far.append((h // 4, lax.rem(h, 4)))
    greet(near + [((yy * 8 + g), zz) for yy, zz in far])
    first = []
    for d in range(1, 8):
        gg = lax.rem(g + d, 8)
        cp = pltpu.make_async_remote_copy(src_ref=part.at[:, gg], dst_ref=got.at[g], send_sem=send1.at[d], recv_sem=recv1.at[g], device_id=near[d - 1], device_id_type=MESH)
        cp.start()
        first.append(cp)
    got[g] = part[:, g]
    cut[...] = jnp.zeros_like(cut)
    for d in range(1, 8):
        gg = lax.rem(g + d, 8)
        pltpu.make_async_remote_copy(src_ref=part.at[:, gg], dst_ref=got.at[gg], send_sem=send1.at[d], recv_sem=recv1.at[gg], device_id=near[0], device_id_type=MESH).wait_recv()
    total = got[0]
    for k in range(1, 8):
        total = total + got[k]
    for zz in range(4):
        cut[:, zz, :, 0:48] = total[:, :, 48 * zz:48 * zz + 48]
    second = []
    for d, (yy, zz) in enumerate(far):
        cp = pltpu.make_async_remote_copy(src_ref=cut.at[yy, zz], dst_ref=got2.at[y, z], send_sem=send2.at[d], recv_sem=recv2.at[y, z], device_id=(yy * 8 + g, zz), device_id_type=MESH)
        cp.start()
        second.append(cp)
    got2[y, z] = cut[y, z]
    for yy, zz in far:
        pltpu.make_async_remote_copy(src_ref=cut.at[yy, zz], dst_ref=got2.at[yy, zz], send_sem=send2.at[0], recv_sem=recv2.at[yy, zz], device_id=(yy * 8 + g, zz), device_id_type=MESH).wait_recv()
    for part_of in range(2):
        result = got2[2 * part_of, 0]
        for k in range(1, 8):
            result = result + got2[2 * part_of + k // 4, k % 4]
        out[part_of] = result
    for cp in first + second:
        cp.wait_send()


def reduce(part):
    vmem = pl.BlockSpec(memory_space=pltpu.VMEM)
    dma = pltpu.SemaphoreType.DMA
    return pl.pallas_call(
        reduce_kernel,
        out_shape=jax.ShapeDtypeStruct((2, 8, 128), F32),
        in_specs=[vmem],
        out_specs=vmem,
        scratch_shapes=[
            pltpu.VMEM((8, 4, 8, 256), F32),
            pltpu.VMEM((4, 4, 8, 128), F32),
            pltpu.VMEM((4, 4, 8, 128), F32),
            dma((8,)), dma((8,)), dma((16,)), dma((4, 4)),
        ],
        compiler_params=pltpu.CompilerParams(collective_id=1, has_side_effects=True),
        name="reduce",
    )(part)


def body(block_list, block_values, atom_offsets, density, metric_inverse):
    own = block_values.transpose(1, 2, 0, 3).reshape(288, 128)
    bq, bp, vt, dexp, codex, codep, meta, sig = gather(own, block_list.T, atom_offsets, density, metric_inverse)
    part = contract(codex, codep, meta, sig, bq.reshape(256, 48, 128), bp.reshape(256, 48, 128), vt, dexp)
    sums = reduce(part.reshape(4, 8, 8, 256))
    return sums[0, :6, :48] + sums[1, :6, :48]


def solution(mesh):
    placed = (
        P(("map", "row"), None),
        P(("map", "row"), None, None, None),
        P(),
        P("row", None),
        P("map", "row"),
    )
    return jax.shard_map(
        body, mesh=mesh, in_specs=placed, out_specs=P("map", "row"), check_vma=False
    )
```

```python
import jax
import jax.numpy as jnp
from jax import lax
from jax.experimental import pallas as pl
from jax.experimental.pallas import tpu as pltpu
from jax.sharding import PartitionSpec as P

HI = lax.Precision.HIGHEST
F32, BF16, I32 = jnp.float32, jnp.bfloat16, jnp.int32
NT = (((1,), (1,)), ((), ()))
MESH = pl.DeviceIdType.MESH
GROUP = 32
CHUNK = 16
XROWS = 44
XUN = 4
HN = 48
NB = 16


def iota(shape, axis):
    return lax.broadcasted_iota(I32, shape, axis)


def contract_kernel(codex, codep, meta, sig, bq, bp, vt, dexp, out, xbuf, hbuf, obuf, sbuf, ebuf, kbuf):
    nf, nh = meta[0, 33], meta[0, 34]
    low_half = iota((8, 128), 1) < 64

    def x_step(step, carry):
        for w in range(XUN):
            ch = XUN * step + w
            src = [codex[0, 8 * ch + u] for u in range(8)]
            rows = jnp.concatenate([bq[s & 255] for s in src], axis=0)
            x = jnp.dot(rows, vt[meta[0, 40 + ch]], preferred_element_type=F32)
            for u in range(8):
                tiles = [x[48 * u + 8 * j:48 * u + 8 * j + 8] for j in range(6)]
                whole = [t[:, :128] for t in tiles]
                half = [jnp.where(low_half, tiles[2 * j][:, 128:], tiles[2 * j + 1][:, 128:]) for j in range(3)]
                xbuf[src[u] >> 8] = jnp.stack(whole + half)
        return carry

    lax.fori_loop(0, (meta[0, 35] + XUN - 1) // XUN, x_step, 0)
    kbuf[...] = jnp.zeros_like(kbuf)
    ebuf[...] = jnp.zeros_like(ebuf)
    sbuf[...] = (iota((256, 2048), 0) == sig[...]).astype(F32).astype(BF16)
    lane, sub = iota((8, 128), 1), iota((8, 128), 0)
    low_mask = (lane % 8 == sub) & (lane < 64)
    high_mask = (lane % 8 == sub) & (lane >= 64)
    row, col = iota((8, 256), 0), iota((8, 256), 1)
    even_device = (iota((64, 128), 0) * 0 + meta[0, 36]) == 0
    left_lanes = iota((64, 128), 1) < 64
    none = jnp.zeros((64, 128), BF16)
    def spread(ld, nu_a, lb, nu_b):
        a = dexp[ld, pl.ds(nu_a, 8, stride=0), :]
        b = dexp[lb, pl.ds(nu_b, 8, stride=0), :]
        return jnp.where(low_mask, a, jnp.where(high_mask, b, 0.0))

    def pair(h):
        n = h.shape[0] // 8
        both = jnp.concatenate([h[:, :128].reshape(n, 8, 128), h[:, 128:].reshape(n, 8, 128)], axis=1)
        return both.astype(BF16)

    def group(half, base, cnt):
        def h_step(t2, carry):
            at, ls = [], []
            for u in range(2):
                t = base + jnp.minimum(2 * t2 + u, cnt - 1)
                code = codep[0, t]
                at.append(code & 255)
                ls.append((code >> 8) & 31)
                ebuf[pl.ds(pl.multiple_of(16 * t2 + 8 * u, 8), 8), :] = (col == 8 * (code >> 13) + row).astype(F32)
            b0, b1 = [jnp.concatenate([bp[k], none[:16]], axis=0) for k in at]
            if not half:
                rhs = jnp.concatenate([jnp.concatenate([b0, none], axis=1), jnp.concatenate([none, b1], axis=1)], axis=0)
                for c in range(0, 192, HN):
                    w = jnp.concatenate([spread(ls[0], nu, ls[1], nu) for nu in range(c, c + HN)], axis=0).astype(BF16)
                    hbuf[c:c + HN, t2] = pair(jnp.dot(w, rhs, preferred_element_type=F32))
            else:
                quads = []
                for b in (b0, b1):
                    wide = b.astype(F32)
                    turned = pltpu.roll(wide, 64, 1)
                    first = jnp.where(even_device, wide, turned)
                    second = jnp.where(even_device, turned, wide)
                    quads.append((jnp.where(left_lanes, first, 0.0).astype(BF16), jnp.where(left_lanes, 0.0, second).astype(BF16)))
                (e0, o0), (e1, o1) = quads
                rhs = jnp.concatenate([jnp.concatenate([p, q], axis=1) for p, q in ((e0, none), (o0, none), (none, e1), (none, o1))], axis=0)
                for c in range(0, 96, HN):
                    w = jnp.concatenate([
                        jnp.concatenate([spread(l, 2 * r, l, 2 * r + 1) for r in range(c, c + HN)], axis=0).astype(BF16)
                        for l in ls], axis=1)
                    hbuf[c:c + HN, t2] = pair(jnp.dot(w, rhs, preferred_element_type=F32))
            return carry

        lax.fori_loop(0, (cnt + 1) // 2, h_step, 0)
        depth, first = (3, 6) if half else (6, 0)

        def chunk(n, k0):
            xs = jnp.concatenate([xbuf[pl.ds(k0, CHUNK), first + j].reshape(CHUNK * 8, 128).astype(BF16) for j in range(depth)], axis=1)
            hs = jnp.concatenate([hbuf[n * depth + j].reshape(GROUP * 8, 128) for j in range(depth)], axis=1)
            o = lax.dot_general(xs, hs, NT, preferred_element_type=F32)
            obuf[pl.ds(pl.multiple_of(8 * k0, 8), CHUNK * 8), :] = o

        def n_step(i, carry):
            ends = [meta[0, NB * i + u] for u in range(NB + 1)]
            for u in range(NB):
                chunk(NB * i + u, ends[u])
            longest = ends[1] - ends[0]
            for u in range(1, NB):
                longest = jnp.maximum(longest, ends[u + 1] - ends[u])

            @pl.when(longest > CHUNK)
            def _():
                def again(n, carry):
                    s0, s1 = meta[0, n], meta[0, n + 1]

                    def c_step(c, carry):
                        chunk(n, s0 + CHUNK * c)
                        return carry

                    return lax.fori_loop(0, (s1 - s0 + CHUNK - 1) // CHUNK, c_step, carry)

                lax.fori_loop(NB * i, NB * i + NB, again, 0)
            return carry

        lax.fori_loop(0, 32 // NB, n_step, 0)
        r = jnp.zeros((256, 256), F32)
        for k in range(8):
            o = obuf[256 * k:256 * k + 256, :]
            high = o.astype(BF16)
            low = (o - high.astype(F32)).astype(BF16)
            s = sbuf[:, 256 * k:256 * k + 256]
            r += jnp.dot(s, high, preferred_element_type=F32) + jnp.dot(s, low, preferred_element_type=F32)
        r = jnp.where(iota((256, 256), 1) < 8 * cnt, r, 0.0)
        kbuf[...] += jnp.dot(r, ebuf[...], preferred_element_type=F32, precision=HI)

    for half, base, total in ((False, 0, nf), (True, nf, nh)):
        def g_step(g, carry, half=half, base=base, total=total):
            group(half, base + GROUP * g, jnp.minimum(total - GROUP * g, GROUP))
            return carry

        lax.fori_loop(0, (total + GROUP - 1) // GROUP, g_step, 0)
    out[...] = kbuf[...].T


def contract(codex, codep, meta, sig, bq, bp, vt, dexp):
    smem = pl.BlockSpec(memory_space=pltpu.SMEM)
    vmem = pl.BlockSpec(memory_space=pltpu.VMEM)
    return pl.pallas_call(
        contract_kernel,
        out_shape=jax.ShapeDtypeStruct((256, 256), F32),
        in_specs=[smem] * 3 + [vmem] * 5,
        out_specs=vmem,
        scratch_shapes=[
            pltpu.VMEM((256 + CHUNK, 9, 8, 128), F32),
            pltpu.VMEM((192, GROUP // 2, 16, 128), BF16),
            pltpu.VMEM(((256 + CHUNK) * 8, 256), F32),
            pltpu.VMEM((256, 2048), BF16),
            pltpu.VMEM((256, 256), F32),
            pltpu.VMEM((256, 256), F32),
        ],
        compiler_params=pltpu.CompilerParams(vmem_limit_bytes=36 << 20),
        name="contract",
    )(codex, codep, meta, sig, bq, bp, vt, dexp)


ROWS = 288
XDIRECT = True


def place():
    m, z = lax.axis_index("map"), lax.axis_index("row")
    return m, (m // 2) % 4, m // 8, z, m % 2


def at_map(x, y, c):
    return (y * 4 + x) * 2 + c


def greet(devices, between=None):
    barrier = pltpu.get_barrier_semaphore()
    for d in devices:
        pl.semaphore_signal(barrier, inc=1, device_id=d, device_id_type=MESH)
    if between is not None:
        between()
    pl.semaphore_wait(barrier, len(devices))


def tables(nq, nn, whole_block, half_block, row_start, parity, codex, codep, meta, sig):
    g = iota((256, 1), 0)
    wide = iota((256, 256), 1)
    lane = iota((256, 128), 1)

    def column(ref, field):
        rows = []
        for t in range(32):
            c, s, u = t // 16, (t // 4) % 4, t % 4
            rows.append(ref[c, s, u, pl.ds(field, 8, stride=0), :])
        spread = jnp.concatenate(rows, axis=0)
        return jnp.sum(jnp.where(lane == g % 8, spread, 0.0), axis=1, keepdims=True).astype(I32)

    def across(col):
        return jnp.sum(jnp.where(wide == g, col.astype(F32), 0.0), axis=0, keepdims=True).astype(I32)

    def lanes(hit):
        return jnp.sum(hit.astype(F32), axis=1, keepdims=True).astype(I32)

    def rows(hit):
        return jnp.sum(hit.astype(F32), axis=0, keepdims=True).astype(I32)

    def rank(col):
        other = across(col)
        return lanes((other < col) | ((other == col) & (wide < g)))

    def put(where, at, code, rest):
        return rest + jnp.sum(jnp.where(where == at, (code - rest).astype(F32), 0.0), axis=0, keepdims=True).astype(I32)

    first, second, q = column(nq, 0), column(nq, 1), column(nq, 2) - row_start
    by_n = rank(second)
    starts = rows(second < lane)
    sig_at = iota((256, 2048), 1)
    where = jnp.sum(jnp.where(by_n == sig_at // 8, first.astype(F32), 0.0), axis=0, keepdims=True).astype(I32)
    inner = iota((1, 2048), 1) % 8
    sig[...] = jnp.where(inner < 6, 6 * where + inner, -1)
    other = across(q)
    within = lanes((other == q) & (wide < g))
    chunks_row = (rows(q == lane) + 7) // 8
    n16, l16 = iota((16, 128), 0), iota((16, 128), 1)
    ends_col = jnp.sum(jnp.where(l16 <= n16, chunks_row.astype(F32), 0.0), axis=1, keepdims=True).astype(I32)
    lead = jnp.sum(jnp.where(lane < q, chunks_row.astype(F32), 0.0), axis=1, keepdims=True).astype(I32)
    codex[...] = put(8 * lead + within, iota((256, 512), 1), g + by_n * 256, 256 * 256)
    at128 = iota((1, 128), 1)
    chunk_q = jnp.minimum(rows((ends_col <= l16 - 40) & (n16 < 12)), 11)
    total = jnp.sum(chunks_row.astype(F32), axis=1, keepdims=True).astype(I32)
    p = column(nn, 2)
    key = jnp.where(p == whole_block, 0, jnp.where(p == half_block, 1, 2))
    piece = g // 8
    place_of = ((piece // 16) * 16 + (piece % 4) * 4 + (piece // 4) % 4) * 8 + g % 8
    codep[...] = put(rank(key), wide, place_of + column(nn, 1) * 256 + column(nn, 0) * 8192, 0)
    n0, n1 = rows(key == 0), rows(key == 1)
    meta[...] = jnp.where(at128 < 33, starts, jnp.where(at128 == 33, n0, jnp.where(at128 == 34, n1, jnp.where(at128 == 35, total, jnp.where(at128 == 36, parity, jnp.where(at128 < 40, 0, chunk_q))))))


def gather_kernel(own, triples, offsets, dens, v, wide_q, wide_p, vt_out, dexp_out, codex, codep, meta, sig, bq, bp, stage, dall, held, vbuf, spread, s_send, s_z, s_d, s_ax, s_ay, s_as, s_by, s_bx, s_bs, s_loc, nq, nn, nz, s_nz, s_nx, s_ny, s_my, s_mx, s_ns):
    m, x, y, z, c = place()
    way = 1 - 2 * c
    o = 1 - c

    def r4(v):
        return lax.rem(v + 8, 4)

    def dev(xx, yy, zz, cc):
        return (at_map(r4(xx), r4(yy), cc), r4(zz))

    sib = dev(x, y, z, o)
    own_piece = bq.at[y, x]
    first = [
        pltpu.make_async_copy(own, bq.at[y, x], s_loc.at[0]),
        pltpu.make_async_copy(dens, dall.at[z], s_loc.at[2]),
        pltpu.make_async_copy(v, held, s_loc.at[3]),
    ]
    for d in first:
        d.start()

    def between():
        r, k = iota((384, 288), 0), iota((384, 288), 1)
        block, j, i = r // 48, (r % 48) // 8, r % 8
        source = jnp.where(i < 6, (i * 6 + j) * 8 + block, -1)
        spread[...] = (k == source).astype(F32).astype(BF16)
        row, lane = iota((8, 128), 0), iota((8, 128), 1)
        tile = jnp.zeros((8, 128), F32)
        for k in range(8):
            a, l, p = offsets[triples[0, k]] // 6, offsets[triples[1, k]] // 6, triples[2, k]
            tile = jnp.where(lane == k, jnp.where(row == 0, a, jnp.where(row == 1, l, p)).astype(F32), tile)
        nq[c, y, x] = tile
        nz[z] = tile
        for d in first[:2]:
            d.wait()

    greet([dev(x + s, y, z, c) for s in (1, 2, 3)] + [dev(x, y + s, z, c) for s in (1, 2, 3)] + [dev(x, y, z + s, c) for s in (1, 2, 3)] + [sib], between)
    sends = []

    def send(src, dst, recv, device):
        n = len(sends)
        d = pltpu.make_async_remote_copy(src_ref=src, dst_ref=dst, send_sem=s_send.at[n], recv_sem=recv, device_id=device, device_id_type=MESH)
        d.start()
        sends.append(d)

    def arrive(dst, recv):
        pltpu.make_async_remote_copy(src_ref=dst, dst_ref=dst, send_sem=s_send.at[0], recv_sem=recv, device_id=sib, device_id_type=MESH).wait_recv()

    def widen(yq, xq, yp, xp):
        two = jnp.concatenate([bq[yq, xq], bp[yp, xp]], axis=1)
        got = jnp.dot(spread[...], two, preferred_element_type=F32).astype(BF16)
        wide_q[c, yq, xq] = got[:, :128]
        wide_p[c, yp, xp] = got[:, 128:]
        send(wide_q.at[c, yq, xq], wide_q.at[c, yq, xq], s_as.at[yq, xq], sib)
        send(wide_p.at[c, yp, xp], wide_p.at[c, yp, xp], s_bs.at[yp, xp], sib)

    peers = (1, 3, 2)
    for s in peers:
        send(own_piece, stage.at[z], s_z.at[z], dev(x, y, z + s, c))
    for s in peers if XDIRECT else (1, 3):
        send(own_piece, own_piece, s_ax.at[x], dev(x + s, y, z, c))
    for s in (1, 3):
        send(own_piece, own_piece, s_ay.at[y, x], dev(x, y + s, z, c))
    for s in peers:
        send(nz.at[z], nz.at[z], s_nz.at[z], dev(x, y, z + s, c))
        send(nq.at[c, y, x], nq.at[c, y, x], s_nx.at[x], dev(x + s, y, z, c))
    for s in peers:
        send(dall.at[z], dall.at[z], s_d.at[z], dev(x, y, z + s, c))
    keep = pltpu.make_async_copy(own_piece, stage.at[z], s_loc.at[0])
    keep.start()
    for s in peers:
        arrive(stage.at[r4(z + s)], s_z.at[r4(z + s)])
    keep.wait()
    for s in peers:
        yt = r4(y + s)
        send(stage.at[yt], bp.at[y, x], s_by.at[y], dev(x, yt, z, c))
    for s in peers:
        arrive(nz.at[r4(z + s)], s_nz.at[r4(z + s)])
    nn[c, x, y] = nz[y]
    for s in peers:
        yt = r4(y + s)
        send(nz.at[yt], nn.at[c, x, y], s_my.at[y], dev(x, yt, z, c))
    mine = pltpu.make_async_copy(stage.at[y], bp.at[y, x], s_loc.at[1])
    mine.start()
    for s in (1, 3):
        send(stage.at[y], bp.at[y, x], s_bx.at[y, x], dev(x + s, y, z, c))

    xf, xb, x2 = r4(x - way), r4(x + way), r4(x + 2)
    yf, yb, y2 = r4(y - way), r4(y + way), r4(y + 2)
    for xx in (xf, xb, x2):
        arrive(bq.at[y, xx], s_ax.at[xx])
        if not XDIRECT and xx is xf:
            send(bq.at[y, xx], bq.at[y, xx], s_ax.at[xx], dev(x + way, y, z, c))
        for s in (1, 3):
            send(bq.at[y, xx], bq.at[y, xx], s_ay.at[y, xx], dev(x, y + s, z, c))
    for xx in (xf, xb, x2):
        arrive(nq.at[c, y, xx], s_nx.at[xx])
    for s in peers:
        send(nq.at[c, y], nq.at[c, y], s_ny.at[y], dev(x, y + s, z, c))
    for yy in (yf, yb, y2):
        arrive(bp.at[yy, x], s_by.at[yy])
        for s in (1, 3):
            send(bp.at[yy, x], bp.at[yy, x], s_bx.at[yy, x], dev(x + s, y, z, c))
    for yy in (yf, yb, y2):
        arrive(nn.at[c, x, yy], s_my.at[yy])
    for s in peers:
        send(nn.at[c, x], nn.at[c, x], s_mx.at[x], dev(x + s, y, z, c))
    mine.wait()
    widen(y, x, y, x)
    for xx, yy in ((x, y), (xf, yf), (xb, yb), (x2, y2)):
        arrive(bq.at[yf, xx], s_ay.at[yf, xx])
        send(bq.at[yf, xx], bq.at[yf, xx], s_ay.at[yf, xx], dev(x, y + way, z, c))
        arrive(bp.at[yy, xf], s_bx.at[yy, xf])
        send(bp.at[yy, xf], bp.at[yy, xf], s_bx.at[yy, xf], dev(x + way, y, z, c))
        if xx is not x:
            widen(y, xx, yy, x)
        widen(yf, xx, yy, xf)
    for s in peers:
        arrive(nq.at[c, r4(y + s)], s_ny.at[r4(y + s)])
        arrive(nn.at[c, r4(x + s)], s_mx.at[r4(x + s)])
    send(nq.at[c], nq.at[c], s_ns.at[0], sib)
    send(nn.at[c], nn.at[c], s_ns.at[1], sib)
    first[2].wait()
    parity = lax.rem(m, 2)
    vbuf[0:128] = held[pl.ds(pl.multiple_of(64 * parity, 64), 128), :]
    half = held[pl.ds(pl.multiple_of(128 * (1 - parity), 64), 64), :]
    vbuf[128:192] = half
    vbuf[192:256] = half
    same = (iota((128, 128), 0) == iota((128, 128), 1)).astype(F32).astype(BF16)
    for q in range(12):
        vt_out[q] = lax.dot_general(same, vbuf[:, 128 * q:128 * q + 128], NT, preferred_element_type=F32).astype(BF16)
    for s in peers:
        arrive(dall.at[r4(z + s)], s_d.at[r4(z + s)])
    same = (iota((192, 192), 0) == iota((192, 192), 1)).astype(F32).astype(BF16)
    full = jnp.concatenate([dall[k] for k in range(4)], axis=0)
    turned = lax.dot_general(same, full, NT, preferred_element_type=F32).astype(BF16)
    lam, lane = iota((192, 128), 0), iota((192, 128), 1)
    part = (lane % 64) // 8
    for l in range(32):
        sel = ((lam == 6 * l + part) & (part < 6)).astype(F32).astype(BF16)
        dexp_out[l] = jnp.dot(turned, sel, preferred_element_type=F32)
    arrive(nq.at[o], s_ns.at[0])
    arrive(nn.at[o], s_ns.at[1])
    chip = m // 2
    tables(nq, nn, 3 * chip + 2 * parity, 3 * chip + 1, z * 12, parity, codex, codep, meta, sig)
    for ya, xa in ((yb, xb), (y2, x2)):
        for xx, yy in ((x, y), (xf, yf), (xb, yb), (x2, y2)):
            arrive(bq.at[ya, xx], s_ay.at[ya, xx])
            arrive(bp.at[yy, xa], s_bx.at[yy, xa])
            widen(ya, xx, yy, xa)
    for yy in (y, yf, yb, y2):
        for xx in (x, xf, xb, x2):
            arrive(wide_q.at[o, yy, xx], s_as.at[yy, xx])
            arrive(wide_p.at[o, yy, xx], s_bs.at[yy, xx])
    for d in sends:
        d.wait_send()


def gather(own, triples, offsets, dens, v):
    hbm = pl.BlockSpec(memory_space=pltpu.HBM)
    smem = pl.BlockSpec(memory_space=pltpu.SMEM)
    vmem = pl.BlockSpec(memory_space=pltpu.VMEM)
    dma = pltpu.SemaphoreType.DMA
    return pl.pallas_call(
        gather_kernel,
        out_shape=[
            jax.ShapeDtypeStruct((2, 4, 4, 384, 128), BF16),
            jax.ShapeDtypeStruct((2, 4, 4, 384, 128), BF16),
            jax.ShapeDtypeStruct((12, 128, 256), BF16),
            jax.ShapeDtypeStruct((32, 192, 128), F32),
            jax.ShapeDtypeStruct((1, 512), I32),
            jax.ShapeDtypeStruct((1, 256), I32),
            jax.ShapeDtypeStruct((1, 128), I32),
            jax.ShapeDtypeStruct((1, 2048), I32),
        ],
        in_specs=[hbm, smem, smem, hbm, hbm],
        out_specs=[vmem] * 8,
        scratch_shapes=[
            pltpu.VMEM((4, 4, ROWS, 128), BF16),
            pltpu.VMEM((4, 4, ROWS, 128), BF16),
            pltpu.VMEM((4, ROWS, 128), BF16),
            pltpu.VMEM((4, 48, 192), BF16),
            pltpu.VMEM((192, 1536), BF16),
            pltpu.VMEM((256, 1536), BF16),
            pltpu.VMEM((384, 288), BF16),
            dma((104,)), dma((4,)), dma((4,)), dma((4,)), dma((4, 4)), dma((4, 4)), dma((4,)), dma((4, 4)), dma((4, 4)), dma((4,)),
            pltpu.VMEM((2, 4, 4, 8, 128), F32),
            pltpu.VMEM((2, 4, 4, 8, 128), F32),
            pltpu.VMEM((4, 8, 128), F32),
            dma((4,)), dma((4,)), dma((4,)), dma((4,)), dma((4,)), dma((2,)),
        ],
        compiler_params=pltpu.CompilerParams(collective_id=0, has_side_effects=True, vmem_limit_bytes=24 << 20),
        name="gather",
    )(own, triples, offsets, dens, v)


def reduce_kernel(part, out, got, cut, got2, send1, recv1, send2, recv2):
    m, x, y, z, c = place()
    g = lax.rem(m, 8)
    near = [(y * 8 + lax.rem(g + d, 8), z) for d in range(1, 8)]
    far = []
    for d in range(1, 16):
        h = lax.rem(y * 4 + z + d, 16)
        far.append((h // 4, lax.rem(h, 4)))
    greet(near + [((yy * 8 + g), zz) for yy, zz in far])
    first = []
    for d in range(1, 8):
        gg = lax.rem(g + d, 8)
        cp = pltpu.make_async_remote_copy(src_ref=part.at[:, gg], dst_ref=got.at[g], send_sem=send1.at[d], recv_sem=recv1.at[g], device_id=near[d - 1], device_id_type=MESH)
        cp.start()
        first.append(cp)
    got[g] = part[:, g]
    cut[...] = jnp.zeros_like(cut)
    for d in range(1, 8):
        gg = lax.rem(g + d, 8)
        pltpu.make_async_remote_copy(src_ref=part.at[:, gg], dst_ref=got.at[gg], send_sem=send1.at[d], recv_sem=recv1.at[gg], device_id=near[0], device_id_type=MESH).wait_recv()
    total = got[0]
    for k in range(1, 8):
        total = total + got[k]
    for zz in range(4):
        cut[:, zz, :, 0:48] = total[:, :, 48 * zz:48 * zz + 48]
    second = []
    for d, (yy, zz) in enumerate(far):
        cp = pltpu.make_async_remote_copy(src_ref=cut.at[yy, zz], dst_ref=got2.at[y, z], send_sem=send2.at[d], recv_sem=recv2.at[y, z], device_id=(yy * 8 + g, zz), device_id_type=MESH)
        cp.start()
        second.append(cp)
    got2[y, z] = cut[y, z]
    for yy, zz in far:
        pltpu.make_async_remote_copy(src_ref=cut.at[yy, zz], dst_ref=got2.at[yy, zz], send_sem=send2.at[0], recv_sem=recv2.at[yy, zz], device_id=(yy * 8 + g, zz), device_id_type=MESH).wait_recv()
    for part_of in range(2):
        result = got2[2 * part_of, 0]
        for k in range(1, 8):
            result = result + got2[2 * part_of + k // 4, k % 4]
        out[part_of] = result
    for cp in first + second:
        cp.wait_send()


def reduce(part):
    vmem = pl.BlockSpec(memory_space=pltpu.VMEM)
    dma = pltpu.SemaphoreType.DMA
    return pl.pallas_call(
        reduce_kernel,
        out_shape=jax.ShapeDtypeStruct((2, 8, 128), F32),
        in_specs=[vmem],
        out_specs=vmem,
        scratch_shapes=[
            pltpu.VMEM((8, 4, 8, 256), F32),
            pltpu.VMEM((4, 4, 8, 128), F32),
            pltpu.VMEM((4, 4, 8, 128), F32),
            dma((8,)), dma((8,)), dma((16,)), dma((4, 4)),
        ],
        compiler_params=pltpu.CompilerParams(collective_id=1, has_side_effects=True, vmem_limit_bytes=8 << 20),
        name="reduce",
    )(part)


def body(block_list, block_values, atom_offsets, density, metric_inverse):
    own = block_values.transpose(1, 2, 0, 3).reshape(288, 128)
    bq, bp, vt, dexp, codex, codep, meta, sig = gather(*[pltpu.with_memory_space_constraint(t, pltpu.HBM) for t in (own, block_list.T, atom_offsets, density, metric_inverse)])
    part = contract(codex, codep, meta, sig, bq.reshape(256, 48, 128), bp.reshape(256, 48, 128), vt, dexp)
    sums = reduce(part.reshape(4, 8, 8, 256))
    return sums[0, :6, :48] + sums[1, :6, :48]


def solution(mesh):
    placed = (
        P(("map", "row"), None),
        P(("map", "row"), None, None, None),
        P(),
        P("row", None),
        P("map", "row"),
    )
    return jax.shard_map(
        body, mesh=mesh, in_specs=placed, out_specs=P("map", "row"), check_vma=False
    )
```

```python
import jax
import jax.numpy as jnp
from jax import lax
from jax.experimental import pallas as pl
from jax.experimental.pallas import tpu as pltpu
from jax.sharding import PartitionSpec as P

HI = lax.Precision.HIGHEST
F32, BF16, I32 = jnp.float32, jnp.bfloat16, jnp.int32
NT = (((1,), (1,)), ((), ()))
MESH = pl.DeviceIdType.MESH
GROUP = 32
CHUNK = 16
XROWS = 44
XUN = 4
HN = 48
NB = 16


def iota(shape, axis):
    return lax.broadcasted_iota(I32, shape, axis)


def contract_kernel(codex, codep, meta, sig, bq, bp, vt, dexp, out, xbuf, hbuf, obuf, sbuf, ebuf, kbuf):
    nf, nh = meta[0, 33], meta[0, 34]
    low_half = iota((8, 128), 1) < 64

    def x_step(step, carry):
        for w in range(XUN):
            ch = XUN * step + w
            src = [codex[0, 8 * ch + u] for u in range(8)]
            rows = jnp.concatenate([bq[s & 255] for s in src], axis=0)
            x = jnp.dot(rows, vt[meta[0, 40 + ch]], preferred_element_type=F32)
            for u in range(8):
                tiles = [x[48 * u + 8 * j:48 * u + 8 * j + 8] for j in range(6)]
                whole = [t[:, :128] for t in tiles]
                half = [jnp.where(low_half, tiles[2 * j][:, 128:], tiles[2 * j + 1][:, 128:]) for j in range(3)]
                xbuf[src[u] >> 8] = jnp.stack(whole + half)
        return carry

    lax.fori_loop(0, (meta[0, 35] + XUN - 1) // XUN, x_step, 0)
    kbuf[...] = jnp.zeros_like(kbuf)
    ebuf[...] = jnp.zeros_like(ebuf)
    sbuf[...] = (iota((256, 2048), 0) == sig[...]).astype(F32).astype(BF16)
    lane, sub = iota((8, 128), 1), iota((8, 128), 0)
    low_mask = (lane % 8 == sub) & (lane < 64)
    high_mask = (lane % 8 == sub) & (lane >= 64)
    row, col = iota((8, 256), 0), iota((8, 256), 1)
    even_device = (iota((64, 128), 0) * 0 + meta[0, 36]) == 0
    left_lanes = iota((64, 128), 1) < 64
    none = jnp.zeros((64, 128), BF16)
    def spread(ld, nu_a, lb, nu_b):
        a = dexp[ld, pl.ds(nu_a, 8, stride=0), :]
        b = dexp[lb, pl.ds(nu_b, 8, stride=0), :]
        return jnp.where(low_mask, a, jnp.where(high_mask, b, 0.0))

    def pair(h):
        n = h.shape[0] // 8
        both = jnp.concatenate([h[:, :128].reshape(n, 8, 128), h[:, 128:].reshape(n, 8, 128)], axis=1)
        return both.astype(BF16)

    def group(half, base, cnt):
        def h_step(t2, carry):
            at, ls = [], []
            for u in range(2):
                t = base + jnp.minimum(2 * t2 + u, cnt - 1)
                code = codep[0, t]
                at.append(code & 255)
                ls.append((code >> 8) & 31)
                ebuf[pl.ds(pl.multiple_of(16 * t2 + 8 * u, 8), 8), :] = (col == 8 * (code >> 13) + row).astype(F32)
            b0, b1 = [jnp.concatenate([bp[k], none[:16]], axis=0) for k in at]
            if not half:
                rhs = jnp.concatenate([jnp.concatenate([b0, none], axis=1), jnp.concatenate([none, b1], axis=1)], axis=0)
                for c in range(0, 192, HN):
                    w = jnp.concatenate([spread(ls[0], nu, ls[1], nu) for nu in range(c, c + HN)], axis=0).astype(BF16)
                    hbuf[c:c + HN, t2] = pair(jnp.dot(w, rhs, preferred_element_type=F32))
            else:
                quads = []
                for b in (b0, b1):
                    wide = b.astype(F32)
                    turned = pltpu.roll(wide, 64, 1)
                    first = jnp.where(even_device, wide, turned)
                    second = jnp.where(even_device, turned, wide)
                    quads.append((jnp.where(left_lanes, first, 0.0).astype(BF16), jnp.where(left_lanes, 0.0, second).astype(BF16)))
                (e0, o0), (e1, o1) = quads
                rhs = jnp.concatenate([jnp.concatenate([p, q], axis=1) for p, q in ((e0, none), (o0, none), (none, e1), (none, o1))], axis=0)
                for c in range(0, 96, HN):
                    w = jnp.concatenate([
                        jnp.concatenate([spread(l, 2 * r, l, 2 * r + 1) for r in range(c, c + HN)], axis=0).astype(BF16)
                        for l in ls], axis=1)
                    hbuf[c:c + HN, t2] = pair(jnp.dot(w, rhs, preferred_element_type=F32))
            return carry

        lax.fori_loop(0, (cnt + 1) // 2, h_step, 0)
        depth, first = (3, 6) if half else (6, 0)

        def chunk(n, k0):
            xs = jnp.concatenate([xbuf[pl.ds(k0, CHUNK), first + j].reshape(CHUNK * 8, 128).astype(BF16) for j in range(depth)], axis=1)
            hs = jnp.concatenate([hbuf[n * depth + j].reshape(GROUP * 8, 128) for j in range(depth)], axis=1)
            o = lax.dot_general(xs, hs, NT, preferred_element_type=F32)
            obuf[pl.ds(pl.multiple_of(8 * k0, 8), CHUNK * 8), :] = o

        def n_step(i, carry):
            ends = [meta[0, NB * i + u] for u in range(NB + 1)]
            for u in range(NB):
                chunk(NB * i + u, ends[u])
            longest = ends[1] - ends[0]
            for u in range(1, NB):
                longest = jnp.maximum(longest, ends[u + 1] - ends[u])

            @pl.when(longest > CHUNK)
            def _():
                def again(n, carry):
                    s0, s1 = meta[0, n], meta[0, n + 1]

                    def c_step(c, carry):
                        chunk(n, s0 + CHUNK * c)
                        return carry

                    return lax.fori_loop(0, (s1 - s0 + CHUNK - 1) // CHUNK, c_step, carry)

                lax.fori_loop(NB * i, NB * i + NB, again, 0)
            return carry

        lax.fori_loop(0, 32 // NB, n_step, 0)
        r = jnp.zeros((256, 256), F32)
        for k in range(8):
            o = obuf[256 * k:256 * k + 256, :]
            high = o.astype(BF16)
            s = sbuf[:, 256 * k:256 * k + 256]
            r += jnp.dot(s, high, preferred_element_type=F32)
        r = jnp.where(iota((256, 256), 1) < 8 * cnt, r, 0.0)
        e = ebuf[...].astype(BF16)
        high = r.astype(BF16)
        low = (r - high.astype(F32)).astype(BF16)
        kbuf[...] += jnp.dot(high, e, preferred_element_type=F32) + jnp.dot(low, e, preferred_element_type=F32)

    for half, base, total in ((False, 0, nf), (True, nf, nh)):
        def g_step(g, carry, half=half, base=base, total=total):
            group(half, base + GROUP * g, jnp.minimum(total - GROUP * g, GROUP))
            return carry

        lax.fori_loop(0, (total + GROUP - 1) // GROUP, g_step, 0)
    out[...] = kbuf[...].T.astype(BF16)


def contract(codex, codep, meta, sig, bq, bp, vt, dexp):
    smem = pl.BlockSpec(memory_space=pltpu.SMEM)
    vmem = pl.BlockSpec(memory_space=pltpu.VMEM)
    return pl.pallas_call(
        contract_kernel,
        out_shape=jax.ShapeDtypeStruct((256, 256), BF16),
        in_specs=[smem] * 3 + [vmem] * 5,
        out_specs=vmem,
        scratch_shapes=[
            pltpu.VMEM((256 + CHUNK, 9, 8, 128), F32),
            pltpu.VMEM((192, GROUP // 2, 16, 128), BF16),
            pltpu.VMEM(((256 + CHUNK) * 8, 256), F32),
            pltpu.VMEM((256, 2048), BF16),
            pltpu.VMEM((256, 256), F32),
            pltpu.VMEM((256, 256), F32),
        ],
        compiler_params=pltpu.CompilerParams(vmem_limit_bytes=36 << 20),
        name="contract",
    )(codex, codep, meta, sig, bq, bp, vt, dexp)


ROWS = 288
XDIRECT = True


def place():
    m, z = lax.axis_index("map"), lax.axis_index("row")
    return m, (m // 2) % 4, m // 8, z, m % 2


def at_map(x, y, c):
    return (y * 4 + x) * 2 + c


def greet(devices, between=None):
    barrier = pltpu.get_barrier_semaphore()
    for d in devices:
        pl.semaphore_signal(barrier, inc=1, device_id=d, device_id_type=MESH)
    if between is not None:
        between()
    pl.semaphore_wait(barrier, len(devices))


def tables(nq, nn, whole_block, half_block, row_start, parity, codex, codep, meta, sig):
    g = iota((256, 1), 0)
    wide = iota((256, 256), 1)
    lane = iota((256, 128), 1)

    def column(ref, field):
        rows = []
        for t in range(32):
            c, s, u = t // 16, (t // 4) % 4, t % 4
            rows.append(ref[c, s, u, pl.ds(field, 8, stride=0), :])
        spread = jnp.concatenate(rows, axis=0)
        return jnp.sum(jnp.where(lane == g % 8, spread, 0.0), axis=1, keepdims=True).astype(I32)

    def across(col):
        return jnp.sum(jnp.where(wide == g, col.astype(F32), 0.0), axis=0, keepdims=True).astype(I32)

    def lanes(hit):
        return jnp.sum(hit.astype(F32), axis=1, keepdims=True).astype(I32)

    def rows(hit):
        return jnp.sum(hit.astype(F32), axis=0, keepdims=True).astype(I32)

    def rank(col):
        other = across(col)
        return lanes((other < col) | ((other == col) & (wide < g)))

    def put(where, at, code, rest):
        return rest + jnp.sum(jnp.where(where == at, (code - rest).astype(F32), 0.0), axis=0, keepdims=True).astype(I32)

    first, second, q = column(nq, 0), column(nq, 1), column(nq, 2) - row_start
    by_n = rank(second)
    starts = rows(second < lane)
    sig_at = iota((256, 2048), 1)
    where = jnp.sum(jnp.where(by_n == sig_at // 8, first.astype(F32), 0.0), axis=0, keepdims=True).astype(I32)
    inner = iota((1, 2048), 1) % 8
    sig[...] = jnp.where(inner < 6, 6 * where + inner, -1)
    other = across(q)
    within = lanes((other == q) & (wide < g))
    chunks_row = (rows(q == lane) + 7) // 8
    n16, l16 = iota((16, 128), 0), iota((16, 128), 1)
    ends_col = jnp.sum(jnp.where(l16 <= n16, chunks_row.astype(F32), 0.0), axis=1, keepdims=True).astype(I32)
    lead = jnp.sum(jnp.where(lane < q, chunks_row.astype(F32), 0.0), axis=1, keepdims=True).astype(I32)
    codex[...] = put(8 * lead + within, iota((256, 512), 1), g + by_n * 256, 256 * 256)
    at128 = iota((1, 128), 1)
    chunk_q = jnp.minimum(rows((ends_col <= l16 - 40) & (n16 < 12)), 11)
    total = jnp.sum(chunks_row.astype(F32), axis=1, keepdims=True).astype(I32)
    p = column(nn, 2)
    key = jnp.where(p == whole_block, 0, jnp.where(p == half_block, 1, 2))
    piece = g // 8
    place_of = ((piece // 16) * 16 + (piece % 4) * 4 + (piece // 4) % 4) * 8 + g % 8
    codep[...] = put(rank(key), wide, place_of + column(nn, 1) * 256 + column(nn, 0) * 8192, 0)
    n0, n1 = rows(key == 0), rows(key == 1)
    meta[...] = jnp.where(at128 < 33, starts, jnp.where(at128 == 33, n0, jnp.where(at128 == 34, n1, jnp.where(at128 == 35, total, jnp.where(at128 == 36, parity, jnp.where(at128 < 40, 0, chunk_q))))))


def gather_kernel(own, triples, offsets, dens, v, wide_q, wide_p, vt_out, dexp_out, codex, codep, meta, sig, bq, bp, stage, dall, held, vbuf, spread, s_send, s_z, s_d, s_ax, s_ay, s_as, s_by, s_bx, s_bs, s_loc, nq, nn, nz, s_nz, s_nx, s_ny, s_my, s_mx, s_ns, s_plane):
    m, x, y, z, c = place()
    way = 1 - 2 * c
    o = 1 - c

    def r4(v):
        return lax.rem(v + 8, 4)

    def dev(xx, yy, zz, cc):
        return (at_map(r4(xx), r4(yy), cc), r4(zz))

    sib = dev(x, y, z, o)
    own_piece = bq.at[y, x]
    first = [
        pltpu.make_async_copy(own, bq.at[y, x], s_loc.at[0]),
        pltpu.make_async_copy(dens, dall.at[z], s_loc.at[2]),
        pltpu.make_async_copy(v, held, s_loc.at[3]),
    ]
    for d in first:
        d.start()

    def between():
        r, k = iota((384, 288), 0), iota((384, 288), 1)
        block, j, i = r // 48, (r % 48) // 8, r % 8
        source = jnp.where(i < 6, (i * 6 + j) * 8 + block, -1)
        spread[...] = (k == source).astype(F32).astype(BF16)
        row, lane = iota((8, 128), 0), iota((8, 128), 1)
        tile = jnp.zeros((8, 128), F32)
        for k in range(8):
            a, l, p = offsets[triples[0, k]] // 6, offsets[triples[1, k]] // 6, triples[2, k]
            tile = jnp.where(lane == k, jnp.where(row == 0, a, jnp.where(row == 1, l, p)).astype(F32), tile)
        nq[c, y, x] = tile
        nz[z] = tile
        for d in first[:2]:
            d.wait()

    greet([dev(x + s, y, z, c) for s in (1, 2, 3)] + [dev(x, y + s, z, c) for s in (1, 2, 3)] + [dev(x, y, z + s, c) for s in (1, 2, 3)] + [sib], between)
    sends = []

    def send(src, dst, recv, device):
        n = len(sends)
        d = pltpu.make_async_remote_copy(src_ref=src, dst_ref=dst, send_sem=s_send.at[n], recv_sem=recv, device_id=device, device_id_type=MESH)
        d.start()
        sends.append(d)

    def arrive(dst, recv):
        pltpu.make_async_remote_copy(src_ref=dst, dst_ref=dst, send_sem=s_send.at[0], recv_sem=recv, device_id=sib, device_id_type=MESH).wait_recv()

    def widen(yq, xq, yp, xp):
        two = jnp.concatenate([bq[yq, xq], bp[yp, xp]], axis=1)
        got = jnp.dot(spread[...], two, preferred_element_type=F32).astype(BF16)
        wide_q[c, yq, xq] = got[:, :128]
        wide_p[c, yp, xp] = got[:, 128:]
        send(wide_q.at[c, yq, xq], wide_q.at[c, yq, xq], s_as.at[yq, xq], sib)
        send(wide_p.at[c, yp, xp], wide_p.at[c, yp, xp], s_bs.at[yp, xp], sib)

    peers = (1, 3, 2)

    def to_plane(src, zz, n):
        return pltpu.make_async_remote_copy(src_ref=src, dst_ref=bp.at[y, x], send_sem=s_plane.at[n], recv_sem=s_by.at[y], device_id=dev(x, zz, z, c), device_id_type=MESH)

    for s in peers:
        send(own_piece, stage.at[z], s_z.at[z], dev(x, y, z + s, c))
    for s in peers if XDIRECT else (1, 3):
        send(own_piece, own_piece, s_ax.at[x], dev(x + s, y, z, c))
    for s in (1, 3):
        send(own_piece, own_piece, s_ay.at[y, x], dev(x, y + s, z, c))
    for s in peers:
        send(nz.at[z], nz.at[z], s_nz.at[z], dev(x, y, z + s, c))
        send(nq.at[c, y, x], nq.at[c, y, x], s_nx.at[x], dev(x + s, y, z, c))
    for s in peers:
        send(dall.at[z], dall.at[z], s_d.at[z], dev(x, y, z + s, c))
    @pl.when(z != y)
    def _():
        to_plane(own_piece, z, 0).start()

    keep = pltpu.make_async_copy(own_piece, stage.at[z], s_loc.at[0])
    keep.start()
    for n, s in enumerate(peers):
        zz = r4(z + s)
        arrive(stage.at[zz], s_z.at[zz])

        @pl.when(zz != y)
        def _(zz=zz, n=n):
            to_plane(stage.at[zz], zz, n + 1).start()

    keep.wait()
    for s in peers:
        arrive(nz.at[r4(z + s)], s_nz.at[r4(z + s)])
    nn[c, x, y] = nz[y]
    for s in peers:
        yt = r4(y + s)
        send(nz.at[yt], nn.at[c, x, y], s_my.at[y], dev(x, yt, z, c))
    mine = pltpu.make_async_copy(stage.at[y], bp.at[y, x], s_loc.at[1])
    mine.start()
    for s in (1, 3):
        send(stage.at[y], bp.at[y, x], s_bx.at[y, x], dev(x + s, y, z, c))

    xf, xb, x2 = r4(x - way), r4(x + way), r4(x + 2)
    yf, yb, y2 = r4(y - way), r4(y + way), r4(y + 2)
    for xx in (xf, xb, x2):
        arrive(bq.at[y, xx], s_ax.at[xx])
        if not XDIRECT and xx is xf:
            send(bq.at[y, xx], bq.at[y, xx], s_ax.at[xx], dev(x + way, y, z, c))
        for s in (1, 3):
            send(bq.at[y, xx], bq.at[y, xx], s_ay.at[y, xx], dev(x, y + s, z, c))
    for xx in (xf, xb, x2):
        arrive(nq.at[c, y, xx], s_nx.at[xx])
    for s in peers:
        send(nq.at[c, y], nq.at[c, y], s_ny.at[y], dev(x, y + s, z, c))
    for yy in (yf, yb, y2):
        arrive(bp.at[yy, x], s_by.at[yy])
        for s in (1, 3):
            send(bp.at[yy, x], bp.at[yy, x], s_bx.at[yy, x], dev(x + s, y, z, c))
    for yy in (yf, yb, y2):
        arrive(nn.at[c, x, yy], s_my.at[yy])
    for s in peers:
        send(nn.at[c, x], nn.at[c, x], s_mx.at[x], dev(x + s, y, z, c))
    mine.wait()
    widen(y, x, y, x)
    for xx, yy in ((x, y), (xf, yf), (xb, yb), (x2, y2)):
        arrive(bq.at[yf, xx], s_ay.at[yf, xx])
        send(bq.at[yf, xx], bq.at[yf, xx], s_ay.at[yf, xx], dev(x, y + way, z, c))
        arrive(bp.at[yy, xf], s_bx.at[yy, xf])
        send(bp.at[yy, xf], bp.at[yy, xf], s_bx.at[yy, xf], dev(x + way, y, z, c))
        if xx is not x:
            widen(y, xx, yy, x)
        widen(yf, xx, yy, xf)
    for s in peers:
        arrive(nq.at[c, r4(y + s)], s_ny.at[r4(y + s)])
        arrive(nn.at[c, r4(x + s)], s_mx.at[r4(x + s)])
    send(nq.at[c], nq.at[c], s_ns.at[0], sib)
    send(nn.at[c], nn.at[c], s_ns.at[1], sib)
    first[2].wait()
    parity = lax.rem(m, 2)
    vbuf[0:128] = held[pl.ds(pl.multiple_of(64 * parity, 64), 128), :]
    half = held[pl.ds(pl.multiple_of(128 * (1 - parity), 64), 64), :]
    vbuf[128:192] = half
    vbuf[192:256] = half
    same = (iota((128, 128), 0) == iota((128, 128), 1)).astype(F32).astype(BF16)
    for q in range(12):
        vt_out[q] = lax.dot_general(same, vbuf[:, 128 * q:128 * q + 128], NT, preferred_element_type=F32).astype(BF16)
    for s in peers:
        arrive(dall.at[r4(z + s)], s_d.at[r4(z + s)])
    same = (iota((192, 192), 0) == iota((192, 192), 1)).astype(F32).astype(BF16)
    full = jnp.concatenate([dall[k] for k in range(4)], axis=0)
    turned = lax.dot_general(same, full, NT, preferred_element_type=F32).astype(BF16)
    lam, lane = iota((192, 128), 0), iota((192, 128), 1)
    part = (lane % 64) // 8
    for l in range(32):
        sel = ((lam == 6 * l + part) & (part < 6)).astype(F32).astype(BF16)
        dexp_out[l] = jnp.dot(turned, sel, preferred_element_type=F32)
    arrive(nq.at[o], s_ns.at[0])
    arrive(nn.at[o], s_ns.at[1])
    chip = m // 2
    tables(nq, nn, 3 * chip + 2 * parity, 3 * chip + 1, z * 12, parity, codex, codep, meta, sig)
    for ya, xa in ((yb, xb), (y2, x2)):
        for xx, yy in ((x, y), (xf, yf), (xb, yb), (x2, y2)):
            arrive(bq.at[ya, xx], s_ay.at[ya, xx])
            arrive(bp.at[yy, xa], s_bx.at[yy, xa])
            widen(ya, xx, yy, xa)
    for yy in (y, yf, yb, y2):
        for xx in (x, xf, xb, x2):
            arrive(wide_q.at[o, yy, xx], s_as.at[yy, xx])
            arrive(wide_p.at[o, yy, xx], s_bs.at[yy, xx])
    for n, s in enumerate((0,) + peers):
        zz = r4(z + s)

        @pl.when(zz != y)
        def _(zz=zz, n=n):
            to_plane(own_piece if n == 0 else stage.at[zz], zz, n).wait_send()

    for d in sends:
        d.wait_send()


def gather(own, triples, offsets, dens, v):
    hbm = pl.BlockSpec(memory_space=pltpu.HBM)
    smem = pl.BlockSpec(memory_space=pltpu.SMEM)
    vmem = pl.BlockSpec(memory_space=pltpu.VMEM)
    dma = pltpu.SemaphoreType.DMA
    return pl.pallas_call(
        gather_kernel,
        out_shape=[
            jax.ShapeDtypeStruct((2, 4, 4, 384, 128), BF16),
            jax.ShapeDtypeStruct((2, 4, 4, 384, 128), BF16),
            jax.ShapeDtypeStruct((12, 128, 256), BF16),
            jax.ShapeDtypeStruct((32, 192, 128), F32),
            jax.ShapeDtypeStruct((1, 512), I32),
            jax.ShapeDtypeStruct((1, 256), I32),
            jax.ShapeDtypeStruct((1, 128), I32),
            jax.ShapeDtypeStruct((1, 2048), I32),
        ],
        in_specs=[hbm, smem, smem, hbm, hbm],
        out_specs=[vmem] * 8,
        scratch_shapes=[
            pltpu.VMEM((4, 4, ROWS, 128), BF16),
            pltpu.VMEM((4, 4, ROWS, 128), BF16),
            pltpu.VMEM((4, ROWS, 128), BF16),
            pltpu.VMEM((4, 48, 192), BF16),
            pltpu.VMEM((192, 1536), BF16),
            pltpu.VMEM((256, 1536), BF16),
            pltpu.VMEM((384, 288), BF16),
            dma((104,)), dma((4,)), dma((4,)), dma((4,)), dma((4, 4)), dma((4, 4)), dma((4,)), dma((4, 4)), dma((4, 4)), dma((4,)),
            pltpu.VMEM((2, 4, 4, 8, 128), F32),
            pltpu.VMEM((2, 4, 4, 8, 128), F32),
            pltpu.VMEM((4, 8, 128), F32),
            dma((4,)), dma((4,)), dma((4,)), dma((4,)), dma((4,)), dma((2,)), dma((4,)),
        ],
        compiler_params=pltpu.CompilerParams(collective_id=0, has_side_effects=True, vmem_limit_bytes=24 << 20),
        name="gather",
    )(own, triples, offsets, dens, v)


def reduce_kernel(part, out, got, cut, got2, send1, recv1, send2, recv2):
    m, x, y, z, c = place()
    g = lax.rem(m, 8)
    near = [(y * 8 + lax.rem(g + d, 8), z) for d in range(1, 8)]
    far = []
    for d in range(1, 16):
        h = lax.rem(y * 4 + z + d, 16)
        far.append((h // 4, lax.rem(h, 4)))
    greet(near + [((yy * 8 + g), zz) for yy, zz in far])
    first = []
    for d in range(1, 8):
        gg = lax.rem(g + d, 8)
        cp = pltpu.make_async_remote_copy(src_ref=part.at[:, gg], dst_ref=got.at[g], send_sem=send1.at[d], recv_sem=recv1.at[g], device_id=near[d - 1], device_id_type=MESH)
        cp.start()
        first.append(cp)
    got[g] = part[:, g]
    cut[...] = jnp.zeros_like(cut)
    for d in range(1, 8):
        gg = lax.rem(g + d, 8)
        pltpu.make_async_remote_copy(src_ref=part.at[:, gg], dst_ref=got.at[gg], send_sem=send1.at[d], recv_sem=recv1.at[gg], device_id=near[0], device_id_type=MESH).wait_recv()
    total = got[0].astype(F32)
    for k in range(1, 8):
        total = total + got[k].astype(F32)
    for zz in range(4):
        cut[:, zz, :, 0:48] = total[:, :, 48 * zz:48 * zz + 48]
    second = []
    for d, (yy, zz) in enumerate(far):
        cp = pltpu.make_async_remote_copy(src_ref=cut.at[yy, zz], dst_ref=got2.at[y, z], send_sem=send2.at[d], recv_sem=recv2.at[y, z], device_id=(yy * 8 + g, zz), device_id_type=MESH)
        cp.start()
        second.append(cp)
    got2[y, z] = cut[y, z]
    for yy, zz in far:
        pltpu.make_async_remote_copy(src_ref=cut.at[yy, zz], dst_ref=got2.at[yy, zz], send_sem=send2.at[0], recv_sem=recv2.at[yy, zz], device_id=(yy * 8 + g, zz), device_id_type=MESH).wait_recv()
    for part_of in range(2):
        result = got2[2 * part_of, 0]
        for k in range(1, 8):
            result = result + got2[2 * part_of + k // 4, k % 4]
        out[part_of] = result
    for cp in first + second:
        cp.wait_send()


def reduce(part):
    vmem = pl.BlockSpec(memory_space=pltpu.VMEM)
    dma = pltpu.SemaphoreType.DMA
    return pl.pallas_call(
        reduce_kernel,
        out_shape=jax.ShapeDtypeStruct((2, 8, 128), F32),
        in_specs=[vmem],
        out_specs=vmem,
        scratch_shapes=[
            pltpu.VMEM((8, 4, 8, 256), BF16),
            pltpu.VMEM((4, 4, 8, 128), F32),
            pltpu.VMEM((4, 4, 8, 128), F32),
            dma((8,)), dma((8,)), dma((16,)), dma((4, 4)),
        ],
        compiler_params=pltpu.CompilerParams(collective_id=1, has_side_effects=True, vmem_limit_bytes=8 << 20),
        name="reduce",
    )(part)


def body(block_list, block_values, atom_offsets, density, metric_inverse):
    own = block_values.transpose(1, 2, 0, 3).reshape(288, 128)
    bq, bp, vt, dexp, codex, codep, meta, sig = gather(*[pltpu.with_memory_space_constraint(t, pltpu.HBM) for t in (own, block_list.T, atom_offsets, density, metric_inverse)])
    part = contract(codex, codep, meta, sig, bq.reshape(256, 48, 128), bp.reshape(256, 48, 128), vt, dexp)
    sums = reduce(part.reshape(4, 8, 8, 256))
    return sums[0, :6, :48] + sums[1, :6, :48]


def solution(mesh):
    placed = (
        P(("map", "row"), None),
        P(("map", "row"), None, None, None),
        P(),
        P("row", None),
        P("map", "row"),
    )
    return jax.shard_map(
        body, mesh=mesh, in_specs=placed, out_specs=P("map", "row"), check_vma=False
    )
```

```python
import jax
import jax.numpy as jnp
from jax import lax
from jax.experimental import pallas as pl
from jax.experimental.pallas import tpu as pltpu
from jax.sharding import PartitionSpec as P

HI = lax.Precision.HIGHEST
F32, BF16, I32 = jnp.float32, jnp.bfloat16, jnp.int32
NT = (((1,), (1,)), ((), ()))
MESH = pl.DeviceIdType.MESH
GROUP = 32
CHUNK = 16
XROWS = 44
XUN = 4
HN = 48
NB = 16
HU = 2


def iota(shape, axis):
    return lax.broadcasted_iota(I32, shape, axis)


def contract_kernel(codex, codep, meta, sig, bq, bp, vt, dexp, out, xbuf, hbuf, obuf, ebuf, kbuf):
    nf, nh = meta[0, 33], meta[0, 34]
    low_half = iota((8, 128), 1) < 64

    def x_step(step, carry):
        for w in range(XUN):
            ch = XUN * step + w
            src = [codex[0, 8 * ch + u] for u in range(8)]
            rows = jnp.concatenate([bq[s & 255] for s in src], axis=0)
            x = jnp.dot(rows, vt[meta[0, 40 + ch]], preferred_element_type=F32)
            for u in range(8):
                tiles = [x[48 * u + 8 * j:48 * u + 8 * j + 8] for j in range(6)]
                whole = [t[:, :128] for t in tiles]
                half = [jnp.where(low_half, tiles[2 * j][:, 128:], tiles[2 * j + 1][:, 128:]) for j in range(3)]
                xbuf[src[u] >> 8] = jnp.stack(whole + half)
        return carry

    lax.fori_loop(0, (meta[0, 35] + XUN - 1) // XUN, x_step, 0)
    kbuf[...] = jnp.zeros_like(kbuf)
    ebuf[...] = jnp.zeros_like(ebuf)
    lane, sub = iota((8, 128), 1), iota((8, 128), 0)
    low_mask = (lane % 8 == sub) & (lane < 64)
    high_mask = (lane % 8 == sub) & (lane >= 64)
    row, col = iota((8, 256), 0), iota((8, 256), 1)
    even_device = (iota((64, 128), 0) * 0 + meta[0, 36]) == 0
    left_lanes = iota((64, 128), 1) < 64
    none = jnp.zeros((64, 128), BF16)
    def spread(ld, nu_a, lb, nu_b):
        a = dexp[ld, pl.ds(nu_a, 8, stride=0), :]
        b = dexp[lb, pl.ds(nu_b, 8, stride=0), :]
        return jnp.where(low_mask, a, jnp.where(high_mask, b, 0.0))

    def pair(h):
        n = h.shape[0] // 8
        both = jnp.concatenate([h[:, :128].reshape(n, 8, 128), h[:, 128:].reshape(n, 8, 128)], axis=1)
        return both.astype(BF16)

    def group(half, base, cnt):
        def h_pair(t2):
            at, ls = [], []
            for u in range(2):
                t = base + jnp.minimum(2 * t2 + u, cnt - 1)
                code = codep[0, t]
                at.append(code & 255)
                ls.append((code >> 8) & 31)
                ebuf[pl.ds(pl.multiple_of(16 * t2 + 8 * u, 8), 8), :] = (col == 8 * (code >> 13) + row).astype(F32)
            b0, b1 = [jnp.concatenate([bp[k], none[:16]], axis=0) for k in at]
            if not half:
                rhs = jnp.concatenate([jnp.concatenate([b0, none], axis=1), jnp.concatenate([none, b1], axis=1)], axis=0)
                for c in range(0, 192, HN):
                    w = jnp.concatenate([spread(ls[0], nu, ls[1], nu) for nu in range(c, c + HN)], axis=0).astype(BF16)
                    hbuf[c:c + HN, t2] = pair(jnp.dot(w, rhs, preferred_element_type=F32))
            else:
                quads = []
                for b in (b0, b1):
                    wide = b.astype(F32)
                    turned = pltpu.roll(wide, 64, 1)
                    first = jnp.where(even_device, wide, turned)
                    second = jnp.where(even_device, turned, wide)
                    quads.append((jnp.where(left_lanes, first, 0.0).astype(BF16), jnp.where(left_lanes, 0.0, second).astype(BF16)))
                (e0, o0), (e1, o1) = quads
                rhs = jnp.concatenate([jnp.concatenate([p, q], axis=1) for p, q in ((e0, none), (o0, none), (none, e1), (none, o1))], axis=0)
                for c in range(0, 96, HN):
                    w = jnp.concatenate([
                        jnp.concatenate([spread(l, 2 * r, l, 2 * r + 1) for r in range(c, c + HN)], axis=0).astype(BF16)
                        for l in ls], axis=1)
                    hbuf[c:c + HN, t2] = pair(jnp.dot(w, rhs, preferred_element_type=F32))

        def h_step(step, carry):
            for u in range(HU):
                h_pair(HU * step + u)
            return carry

        lax.fori_loop(0, (cnt + 2 * HU - 1) // (2 * HU), h_step, 0)
        depth, first = (3, 6) if half else (6, 0)

        def chunk(n, k0):
            xs = jnp.concatenate([xbuf[pl.ds(k0, CHUNK), first + j].reshape(CHUNK * 8, 128).astype(BF16) for j in range(depth)], axis=1)
            hs = jnp.concatenate([hbuf[n * depth + j].reshape(GROUP * 8, 128) for j in range(depth)], axis=1)
            o = lax.dot_general(xs, hs, NT, preferred_element_type=F32)
            obuf[pl.ds(pl.multiple_of(8 * k0, 8), CHUNK * 8), :] = o

        def n_step(i, carry):
            ends = [meta[0, NB * i + u] for u in range(NB + 1)]
            for u in range(NB):
                chunk(NB * i + u, ends[u])
            longest = ends[1] - ends[0]
            for u in range(1, NB):
                longest = jnp.maximum(longest, ends[u + 1] - ends[u])

            @pl.when(longest > CHUNK)
            def _():
                def more(n, carry):
                    s0, s1 = meta[0, n], meta[0, n + 1]

                    def c_step(c, carry):
                        chunk(n, jnp.minimum(s0 + CHUNK * c, s1 - CHUNK))
                        return carry

                    return lax.fori_loop(1, (s1 - s0 + CHUNK - 1) // CHUNK, c_step, carry)

                lax.fori_loop(NB * i, NB * i + NB, more, 0)
            return carry

        lax.fori_loop(0, 32 // NB, n_step, 0)
        r = jnp.zeros((256, 256), F32)
        for k in range(8):
            o = obuf[256 * k:256 * k + 256, :]
            high = o.astype(BF16)
            s = sig[:, 256 * k:256 * k + 256]
            r += jnp.dot(s, high, preferred_element_type=F32)
        r = jnp.where(iota((256, 256), 1) < 8 * cnt, r, 0.0)
        e = ebuf[...].astype(BF16)
        high = r.astype(BF16)
        low = (r - high.astype(F32)).astype(BF16)
        kbuf[...] += jnp.dot(high, e, preferred_element_type=F32) + jnp.dot(low, e, preferred_element_type=F32)

    for half, base, total in ((False, 0, nf), (True, nf, nh)):
        def g_step(g, carry, half=half, base=base, total=total):
            group(half, base + GROUP * g, jnp.minimum(total - GROUP * g, GROUP))
            return carry

        lax.fori_loop(0, (total + GROUP - 1) // GROUP, g_step, 0)
    out[...] = kbuf[...].T.astype(BF16)


def contract(codex, codep, meta, sig, bq, bp, vt, dexp):
    smem = pl.BlockSpec(memory_space=pltpu.SMEM)
    vmem = pl.BlockSpec(memory_space=pltpu.VMEM)
    return pl.pallas_call(
        contract_kernel,
        out_shape=jax.ShapeDtypeStruct((256, 256), BF16),
        in_specs=[smem] * 3 + [vmem] * 5,
        out_specs=vmem,
        scratch_shapes=[
            pltpu.VMEM((256 + CHUNK, 9, 8, 128), F32),
            pltpu.VMEM((192, GROUP // 2, 16, 128), BF16),
            pltpu.VMEM(((256 + CHUNK) * 8, 256), F32),
            pltpu.VMEM((256, 256), F32),
            pltpu.VMEM((256, 256), F32),
        ],
        compiler_params=pltpu.CompilerParams(vmem_limit_bytes=36 << 20),
        name="contract",
    )(codex, codep, meta, sig, bq, bp, vt, dexp)


ROWS = 288
XDIRECT = True


def place():
    m, z = lax.axis_index("map"), lax.axis_index("row")
    return m, (m // 2) % 4, m // 8, z, m % 2


def at_map(x, y, c):
    return (y * 4 + x) * 2 + c


def greet(devices, between=None):
    barrier = pltpu.get_barrier_semaphore()
    for d in devices:
        pl.semaphore_signal(barrier, inc=1, device_id=d, device_id_type=MESH)
    if between is not None:
        between()
    pl.semaphore_wait(barrier, len(devices))


def tables(nq, nn, whole_block, half_block, row_start, parity, codex, codep, meta, sig):
    g = iota((256, 1), 0)
    wide = iota((256, 256), 1)
    lane = iota((256, 128), 1)

    def column(ref, field):
        rows = []
        for t in range(32):
            c, s, u = t // 16, (t // 4) % 4, t % 4
            rows.append(ref[c, s, u, pl.ds(field, 8, stride=0), :])
        spread = jnp.concatenate(rows, axis=0)
        return jnp.sum(jnp.where(lane == g % 8, spread, 0.0), axis=1, keepdims=True).astype(I32)

    def across(col):
        return jnp.sum(jnp.where(wide == g, col.astype(F32), 0.0), axis=0, keepdims=True).astype(I32)

    def lanes(hit):
        return jnp.sum(hit.astype(F32), axis=1, keepdims=True).astype(I32)

    def rows(hit):
        return jnp.sum(hit.astype(F32), axis=0, keepdims=True).astype(I32)

    def rank(col):
        other = across(col)
        return lanes((other < col) | ((other == col) & (wide < g)))

    def put(where, at, code, rest):
        return rest + jnp.sum(jnp.where(where == at, (code - rest).astype(F32), 0.0), axis=0, keepdims=True).astype(I32)

    first, second, q = column(nq, 0), column(nq, 1), column(nq, 2) - row_start
    by_n = rank(second)
    starts = rows(second < lane)
    sig_at = iota((256, 2048), 1)
    where = jnp.sum(jnp.where(by_n == sig_at // 8, first.astype(F32), 0.0), axis=0, keepdims=True).astype(I32)
    inner = iota((1, 2048), 1) % 8
    target = jnp.where(inner < 6, 6 * where + inner, -1)
    sig[...] = (iota((256, 2048), 0) == target).astype(F32).astype(BF16)
    other = across(q)
    within = lanes((other == q) & (wide < g))
    chunks_row = (rows(q == lane) + 7) // 8
    n16, l16 = iota((16, 128), 0), iota((16, 128), 1)
    ends_col = jnp.sum(jnp.where(l16 <= n16, chunks_row.astype(F32), 0.0), axis=1, keepdims=True).astype(I32)
    lead = jnp.sum(jnp.where(lane < q, chunks_row.astype(F32), 0.0), axis=1, keepdims=True).astype(I32)
    codex[...] = put(8 * lead + within, iota((256, 512), 1), g + by_n * 256, 256 * 256)
    at128 = iota((1, 128), 1)
    chunk_q = jnp.minimum(rows((ends_col <= l16 - 40) & (n16 < 12)), 11)
    total = jnp.sum(chunks_row.astype(F32), axis=1, keepdims=True).astype(I32)
    p = column(nn, 2)
    key = jnp.where(p == whole_block, 0, jnp.where(p == half_block, 1, 2))
    piece = g // 8
    place_of = ((piece // 16) * 16 + (piece % 4) * 4 + (piece // 4) % 4) * 8 + g % 8
    codep[...] = put(rank(key), wide, place_of + column(nn, 1) * 256 + column(nn, 0) * 8192, 0)
    n0, n1 = rows(key == 0), rows(key == 1)
    meta[...] = jnp.where(at128 < 33, starts, jnp.where(at128 == 33, n0, jnp.where(at128 == 34, n1, jnp.where(at128 == 35, total, jnp.where(at128 == 36, parity, jnp.where(at128 < 40, 0, chunk_q))))))


def gather_kernel(own, triples, offsets, dens, v, wide_q, wide_p, vt_out, dexp_out, codex, codep, meta, sig, bq, bp, stage, dall, held, vbuf, spread, s_send, s_z, s_d, s_ax, s_ay, s_as, s_by, s_bx, s_bs, s_loc, nq, nn, nz, s_nz, s_nx, s_ny, s_my, s_mx, s_ns, s_plane):
    m, x, y, z, c = place()
    way = 1 - 2 * c
    o = 1 - c

    def r4(v):
        return lax.rem(v + 8, 4)

    def dev(xx, yy, zz, cc):
        return (at_map(r4(xx), r4(yy), cc), r4(zz))

    sib = dev(x, y, z, o)
    own_piece = bq.at[y, x]
    first = [
        pltpu.make_async_copy(own, bq.at[y, x], s_loc.at[0]),
        pltpu.make_async_copy(dens, dall.at[z], s_loc.at[2]),
        pltpu.make_async_copy(v, held, s_loc.at[3]),
    ]
    for d in first:
        d.start()

    def between():
        r, k = iota((384, 288), 0), iota((384, 288), 1)
        block, j, i = r // 48, (r % 48) // 8, r % 8
        source = jnp.where(i < 6, (i * 6 + j) * 8 + block, -1)
        spread[...] = (k == source).astype(F32).astype(BF16)
        row, lane = iota((8, 128), 0), iota((8, 128), 1)
        tile = jnp.zeros((8, 128), F32)
        for k in range(8):
            a, l, p = offsets[triples[0, k]] // 6, offsets[triples[1, k]] // 6, triples[2, k]
            tile = jnp.where(lane == k, jnp.where(row == 0, a, jnp.where(row == 1, l, p)).astype(F32), tile)
        nq[c, y, x] = tile
        nz[z] = tile
        for d in first[:2]:
            d.wait()

    greet([dev(x + s, y, z, c) for s in (1, 2, 3)] + [dev(x, y + s, z, c) for s in (1, 2, 3)] + [dev(x, y, z + s, c) for s in (1, 2, 3)] + [sib], between)
    sends = []

    def send(src, dst, recv, device):
        n = len(sends)
        d = pltpu.make_async_remote_copy(src_ref=src, dst_ref=dst, send_sem=s_send.at[n], recv_sem=recv, device_id=device, device_id_type=MESH)
        d.start()
        sends.append(d)

    def arrive(dst, recv):
        pltpu.make_async_remote_copy(src_ref=dst, dst_ref=dst, send_sem=s_send.at[0], recv_sem=recv, device_id=sib, device_id_type=MESH).wait_recv()

    def widen(yq, xq, yp, xp):
        two = jnp.concatenate([bq[yq, xq], bp[yp, xp]], axis=1)
        got = jnp.dot(spread[...], two, preferred_element_type=F32).astype(BF16)
        wide_q[c, yq, xq] = got[:, :128]
        wide_p[c, yp, xp] = got[:, 128:]
        send(wide_q.at[c, yq, xq], wide_q.at[c, yq, xq], s_as.at[yq, xq], sib)
        send(wide_p.at[c, yp, xp], wide_p.at[c, yp, xp], s_bs.at[yp, xp], sib)

    peers = (1, 3, 2)

    def to_plane(src, zz, n):
        return pltpu.make_async_remote_copy(src_ref=src, dst_ref=bp.at[y, x], send_sem=s_plane.at[n], recv_sem=s_by.at[y], device_id=dev(x, zz, z, c), device_id_type=MESH)

    for s in peers:
        send(own_piece, stage.at[z], s_z.at[z], dev(x, y, z + s, c))
    for s in peers if XDIRECT else (1, 3):
        send(own_piece, own_piece, s_ax.at[x], dev(x + s, y, z, c))
    for s in (1, 3):
        send(own_piece, own_piece, s_ay.at[y, x], dev(x, y + s, z, c))
    for s in peers:
        send(nz.at[z], nz.at[z], s_nz.at[z], dev(x, y, z + s, c))
        send(nq.at[c, y, x], nq.at[c, y, x], s_nx.at[x], dev(x + s, y, z, c))
    for s in peers:
        send(dall.at[z], dall.at[z], s_d.at[z], dev(x, y, z + s, c))
    @pl.when(z != y)
    def _():
        to_plane(own_piece, z, 0).start()

    keep = pltpu.make_async_copy(own_piece, stage.at[z], s_loc.at[0])
    keep.start()
    for n, s in enumerate(peers):
        zz = r4(z + s)
        arrive(stage.at[zz], s_z.at[zz])

        @pl.when(zz != y)
        def _(zz=zz, n=n):
            to_plane(stage.at[zz], zz, n + 1).start()

    keep.wait()
    for s in peers:
        arrive(nz.at[r4(z + s)], s_nz.at[r4(z + s)])
    nn[c, x, y] = nz[y]
    for s in peers:
        yt = r4(y + s)
        send(nz.at[yt], nn.at[c, x, y], s_my.at[y], dev(x, yt, z, c))
    mine = pltpu.make_async_copy(stage.at[y], bp.at[y, x], s_loc.at[1])
    mine.start()
    for s in (1, 3):
        send(stage.at[y], bp.at[y, x], s_bx.at[y, x], dev(x + s, y, z, c))

    xf, xb, x2 = r4(x - way), r4(x + way), r4(x + 2)
    yf, yb, y2 = r4(y - way), r4(y + way), r4(y + 2)
    for xx in (xf, xb, x2):
        arrive(bq.at[y, xx], s_ax.at[xx])
        if not XDIRECT and xx is xf:
            send(bq.at[y, xx], bq.at[y, xx], s_ax.at[xx], dev(x + way, y, z, c))
        for s in (1, 3):
            send(bq.at[y, xx], bq.at[y, xx], s_ay.at[y, xx], dev(x, y + s, z, c))
    for xx in (xf, xb, x2):
        arrive(nq.at[c, y, xx], s_nx.at[xx])
    for s in peers:
        send(nq.at[c, y], nq.at[c, y], s_ny.at[y], dev(x, y + s, z, c))
    for yy in (yf, yb, y2):
        arrive(bp.at[yy, x], s_by.at[yy])
        for s in (1, 3):
            send(bp.at[yy, x], bp.at[yy, x], s_bx.at[yy, x], dev(x + s, y, z, c))
    for yy in (yf, yb, y2):
        arrive(nn.at[c, x, yy], s_my.at[yy])
    for s in peers:
        send(nn.at[c, x], nn.at[c, x], s_mx.at[x], dev(x + s, y, z, c))
    mine.wait()
    widen(y, x, y, x)
    for xx, yy in ((x, y), (xf, yf), (xb, yb), (x2, y2)):
        arrive(bq.at[yf, xx], s_ay.at[yf, xx])
        send(bq.at[yf, xx], bq.at[yf, xx], s_ay.at[yf, xx], dev(x, y + way, z, c))
        arrive(bp.at[yy, xf], s_bx.at[yy, xf])
        send(bp.at[yy, xf], bp.at[yy, xf], s_bx.at[yy, xf], dev(x + way, y, z, c))
        if xx is not x:
            widen(y, xx, yy, x)
        widen(yf, xx, yy, xf)
    for s in peers:
        arrive(nq.at[c, r4(y + s)], s_ny.at[r4(y + s)])
        arrive(nn.at[c, r4(x + s)], s_mx.at[r4(x + s)])
    send(nq.at[c], nq.at[c], s_ns.at[0], sib)
    send(nn.at[c], nn.at[c], s_ns.at[1], sib)
    first[2].wait()
    parity = lax.rem(m, 2)
    vbuf[0:128] = held[pl.ds(pl.multiple_of(64 * parity, 64), 128), :]
    half = held[pl.ds(pl.multiple_of(128 * (1 - parity), 64), 64), :]
    vbuf[128:192] = half
    vbuf[192:256] = half
    same = (iota((128, 128), 0) == iota((128, 128), 1)).astype(F32).astype(BF16)
    for q in range(12):
        vt_out[q] = lax.dot_general(same, vbuf[:, 128 * q:128 * q + 128], NT, preferred_element_type=F32).astype(BF16)
    for s in peers:
        arrive(dall.at[r4(z + s)], s_d.at[r4(z + s)])
    same = (iota((192, 192), 0) == iota((192, 192), 1)).astype(F32).astype(BF16)
    full = jnp.concatenate([dall[k] for k in range(4)], axis=0)
    turned = lax.dot_general(same, full, NT, preferred_element_type=F32).astype(BF16)
    lam, lane = iota((192, 128), 0), iota((192, 128), 1)
    part = (lane % 64) // 8
    for l in range(32):
        sel = ((lam == 6 * l + part) & (part < 6)).astype(F32).astype(BF16)
        dexp_out[l] = jnp.dot(turned, sel, preferred_element_type=F32)
    arrive(nq.at[o], s_ns.at[0])
    arrive(nn.at[o], s_ns.at[1])
    chip = m // 2
    tables(nq, nn, 3 * chip + 2 * parity, 3 * chip + 1, z * 12, parity, codex, codep, meta, sig)
    for ya, xa in ((yb, xb), (y2, x2)):
        for xx, yy in ((x, y), (xf, yf), (xb, yb), (x2, y2)):
            arrive(bq.at[ya, xx], s_ay.at[ya, xx])
            arrive(bp.at[yy, xa], s_bx.at[yy, xa])
            widen(ya, xx, yy, xa)
    for yy in (y, yf, yb, y2):
        for xx in (x, xf, xb, x2):
            arrive(wide_q.at[o, yy, xx], s_as.at[yy, xx])
            arrive(wide_p.at[o, yy, xx], s_bs.at[yy, xx])
    for n, s in enumerate((0,) + peers):
        zz = r4(z + s)

        @pl.when(zz != y)
        def _(zz=zz, n=n):
            to_plane(own_piece if n == 0 else stage.at[zz], zz, n).wait_send()

    for d in sends:
        d.wait_send()


def gather(own, triples, offsets, dens, v):
    hbm = pl.BlockSpec(memory_space=pltpu.HBM)
    smem = pl.BlockSpec(memory_space=pltpu.SMEM)
    vmem = pl.BlockSpec(memory_space=pltpu.VMEM)
    dma = pltpu.SemaphoreType.DMA
    return pl.pallas_call(
        gather_kernel,
        out_shape=[
            jax.ShapeDtypeStruct((2, 4, 4, 384, 128), BF16),
            jax.ShapeDtypeStruct((2, 4, 4, 384, 128), BF16),
            jax.ShapeDtypeStruct((12, 128, 256), BF16),
            jax.ShapeDtypeStruct((32, 192, 128), F32),
            jax.ShapeDtypeStruct((1, 512), I32),
            jax.ShapeDtypeStruct((1, 256), I32),
            jax.ShapeDtypeStruct((1, 128), I32),
            jax.ShapeDtypeStruct((256, 2048), BF16),
        ],
        in_specs=[hbm, smem, smem, hbm, hbm],
        out_specs=[vmem] * 8,
        scratch_shapes=[
            pltpu.VMEM((4, 4, ROWS, 128), BF16),
            pltpu.VMEM((4, 4, ROWS, 128), BF16),
            pltpu.VMEM((4, ROWS, 128), BF16),
            pltpu.VMEM((4, 48, 192), BF16),
            pltpu.VMEM((192, 1536), BF16),
            pltpu.VMEM((256, 1536), BF16),
            pltpu.VMEM((384, 288), BF16),
            dma((104,)), dma((4,)), dma((4,)), dma((4,)), dma((4, 4)), dma((4, 4)), dma((4,)), dma((4, 4)), dma((4, 4)), dma((4,)),
            pltpu.VMEM((2, 4, 4, 8, 128), F32),
            pltpu.VMEM((2, 4, 4, 8, 128), F32),
            pltpu.VMEM((4, 8, 128), F32),
            dma((4,)), dma((4,)), dma((4,)), dma((4,)), dma((4,)), dma((2,)), dma((4,)),
        ],
        compiler_params=pltpu.CompilerParams(collective_id=0, has_side_effects=True, vmem_limit_bytes=24 << 20),
        name="gather",
    )(own, triples, offsets, dens, v)


def reduce_kernel(part, out, got, cut, got2, send1, recv1, send2, recv2):
    m, x, y, z, c = place()
    g = lax.rem(m, 8)
    near = [(y * 8 + lax.rem(g + d, 8), z) for d in range(1, 8)]
    far = []
    for d in range(1, 16):
        h = lax.rem(y * 4 + z + d, 16)
        far.append((h // 4, lax.rem(h, 4)))
    greet(near + [((yy * 8 + g), zz) for yy, zz in far])
    first = []
    for d in range(1, 8):
        gg = lax.rem(g + d, 8)
        cp = pltpu.make_async_remote_copy(src_ref=part.at[:, gg], dst_ref=got.at[g], send_sem=send1.at[d], recv_sem=recv1.at[g], device_id=near[d - 1], device_id_type=MESH)
        cp.start()
        first.append(cp)
    got[g] = part[:, g]
    cut[...] = jnp.zeros_like(cut)
    for d in range(1, 8):
        gg = lax.rem(g + d, 8)
        pltpu.make_async_remote_copy(src_ref=part.at[:, gg], dst_ref=got.at[gg], send_sem=send1.at[d], recv_sem=recv1.at[gg], device_id=near[0], device_id_type=MESH).wait_recv()
    total = got[0].astype(F32)
    for k in range(1, 8):
        total = total + got[k].astype(F32)
    for zz in range(4):
        cut[:, zz, :, 0:48] = total[:, :, 48 * zz:48 * zz + 48]
    second = []
    for d, (yy, zz) in enumerate(far):
        cp = pltpu.make_async_remote_copy(src_ref=cut.at[yy, zz], dst_ref=got2.at[y, z], send_sem=send2.at[d], recv_sem=recv2.at[y, z], device_id=(yy * 8 + g, zz), device_id_type=MESH)
        cp.start()
        second.append(cp)
    got2[y, z] = cut[y, z]
    for yy, zz in far:
        pltpu.make_async_remote_copy(src_ref=cut.at[yy, zz], dst_ref=got2.at[yy, zz], send_sem=send2.at[0], recv_sem=recv2.at[yy, zz], device_id=(yy * 8 + g, zz), device_id_type=MESH).wait_recv()
    for part_of in range(2):
        result = got2[2 * part_of, 0]
        for k in range(1, 8):
            result = result + got2[2 * part_of + k // 4, k % 4]
        out[part_of] = result
    for cp in first + second:
        cp.wait_send()


def reduce(part):
    vmem = pl.BlockSpec(memory_space=pltpu.VMEM)
    dma = pltpu.SemaphoreType.DMA
    return pl.pallas_call(
        reduce_kernel,
        out_shape=jax.ShapeDtypeStruct((2, 8, 128), F32),
        in_specs=[vmem],
        out_specs=vmem,
        scratch_shapes=[
            pltpu.VMEM((8, 4, 8, 256), BF16),
            pltpu.VMEM((4, 4, 8, 128), F32),
            pltpu.VMEM((4, 4, 8, 128), F32),
            dma((8,)), dma((8,)), dma((16,)), dma((4, 4)),
        ],
        compiler_params=pltpu.CompilerParams(collective_id=1, has_side_effects=True, vmem_limit_bytes=8 << 20),
        name="reduce",
    )(part)


def body(block_list, block_values, atom_offsets, density, metric_inverse):
    own = block_values.transpose(1, 2, 0, 3).reshape(288, 128)
    bq, bp, vt, dexp, codex, codep, meta, sig = gather(*[pltpu.with_memory_space_constraint(t, pltpu.HBM) for t in (own, block_list.T, atom_offsets, density, metric_inverse)])
    part = contract(codex, codep, meta, sig, bq.reshape(256, 48, 128), bp.reshape(256, 48, 128), vt, dexp)
    sums = reduce(part.reshape(4, 8, 8, 256))
    return sums[0, :6, :48] + sums[1, :6, :48]


def solution(mesh):
    placed = (
        P(("map", "row"), None),
        P(("map", "row"), None, None, None),
        P(),
        P("row", None),
        P("map", "row"),
    )
    return jax.shard_map(
        body, mesh=mesh, in_specs=placed, out_specs=P("map", "row"), check_vma=False
    )
```

```python
import jax
import jax.numpy as jnp
from jax import lax
from jax.experimental import pallas as pl
from jax.experimental.pallas import tpu as pltpu
from jax.sharding import PartitionSpec as P

HI = lax.Precision.HIGHEST
F32, BF16, I32 = jnp.float32, jnp.bfloat16, jnp.int32
NT = (((1,), (1,)), ((), ()))
MESH = pl.DeviceIdType.MESH
GROUP = 32
CHUNK = 16
XROWS = 44
XUN = 11
HN = 48
NB = 32
HU = 2


def iota(shape, axis):
    return lax.broadcasted_iota(I32, shape, axis)


def contract_kernel(codex, codep, meta, sig, bq, bp, vt, dexp, out, xbuf, hbuf, obuf, ebuf, kbuf):
    nf, nh = meta[0, 33], meta[0, 34]
    low_half = iota((8, 128), 1) < 64

    def x_step(step, carry):
        for w in range(XUN):
            ch = XUN * step + w
            src = [codex[0, 8 * ch + u] for u in range(8)]
            rows = jnp.concatenate([bq[s & 255] for s in src], axis=0)
            x = jnp.dot(rows, vt[meta[0, 40 + ch]], preferred_element_type=F32)
            for u in range(8):
                tiles = [x[48 * u + 8 * j:48 * u + 8 * j + 8] for j in range(6)]
                whole = [t[:, :128] for t in tiles]
                half = [jnp.where(low_half, tiles[2 * j][:, 128:], tiles[2 * j + 1][:, 128:]) for j in range(3)]
                xbuf[src[u] >> 8] = jnp.stack(whole + half)
        return carry

    lax.fori_loop(0, (meta[0, 35] + XUN - 1) // XUN, x_step, 0)
    kbuf[...] = jnp.zeros_like(kbuf)
    ebuf[...] = jnp.zeros_like(ebuf)
    lane, sub = iota((8, 128), 1), iota((8, 128), 0)
    low_mask = (lane % 8 == sub) & (lane < 64)
    high_mask = (lane % 8 == sub) & (lane >= 64)
    row, col = iota((8, 256), 0), iota((8, 256), 1)
    even_device = (iota((64, 128), 0) * 0 + meta[0, 36]) == 0
    left_lanes = iota((64, 128), 1) < 64
    none = jnp.zeros((64, 128), BF16)
    def spread(ld, nu_a, lb, nu_b):
        a = dexp[ld, pl.ds(nu_a, 8, stride=0), :]
        b = dexp[lb, pl.ds(nu_b, 8, stride=0), :]
        return jnp.where(low_mask, a, jnp.where(high_mask, b, 0.0))

    def pair(h):
        n = h.shape[0] // 8
        both = jnp.concatenate([h[:, :128].reshape(n, 8, 128), h[:, 128:].reshape(n, 8, 128)], axis=1)
        return both.astype(BF16)

    def group(half, base, cnt):
        def h_pair(t2):
            at, ls = [], []
            for u in range(2):
                t = base + jnp.minimum(2 * t2 + u, cnt - 1)
                code = codep[0, t]
                at.append(code & 255)
                ls.append((code >> 8) & 31)
                ebuf[pl.ds(pl.multiple_of(16 * t2 + 8 * u, 8), 8), :] = (col == 8 * (code >> 13) + row).astype(F32)
            b0, b1 = [jnp.concatenate([bp[k], none[:16]], axis=0) for k in at]
            if not half:
                rhs = jnp.concatenate([jnp.concatenate([b0, none], axis=1), jnp.concatenate([none, b1], axis=1)], axis=0)
                for c in range(0, 192, HN):
                    w = jnp.concatenate([spread(ls[0], nu, ls[1], nu) for nu in range(c, c + HN)], axis=0).astype(BF16)
                    hbuf[c:c + HN, t2] = pair(jnp.dot(w, rhs, preferred_element_type=F32))
            else:
                quads = []
                for b in (b0, b1):
                    wide = b.astype(F32)
                    turned = pltpu.roll(wide, 64, 1)
                    first = jnp.where(even_device, wide, turned)
                    second = jnp.where(even_device, turned, wide)
                    quads.append((jnp.where(left_lanes, first, 0.0).astype(BF16), jnp.where(left_lanes, 0.0, second).astype(BF16)))
                (e0, o0), (e1, o1) = quads
                rhs = jnp.concatenate([jnp.concatenate([p, q], axis=1) for p, q in ((e0, none), (o0, none), (none, e1), (none, o1))], axis=0)
                for c in range(0, 96, HN):
                    w = jnp.concatenate([
                        jnp.concatenate([spread(l, 2 * r, l, 2 * r + 1) for r in range(c, c + HN)], axis=0).astype(BF16)
                        for l in ls], axis=1)
                    hbuf[c:c + HN, t2] = pair(jnp.dot(w, rhs, preferred_element_type=F32))

        def h_step(step, carry):
            for u in range(HU):
                h_pair(HU * step + u)
            return carry

        lax.fori_loop(0, (cnt + 2 * HU - 1) // (2 * HU), h_step, 0)
        depth, first = (3, 6) if half else (6, 0)

        def chunk(n, k0):
            xs = jnp.concatenate([xbuf[pl.ds(k0, CHUNK), first + j].reshape(CHUNK * 8, 128).astype(BF16) for j in range(depth)], axis=1)
            hs = jnp.concatenate([hbuf[n * depth + j].reshape(GROUP * 8, 128) for j in range(depth)], axis=1)
            o = lax.dot_general(xs, hs, NT, preferred_element_type=F32)
            obuf[pl.ds(pl.multiple_of(8 * k0, 8), CHUNK * 8), :] = o

        def n_step(i, carry):
            ends = [meta[0, NB * i + u] for u in range(NB + 1)]
            for u in range(NB):
                chunk(NB * i + u, ends[u])
            longest = ends[1] - ends[0]
            for u in range(1, NB):
                longest = jnp.maximum(longest, ends[u + 1] - ends[u])

            @pl.when(longest > CHUNK)
            def _():
                def more(n, carry):
                    s0, s1 = meta[0, n], meta[0, n + 1]

                    def c_step(c, carry):
                        chunk(n, jnp.minimum(s0 + CHUNK * c, s1 - CHUNK))
                        return carry

                    return lax.fori_loop(1, (s1 - s0 + CHUNK - 1) // CHUNK, c_step, carry)

                lax.fori_loop(NB * i, NB * i + NB, more, 0)
            return carry

        lax.fori_loop(0, 32 // NB, n_step, 0)
        r = jnp.zeros((256, 256), F32)
        for k in range(8):
            o = obuf[256 * k:256 * k + 256, :]
            high = o.astype(BF16)
            s = sig[:, 256 * k:256 * k + 256]
            r += jnp.dot(s, high, preferred_element_type=F32)
        r = jnp.where(iota((256, 256), 1) < 8 * cnt, r, 0.0)
        e = ebuf[...].astype(BF16)
        high = r.astype(BF16)
        low = (r - high.astype(F32)).astype(BF16)
        kbuf[...] += jnp.dot(high, e, preferred_element_type=F32) + jnp.dot(low, e, preferred_element_type=F32)

    for half, base, total in ((False, 0, nf), (True, nf, nh)):
        def g_step(g, carry, half=half, base=base, total=total):
            group(half, base + GROUP * g, jnp.minimum(total - GROUP * g, GROUP))
            return carry

        lax.fori_loop(0, (total + GROUP - 1) // GROUP, g_step, 0)
    out[...] = kbuf[...].T.astype(BF16)


def contract(codex, codep, meta, sig, bq, bp, vt, dexp):
    smem = pl.BlockSpec(memory_space=pltpu.SMEM)
    vmem = pl.BlockSpec(memory_space=pltpu.VMEM)
    return pl.pallas_call(
        contract_kernel,
        out_shape=jax.ShapeDtypeStruct((256, 256), BF16),
        in_specs=[smem] * 3 + [vmem] * 5,
        out_specs=vmem,
        scratch_shapes=[
            pltpu.VMEM((256 + CHUNK, 9, 8, 128), F32),
            pltpu.VMEM((192, GROUP // 2, 16, 128), BF16),
            pltpu.VMEM(((256 + CHUNK) * 8, 256), F32),
            pltpu.VMEM((256, 256), F32),
            pltpu.VMEM((256, 256), F32),
        ],
        compiler_params=pltpu.CompilerParams(vmem_limit_bytes=36 << 20),
        name="contract",
    )(codex, codep, meta, sig, bq, bp, vt, dexp)


ROWS = 288
XDIRECT = True


def place():
    m, z = lax.axis_index("map"), lax.axis_index("row")
    return m, (m // 2) % 4, m // 8, z, m % 2


def at_map(x, y, c):
    return (y * 4 + x) * 2 + c


def greet(devices, between=None):
    barrier = pltpu.get_barrier_semaphore()
    for d in devices:
        pl.semaphore_signal(barrier, inc=1, device_id=d, device_id_type=MESH)
    if between is not None:
        between()
    pl.semaphore_wait(barrier, len(devices))


def tables(nq, nn, whole_block, half_block, row_start, parity, codex, codep, meta, sig):
    g = iota((256, 1), 0)
    wide = iota((256, 256), 1)
    lane = iota((256, 128), 1)

    def column(ref, field):
        rows = []
        for t in range(32):
            c, s, u = t // 16, (t // 4) % 4, t % 4
            rows.append(ref[c, s, u, pl.ds(field, 8, stride=0), :])
        spread = jnp.concatenate(rows, axis=0)
        return jnp.sum(jnp.where(lane == g % 8, spread, 0.0), axis=1, keepdims=True).astype(I32)

    def across(col):
        return jnp.sum(jnp.where(wide == g, col.astype(F32), 0.0), axis=0, keepdims=True).astype(I32)

    def lanes(hit):
        return jnp.sum(hit.astype(F32), axis=1, keepdims=True).astype(I32)

    def rows(hit):
        return jnp.sum(hit.astype(F32), axis=0, keepdims=True).astype(I32)

    def rank(col):
        other = across(col)
        return lanes((other < col) | ((other == col) & (wide < g)))

    def put(where, at, code, rest):
        return rest + jnp.sum(jnp.where(where == at, (code - rest).astype(F32), 0.0), axis=0, keepdims=True).astype(I32)

    first, second, q = column(nq, 0), column(nq, 1), column(nq, 2) - row_start
    by_n = rank(second)
    starts = rows(second < lane)
    sig_at = iota((256, 2048), 1)
    where = jnp.sum(jnp.where(by_n == sig_at // 8, first.astype(F32), 0.0), axis=0, keepdims=True).astype(I32)
    inner = iota((1, 2048), 1) % 8
    target = jnp.where(inner < 6, 6 * where + inner, -1)
    sig[...] = (iota((256, 2048), 0) == target).astype(F32).astype(BF16)
    other = across(q)
    within = lanes((other == q) & (wide < g))
    chunks_row = (rows(q == lane) + 7) // 8
    n16, l16 = iota((16, 128), 0), iota((16, 128), 1)
    ends_col = jnp.sum(jnp.where(l16 <= n16, chunks_row.astype(F32), 0.0), axis=1, keepdims=True).astype(I32)
    lead = jnp.sum(jnp.where(lane < q, chunks_row.astype(F32), 0.0), axis=1, keepdims=True).astype(I32)
    codex[...] = put(8 * lead + within, iota((256, 512), 1), g + by_n * 256, 256 * 256)
    at128 = iota((1, 128), 1)
    chunk_q = jnp.minimum(rows((ends_col <= l16 - 40) & (n16 < 12)), 11)
    total = jnp.sum(chunks_row.astype(F32), axis=1, keepdims=True).astype(I32)
    p = column(nn, 2)
    key = jnp.where(p == whole_block, 0, jnp.where(p == half_block, 1, 2))
    piece = g // 8
    place_of = ((piece // 16) * 16 + (piece % 4) * 4 + (piece // 4) % 4) * 8 + g % 8
    codep[...] = put(rank(key), wide, place_of + column(nn, 1) * 256 + column(nn, 0) * 8192, 0)
    n0, n1 = rows(key == 0), rows(key == 1)
    meta[...] = jnp.where(at128 < 33, starts, jnp.where(at128 == 33, n0, jnp.where(at128 == 34, n1, jnp.where(at128 == 35, total, jnp.where(at128 == 36, parity, jnp.where(at128 < 40, 0, chunk_q))))))


def gather_kernel(own, triples, offsets, dens, v, wide_q, wide_p, vt_out, dexp_out, codex, codep, meta, sig, bq, bp, stage, dall, held, vbuf, spread, s_send, s_z, s_d, s_ax, s_ay, s_as, s_by, s_bx, s_bs, s_loc, nq, nn, nz, s_nz, s_nx, s_ny, s_my, s_mx, s_ns, s_plane):
    m, x, y, z, c = place()
    way = 1 - 2 * c
    o = 1 - c

    def r4(v):
        return lax.rem(v + 8, 4)

    def dev(xx, yy, zz, cc):
        return (at_map(r4(xx), r4(yy), cc), r4(zz))

    sib = dev(x, y, z, o)
    own_piece = bq.at[y, x]
    first = [
        pltpu.make_async_copy(own, bq.at[y, x], s_loc.at[0]),
        pltpu.make_async_copy(dens, dall.at[z], s_loc.at[2]),
        pltpu.make_async_copy(v, held, s_loc.at[3]),
    ]
    for d in first:
        d.start()

    def between():
        r, k = iota((384, 288), 0), iota((384, 288), 1)
        block, j, i = r // 48, (r % 48) // 8, r % 8
        source = jnp.where(i < 6, (i * 6 + j) * 8 + block, -1)
        spread[...] = (k == source).astype(F32).astype(BF16)
        row, lane = iota((8, 128), 0), iota((8, 128), 1)
        tile = jnp.zeros((8, 128), F32)
        for k in range(8):
            a, l, p = offsets[triples[0, k]] // 6, offsets[triples[1, k]] // 6, triples[2, k]
            tile = jnp.where(lane == k, jnp.where(row == 0, a, jnp.where(row == 1, l, p)).astype(F32), tile)
        nq[c, y, x] = tile
        nz[z] = tile
        for d in first[:2]:
            d.wait()

    greet([dev(x + s, y, z, c) for s in (1, 2, 3)] + [dev(x, y + s, z, c) for s in (1, 2, 3)] + [dev(x, y, z + s, c) for s in (1, 2, 3)] + [sib], between)
    sends = []

    def send(src, dst, recv, device):
        n = len(sends)
        d = pltpu.make_async_remote_copy(src_ref=src, dst_ref=dst, send_sem=s_send.at[n], recv_sem=recv, device_id=device, device_id_type=MESH)
        d.start()
        sends.append(d)

    def arrive(dst, recv):
        pltpu.make_async_remote_copy(src_ref=dst, dst_ref=dst, send_sem=s_send.at[0], recv_sem=recv, device_id=sib, device_id_type=MESH).wait_recv()

    def widen(yq, xq, yp, xp):
        two = jnp.concatenate([bq[yq, xq], bp[yp, xp]], axis=1)
        got = jnp.dot(spread[...], two, preferred_element_type=F32).astype(BF16)
        wide_q[c, yq, xq] = got[:, :128]
        wide_p[c, yp, xp] = got[:, 128:]
        send(wide_q.at[c, yq, xq], wide_q.at[c, yq, xq], s_as.at[yq, xq], sib)
        send(wide_p.at[c, yp, xp], wide_p.at[c, yp, xp], s_bs.at[yp, xp], sib)

    peers = (1, 3, 2)

    def to_plane(src, zz, n):
        return pltpu.make_async_remote_copy(src_ref=src, dst_ref=bp.at[y, x], send_sem=s_plane.at[n], recv_sem=s_by.at[y], device_id=dev(x, zz, z, c), device_id_type=MESH)

    for s in peers:
        send(own_piece, stage.at[z], s_z.at[z], dev(x, y, z + s, c))
    for s in peers if XDIRECT else (1, 3):
        send(own_piece, own_piece, s_ax.at[x], dev(x + s, y, z, c))
    for s in (1, 3):
        send(own_piece, own_piece, s_ay.at[y, x], dev(x, y + s, z, c))
    for s in peers:
        send(nz.at[z], nz.at[z], s_nz.at[z], dev(x, y, z + s, c))
        send(nq.at[c, y, x], nq.at[c, y, x], s_nx.at[x], dev(x + s, y, z, c))
    for s in peers:
        send(dall.at[z], dall.at[z], s_d.at[z], dev(x, y, z + s, c))
    @pl.when(z != y)
    def _():
        to_plane(own_piece, z, 0).start()

    keep = pltpu.make_async_copy(own_piece, stage.at[z], s_loc.at[0])
    keep.start()
    for n, s in enumerate(peers):
        zz = r4(z + s)
        arrive(stage.at[zz], s_z.at[zz])

        @pl.when(zz != y)
        def _(zz=zz, n=n):
            to_plane(stage.at[zz], zz, n + 1).start()

    keep.wait()
    for s in peers:
        arrive(nz.at[r4(z + s)], s_nz.at[r4(z + s)])
    nn[c, x, y] = nz[y]
    for s in peers:
        yt = r4(y + s)
        send(nz.at[yt], nn.at[c, x, y], s_my.at[y], dev(x, yt, z, c))
    mine = pltpu.make_async_copy(stage.at[y], bp.at[y, x], s_loc.at[1])
    mine.start()
    for s in (1, 3):
        send(stage.at[y], bp.at[y, x], s_bx.at[y, x], dev(x + s, y, z, c))

    xf, xb, x2 = r4(x - way), r4(x + way), r4(x + 2)
    yf, yb, y2 = r4(y - way), r4(y + way), r4(y + 2)
    for xx in (xf, xb, x2):
        arrive(bq.at[y, xx], s_ax.at[xx])
        if not XDIRECT and xx is xf:
            send(bq.at[y, xx], bq.at[y, xx], s_ax.at[xx], dev(x + way, y, z, c))
        for s in (1, 3):
            send(bq.at[y, xx], bq.at[y, xx], s_ay.at[y, xx], dev(x, y + s, z, c))
    for xx in (xf, xb, x2):
        arrive(nq.at[c, y, xx], s_nx.at[xx])
    for s in peers:
        send(nq.at[c, y], nq.at[c, y], s_ny.at[y], dev(x, y + s, z, c))
    for yy in (yf, yb, y2):
        arrive(bp.at[yy, x], s_by.at[yy])
        for s in (1, 3):
            send(bp.at[yy, x], bp.at[yy, x], s_bx.at[yy, x], dev(x + s, y, z, c))
    for yy in (yf, yb, y2):
        arrive(nn.at[c, x, yy], s_my.at[yy])
    for s in peers:
        send(nn.at[c, x], nn.at[c, x], s_mx.at[x], dev(x + s, y, z, c))
    mine.wait()
    widen(y, x, y, x)
    for xx, yy in ((x, y), (xf, yf), (xb, yb), (x2, y2)):
        arrive(bq.at[yf, xx], s_ay.at[yf, xx])
        send(bq.at[yf, xx], bq.at[yf, xx], s_ay.at[yf, xx], dev(x, y + way, z, c))
        arrive(bp.at[yy, xf], s_bx.at[yy, xf])
        send(bp.at[yy, xf], bp.at[yy, xf], s_bx.at[yy, xf], dev(x + way, y, z, c))
        if xx is not x:
            widen(y, xx, yy, x)
        widen(yf, xx, yy, xf)
    for s in peers:
        arrive(nq.at[c, r4(y + s)], s_ny.at[r4(y + s)])
        arrive(nn.at[c, r4(x + s)], s_mx.at[r4(x + s)])
    send(nq.at[c], nq.at[c], s_ns.at[0], sib)
    send(nn.at[c], nn.at[c], s_ns.at[1], sib)
    first[2].wait()
    parity = lax.rem(m, 2)
    vbuf[0:128] = held[pl.ds(pl.multiple_of(64 * parity, 64), 128), :]
    half = held[pl.ds(pl.multiple_of(128 * (1 - parity), 64), 64), :]
    vbuf[128:192] = half
    vbuf[192:256] = half
    same = (iota((128, 128), 0) == iota((128, 128), 1)).astype(F32).astype(BF16)
    for q in range(12):
        vt_out[q] = lax.dot_general(same, vbuf[:, 128 * q:128 * q + 128], NT, preferred_element_type=F32).astype(BF16)
    for s in peers:
        arrive(dall.at[r4(z + s)], s_d.at[r4(z + s)])
    same = (iota((192, 192), 0) == iota((192, 192), 1)).astype(F32).astype(BF16)
    full = jnp.concatenate([dall[k] for k in range(4)], axis=0)
    turned = lax.dot_general(same, full, NT, preferred_element_type=F32).astype(BF16)
    lam, lane = iota((192, 128), 0), iota((192, 128), 1)
    part = (lane % 64) // 8
    for l in range(32):
        sel = ((lam == 6 * l + part) & (part < 6)).astype(F32).astype(BF16)
        dexp_out[l] = jnp.dot(turned, sel, preferred_element_type=F32)
    arrive(nq.at[o], s_ns.at[0])
    arrive(nn.at[o], s_ns.at[1])
    chip = m // 2
    tables(nq, nn, 3 * chip + 2 * parity, 3 * chip + 1, z * 12, parity, codex, codep, meta, sig)
    for ya, xa in ((yb, xb), (y2, x2)):
        for xx, yy in ((x, y), (xf, yf), (xb, yb), (x2, y2)):
            arrive(bq.at[ya, xx], s_ay.at[ya, xx])
            arrive(bp.at[yy, xa], s_bx.at[yy, xa])
            widen(ya, xx, yy, xa)
    for yy in (y, yf, yb, y2):
        for xx in (x, xf, xb, x2):
            arrive(wide_q.at[o, yy, xx], s_as.at[yy, xx])
            arrive(wide_p.at[o, yy, xx], s_bs.at[yy, xx])
    for n, s in enumerate((0,) + peers):
        zz = r4(z + s)

        @pl.when(zz != y)
        def _(zz=zz, n=n):
            to_plane(own_piece if n == 0 else stage.at[zz], zz, n).wait_send()

    for d in sends:
        d.wait_send()


def gather(own, triples, offsets, dens, v):
    hbm = pl.BlockSpec(memory_space=pltpu.HBM)
    smem = pl.BlockSpec(memory_space=pltpu.SMEM)
    vmem = pl.BlockSpec(memory_space=pltpu.VMEM)
    dma = pltpu.SemaphoreType.DMA
    return pl.pallas_call(
        gather_kernel,
        out_shape=[
            jax.ShapeDtypeStruct((2, 4, 4, 384, 128), BF16),
            jax.ShapeDtypeStruct((2, 4, 4, 384, 128), BF16),
            jax.ShapeDtypeStruct((12, 128, 256), BF16),
            jax.ShapeDtypeStruct((32, 192, 128), F32),
            jax.ShapeDtypeStruct((1, 512), I32),
            jax.ShapeDtypeStruct((1, 256), I32),
            jax.ShapeDtypeStruct((1, 128), I32),
            jax.ShapeDtypeStruct((256, 2048), BF16),
        ],
        in_specs=[hbm, smem, smem, hbm, hbm],
        out_specs=[vmem] * 8,
        scratch_shapes=[
            pltpu.VMEM((4, 4, ROWS, 128), BF16),
            pltpu.VMEM((4, 4, ROWS, 128), BF16),
            pltpu.VMEM((4, ROWS, 128), BF16),
            pltpu.VMEM((4, 48, 192), BF16),
            pltpu.VMEM((192, 1536), BF16),
            pltpu.VMEM((256, 1536), BF16),
            pltpu.VMEM((384, 288), BF16),
            dma((104,)), dma((4,)), dma((4,)), dma((4,)), dma((4, 4)), dma((4, 4)), dma((4,)), dma((4, 4)), dma((4, 4)), dma((4,)),
            pltpu.VMEM((2, 4, 4, 8, 128), F32),
            pltpu.VMEM((2, 4, 4, 8, 128), F32),
            pltpu.VMEM((4, 8, 128), F32),
            dma((4,)), dma((4,)), dma((4,)), dma((4,)), dma((4,)), dma((2,)), dma((4,)),
        ],
        compiler_params=pltpu.CompilerParams(collective_id=0, has_side_effects=True, vmem_limit_bytes=24 << 20),
        name="gather",
    )(own, triples, offsets, dens, v)


def reduce_kernel(part, out, got, cut, got2, send1, recv1, send2, recv2):
    m, x, y, z, c = place()
    g = lax.rem(m, 8)
    near = [(y * 8 + lax.rem(g + d, 8), z) for d in range(1, 8)]
    far = []
    for d in range(1, 16):
        h = lax.rem(y * 4 + z + d, 16)
        far.append((h // 4, lax.rem(h, 4)))
    greet(near + [((yy * 8 + g), zz) for yy, zz in far])
    first = []
    for d in range(1, 8):
        gg = lax.rem(g + d, 8)
        cp = pltpu.make_async_remote_copy(src_ref=part.at[:, gg], dst_ref=got.at[g], send_sem=send1.at[d], recv_sem=recv1.at[g], device_id=near[d - 1], device_id_type=MESH)
        cp.start()
        first.append(cp)
    got[g] = part[:, g]
    cut[...] = jnp.zeros_like(cut)
    for d in range(1, 8):
        gg = lax.rem(g + d, 8)
        pltpu.make_async_remote_copy(src_ref=part.at[:, gg], dst_ref=got.at[gg], send_sem=send1.at[d], recv_sem=recv1.at[gg], device_id=near[0], device_id_type=MESH).wait_recv()
    total = got[0].astype(F32)
    for k in range(1, 8):
        total = total + got[k].astype(F32)
    for zz in range(4):
        cut[:, zz, :, 0:48] = total[:, :, 48 * zz:48 * zz + 48]
    second = []
    for d, (yy, zz) in enumerate(far):
        cp = pltpu.make_async_remote_copy(src_ref=cut.at[yy, zz], dst_ref=got2.at[y, z], send_sem=send2.at[d], recv_sem=recv2.at[y, z], device_id=(yy * 8 + g, zz), device_id_type=MESH)
        cp.start()
        second.append(cp)
    got2[y, z] = cut[y, z]
    for yy, zz in far:
        pltpu.make_async_remote_copy(src_ref=cut.at[yy, zz], dst_ref=got2.at[yy, zz], send_sem=send2.at[0], recv_sem=recv2.at[yy, zz], device_id=(yy * 8 + g, zz), device_id_type=MESH).wait_recv()
    for part_of in range(2):
        result = got2[2 * part_of, 0]
        for k in range(1, 8):
            result = result + got2[2 * part_of + k // 4, k % 4]
        out[part_of] = result
    for cp in first + second:
        cp.wait_send()


def reduce(part):
    vmem = pl.BlockSpec(memory_space=pltpu.VMEM)
    dma = pltpu.SemaphoreType.DMA
    return pl.pallas_call(
        reduce_kernel,
        out_shape=jax.ShapeDtypeStruct((2, 8, 128), F32),
        in_specs=[vmem],
        out_specs=vmem,
        scratch_shapes=[
            pltpu.VMEM((8, 4, 8, 256), BF16),
            pltpu.VMEM((4, 4, 8, 128), F32),
            pltpu.VMEM((4, 4, 8, 128), F32),
            dma((8,)), dma((8,)), dma((16,)), dma((4, 4)),
        ],
        compiler_params=pltpu.CompilerParams(collective_id=1, has_side_effects=True, vmem_limit_bytes=8 << 20),
        name="reduce",
    )(part)


def body(block_list, block_values, atom_offsets, density, metric_inverse):
    own = block_values.transpose(1, 2, 0, 3).reshape(288, 128)
    bq, bp, vt, dexp, codex, codep, meta, sig = gather(*[pltpu.with_memory_space_constraint(t, pltpu.HBM) for t in (own, block_list.T, atom_offsets, density, metric_inverse)])
    part = contract(codex, codep, meta, sig, bq.reshape(256, 48, 128), bp.reshape(256, 48, 128), vt, dexp)
    sums = reduce(part.reshape(4, 8, 8, 256))
    return sums[0, :6, :48] + sums[1, :6, :48]


def solution(mesh):
    placed = (
        P(("map", "row"), None),
        P(("map", "row"), None, None, None),
        P(),
        P("row", None),
        P("map", "row"),
    )
    return jax.shard_map(
        body, mesh=mesh, in_specs=placed, out_specs=P("map", "row"), check_vma=False
    )
```

```python
import jax
import jax.numpy as jnp
from jax import lax
from jax.experimental import pallas as pl
from jax.experimental.pallas import tpu as pltpu
from jax.sharding import PartitionSpec as P

HI = lax.Precision.HIGHEST
F32, BF16, I32 = jnp.float32, jnp.bfloat16, jnp.int32
NT = (((1,), (1,)), ((), ()))
MESH = pl.DeviceIdType.MESH
GROUP = 32
CHUNK = 16
XROWS = 44
XUN = 11
HN = 48
NB = 32
HU = 2


def iota(shape, axis):
    return lax.broadcasted_iota(I32, shape, axis)


def contract_kernel(codex, codep, meta, sig, bq, bp, vt, dexp, out, xbuf, hbuf, obuf, ebuf, kbuf):
    nf, nh = meta[0, 33], meta[0, 34]
    low_half = iota((8, 128), 1) < 64

    def x_step(step, carry):
        for w in range(XUN):
            ch = XUN * step + w
            src = [codex[0, 8 * ch + u] for u in range(8)]
            rows = jnp.concatenate([bq[s & 255] for s in src], axis=0)
            x = jnp.dot(rows, vt[meta[0, 40 + ch]], preferred_element_type=F32)
            for u in range(8):
                tiles = [x[48 * u + 8 * j:48 * u + 8 * j + 8] for j in range(6)]
                whole = [t[:, :128] for t in tiles]
                half = [jnp.where(low_half, tiles[2 * j][:, 128:], tiles[2 * j + 1][:, 128:]) for j in range(3)]
                xbuf[src[u] >> 8] = jnp.stack(whole + half)
        return carry

    lax.fori_loop(0, (meta[0, 35] + XUN - 1) // XUN, x_step, 0)
    kbuf[...] = jnp.zeros_like(kbuf)
    ebuf[...] = jnp.zeros_like(ebuf)
    lane, sub = iota((8, 128), 1), iota((8, 128), 0)
    low_mask = (lane % 8 == sub) & (lane < 64)
    high_mask = (lane % 8 == sub) & (lane >= 64)
    row, col = iota((8, 256), 0), iota((8, 256), 1)
    even_device = (iota((64, 128), 0) * 0 + meta[0, 36]) == 0
    left_lanes = iota((64, 128), 1) < 64
    none = jnp.zeros((64, 128), BF16)
    def spread(ld, nu_a, lb, nu_b):
        a = dexp[ld, pl.ds(nu_a, 8, stride=0), :]
        b = dexp[lb, pl.ds(nu_b, 8, stride=0), :]
        return jnp.where(low_mask, a, jnp.where(high_mask, b, 0.0))

    def pair(h):
        n = h.shape[0] // 8
        both = jnp.concatenate([h[:, :128].reshape(n, 8, 128), h[:, 128:].reshape(n, 8, 128)], axis=1)
        return both.astype(BF16)

    def group(half, base, cnt):
        def h_pair(t2):
            at, ls = [], []
            for u in range(2):
                t = base + jnp.minimum(2 * t2 + u, cnt - 1)
                code = codep[0, t]
                at.append(code & 255)
                ls.append((code >> 8) & 31)
                ebuf[pl.ds(pl.multiple_of(16 * t2 + 8 * u, 8), 8), :] = (col == 8 * (code >> 13) + row).astype(F32)
            b0, b1 = [jnp.concatenate([bp[k], none[:16]], axis=0) for k in at]
            if not half:
                rhs = jnp.concatenate([jnp.concatenate([b0, none], axis=1), jnp.concatenate([none, b1], axis=1)], axis=0)
                for c in range(0, 192, HN):
                    w = jnp.concatenate([spread(ls[0], nu, ls[1], nu) for nu in range(c, c + HN)], axis=0).astype(BF16)
                    hbuf[c:c + HN, t2] = pair(jnp.dot(w, rhs, preferred_element_type=F32))
            else:
                quads = []
                for b in (b0, b1):
                    wide = b.astype(F32)
                    turned = pltpu.roll(wide, 64, 1)
                    first = jnp.where(even_device, wide, turned)
                    second = jnp.where(even_device, turned, wide)
                    quads.append((jnp.where(left_lanes, first, 0.0).astype(BF16), jnp.where(left_lanes, 0.0, second).astype(BF16)))
                (e0, o0), (e1, o1) = quads
                rhs = jnp.concatenate([jnp.concatenate([p, q], axis=1) for p, q in ((e0, none), (o0, none), (none, e1), (none, o1))], axis=0)
                for c in range(0, 96, HN):
                    w = jnp.concatenate([
                        jnp.concatenate([spread(l, 2 * r, l, 2 * r + 1) for r in range(c, c + HN)], axis=0).astype(BF16)
                        for l in ls], axis=1)
                    hbuf[c:c + HN, t2] = pair(jnp.dot(w, rhs, preferred_element_type=F32))

        def h_step(step, carry):
            for u in range(HU):
                h_pair(HU * step + u)
            return carry

        lax.fori_loop(0, (cnt + 2 * HU - 1) // (2 * HU), h_step, 0)
        depth, first = (3, 6) if half else (6, 0)

        def finish(pairs):
            lanes = max(pairs * 16, 128)
            def chunk(n, k0):
                xs = jnp.concatenate([xbuf[pl.ds(k0, CHUNK), first + j].reshape(CHUNK * 8, 128).astype(BF16) for j in range(depth)], axis=1)
                hs = jnp.concatenate([hbuf[n * depth + j, 0:pairs].reshape(pairs * 16, 128) for j in range(depth)], axis=1)
                o = lax.dot_general(xs, hs, NT, preferred_element_type=F32)
                obuf[pl.ds(pl.multiple_of(8 * k0, 8), CHUNK * 8), 0:pairs * 16] = o

            def n_step(i, carry):
                ends = [meta[0, NB * i + u] for u in range(NB + 1)]
                for u in range(NB):
                    chunk(NB * i + u, ends[u])
                longest = ends[1] - ends[0]
                for u in range(1, NB):
                    longest = jnp.maximum(longest, ends[u + 1] - ends[u])

                @pl.when(longest > CHUNK)
                def _():
                    def more(n, carry):
                        s0, s1 = meta[0, n], meta[0, n + 1]

                        def c_step(c, carry):
                            chunk(n, jnp.minimum(s0 + CHUNK * c, s1 - CHUNK))
                            return carry

                        return lax.fori_loop(1, (s1 - s0 + CHUNK - 1) // CHUNK, c_step, carry)

                    lax.fori_loop(NB * i, NB * i + NB, more, 0)
                return carry

            lax.fori_loop(0, 32 // NB, n_step, 0)
            r = jnp.zeros((256, lanes), F32)
            for k in range(8):
                o = obuf[256 * k:256 * k + 256, 0:lanes]
                high = o.astype(BF16)
                s = sig[:, 256 * k:256 * k + 256]
                r += jnp.dot(s, high, preferred_element_type=F32)
            r = jnp.where(iota((256, lanes), 1) < 8 * cnt, r, 0.0)
            e = ebuf[0:lanes, :].astype(BF16)
            high = r.astype(BF16)
            low = (r - high.astype(F32)).astype(BF16)
            kbuf[...] += jnp.dot(high, e, preferred_element_type=F32) + jnp.dot(low, e, preferred_element_type=F32)

        @pl.when(cnt <= 8)
        def _():
            finish(4)

        @pl.when(cnt > 8)
        def _():
            finish(GROUP // 2)

    for half, base, total in ((False, 0, nf), (True, nf, nh)):
        def g_step(g, carry, half=half, base=base, total=total):
            group(half, base + GROUP * g, jnp.minimum(total - GROUP * g, GROUP))
            return carry

        lax.fori_loop(0, (total + GROUP - 1) // GROUP, g_step, 0)
    out[...] = kbuf[...].T.astype(BF16)


def contract(codex, codep, meta, sig, bq, bp, vt, dexp):
    smem = pl.BlockSpec(memory_space=pltpu.SMEM)
    vmem = pl.BlockSpec(memory_space=pltpu.VMEM)
    return pl.pallas_call(
        contract_kernel,
        out_shape=jax.ShapeDtypeStruct((256, 256), BF16),
        in_specs=[smem] * 3 + [vmem] * 5,
        out_specs=vmem,
        scratch_shapes=[
            pltpu.VMEM((256 + CHUNK, 9, 8, 128), F32),
            pltpu.VMEM((192, GROUP // 2, 16, 128), BF16),
            pltpu.VMEM(((256 + CHUNK) * 8, 256), F32),
            pltpu.VMEM((256, 256), F32),
            pltpu.VMEM((256, 256), F32),
        ],
        compiler_params=pltpu.CompilerParams(vmem_limit_bytes=36 << 20),
        name="contract",
    )(codex, codep, meta, sig, bq, bp, vt, dexp)


ROWS = 288
XDIRECT = True


def place():
    m, z = lax.axis_index("map"), lax.axis_index("row")
    return m, (m // 2) % 4, m // 8, z, m % 2


def at_map(x, y, c):
    return (y * 4 + x) * 2 + c


def greet(devices, between=None):
    barrier = pltpu.get_barrier_semaphore()
    for d in devices:
        pl.semaphore_signal(barrier, inc=1, device_id=d, device_id_type=MESH)
    if between is not None:
        between()
    pl.semaphore_wait(barrier, len(devices))


def tables(nq, nn, whole_block, half_block, row_start, parity, codex, codep, meta, sig):
    g = iota((256, 1), 0)
    wide = iota((256, 256), 1)
    lane = iota((256, 128), 1)

    def column(ref, field):
        rows = []
        for t in range(32):
            c, s, u = t // 16, (t // 4) % 4, t % 4
            rows.append(ref[c, s, u, pl.ds(field, 8, stride=0), :])
        spread = jnp.concatenate(rows, axis=0)
        return jnp.sum(jnp.where(lane == g % 8, spread, 0.0), axis=1, keepdims=True).astype(I32)

    def across(col):
        return jnp.sum(jnp.where(wide == g, col.astype(F32), 0.0), axis=0, keepdims=True).astype(I32)

    def lanes(hit):
        return jnp.sum(hit.astype(F32), axis=1, keepdims=True).astype(I32)

    def rows(hit):
        return jnp.sum(hit.astype(F32), axis=0, keepdims=True).astype(I32)

    def rank(col):
        other = across(col)
        return lanes((other < col) | ((other == col) & (wide < g)))

    def put(where, at, code, rest):
        return rest + jnp.sum(jnp.where(where == at, (code - rest).astype(F32), 0.0), axis=0, keepdims=True).astype(I32)

    first, second, q = column(nq, 0), column(nq, 1), column(nq, 2) - row_start
    by_n = rank(second)
    starts = rows(second < lane)
    sig_at = iota((256, 2048), 1)
    where = jnp.sum(jnp.where(by_n == sig_at // 8, first.astype(F32), 0.0), axis=0, keepdims=True).astype(I32)
    inner = iota((1, 2048), 1) % 8
    target = jnp.where(inner < 6, 6 * where + inner, -1)
    sig[...] = (iota((256, 2048), 0) == target).astype(F32).astype(BF16)
    other = across(q)
    within = lanes((other == q) & (wide < g))
    chunks_row = (rows(q == lane) + 7) // 8
    n16, l16 = iota((16, 128), 0), iota((16, 128), 1)
    ends_col = jnp.sum(jnp.where(l16 <= n16, chunks_row.astype(F32), 0.0), axis=1, keepdims=True).astype(I32)
    lead = jnp.sum(jnp.where(lane < q, chunks_row.astype(F32), 0.0), axis=1, keepdims=True).astype(I32)
    codex[...] = put(8 * lead + within, iota((256, 512), 1), g + by_n * 256, 256 * 256)
    at128 = iota((1, 128), 1)
    chunk_q = jnp.minimum(rows((ends_col <= l16 - 40) & (n16 < 12)), 11)
    total = jnp.sum(chunks_row.astype(F32), axis=1, keepdims=True).astype(I32)
    p = column(nn, 2)
    key = jnp.where(p == whole_block, 0, jnp.where(p == half_block, 1, 2))
    piece = g // 8
    place_of = ((piece // 16) * 16 + (piece % 4) * 4 + (piece // 4) % 4) * 8 + g % 8
    codep[...] = put(rank(key), wide, place_of + column(nn, 1) * 256 + column(nn, 0) * 8192, 0)
    n0, n1 = rows(key == 0), rows(key == 1)
    meta[...] = jnp.where(at128 < 33, starts, jnp.where(at128 == 33, n0, jnp.where(at128 == 34, n1, jnp.where(at128 == 35, total, jnp.where(at128 == 36, parity, jnp.where(at128 < 40, 0, chunk_q))))))


def gather_kernel(own, triples, offsets, dens, v, wide_q, wide_p, vt_out, dexp_out, codex, codep, meta, sig, bq, bp, stage, dall, held, vbuf, spread, s_send, s_z, s_d, s_ax, s_ay, s_as, s_by, s_bx, s_bs, s_loc, nq, nn, nz, s_nz, s_nx, s_ny, s_my, s_mx, s_ns, s_plane):
    m, x, y, z, c = place()
    way = 1 - 2 * c
    o = 1 - c

    def r4(v):
        return lax.rem(v + 8, 4)

    def dev(xx, yy, zz, cc):
        return (at_map(r4(xx), r4(yy), cc), r4(zz))

    sib = dev(x, y, z, o)
    own_piece = bq.at[y, x]
    first = [
        pltpu.make_async_copy(own, bq.at[y, x], s_loc.at[0]),
        pltpu.make_async_copy(dens, dall.at[z], s_loc.at[2]),
        pltpu.make_async_copy(v, held, s_loc.at[3]),
    ]
    for d in first:
        d.start()

    def between():
        r, k = iota((384, 288), 0), iota((384, 288), 1)
        block, j, i = r // 48, (r % 48) // 8, r % 8
        source = jnp.where(i < 6, (i * 6 + j) * 8 + block, -1)
        spread[...] = (k == source).astype(F32).astype(BF16)
        row, lane = iota((8, 128), 0), iota((8, 128), 1)
        tile = jnp.zeros((8, 128), F32)
        for k in range(8):
            a, l, p = offsets[triples[0, k]] // 6, offsets[triples[1, k]] // 6, triples[2, k]
            tile = jnp.where(lane == k, jnp.where(row == 0, a, jnp.where(row == 1, l, p)).astype(F32), tile)
        nq[c, y, x] = tile
        nz[z] = tile
        for d in first[:2]:
            d.wait()

    greet([dev(x + s, y, z, c) for s in (1, 2, 3)] + [dev(x, y + s, z, c) for s in (1, 2, 3)] + [dev(x, y, z + s, c) for s in (1, 2, 3)] + [sib], between)
    sends = []

    def send(src, dst, recv, device):
        n = len(sends)
        d = pltpu.make_async_remote_copy(src_ref=src, dst_ref=dst, send_sem=s_send.at[n], recv_sem=recv, device_id=device, device_id_type=MESH)
        d.start()
        sends.append(d)

    def arrive(dst, recv):
        pltpu.make_async_remote_copy(src_ref=dst, dst_ref=dst, send_sem=s_send.at[0], recv_sem=recv, device_id=sib, device_id_type=MESH).wait_recv()

    def widen(yq, xq, yp, xp):
        two = jnp.concatenate([bq[yq, xq], bp[yp, xp]], axis=1)
        got = jnp.dot(spread[...], two, preferred_element_type=F32).astype(BF16)
        wide_q[c, yq, xq] = got[:, :128]
        wide_p[c, yp, xp] = got[:, 128:]
        send(wide_q.at[c, yq, xq], wide_q.at[c, yq, xq], s_as.at[yq, xq], sib)
        send(wide_p.at[c, yp, xp], wide_p.at[c, yp, xp], s_bs.at[yp, xp], sib)

    peers = (1, 3, 2)

    def to_plane(src, zz, n):
        return pltpu.make_async_remote_copy(src_ref=src, dst_ref=bp.at[y, x], send_sem=s_plane.at[n], recv_sem=s_by.at[y], device_id=dev(x, zz, z, c), device_id_type=MESH)

    for s in peers:
        send(own_piece, stage.at[z], s_z.at[z], dev(x, y, z + s, c))
    for s in peers if XDIRECT else (1, 3):
        send(own_piece, own_piece, s_ax.at[x], dev(x + s, y, z, c))
    for s in (1, 3):
        send(own_piece, own_piece, s_ay.at[y, x], dev(x, y + s, z, c))
    for s in peers:
        send(nz.at[z], nz.at[z], s_nz.at[z], dev(x, y, z + s, c))
        send(nq.at[c, y, x], nq.at[c, y, x], s_nx.at[x], dev(x + s, y, z, c))
    for s in peers:
        send(dall.at[z], dall.at[z], s_d.at[z], dev(x, y, z + s, c))
    @pl.when(z != y)
    def _():
        to_plane(own_piece, z, 0).start()

    keep = pltpu.make_async_copy(own_piece, stage.at[z], s_loc.at[0])
    keep.start()
    for n, s in enumerate(peers):
        zz = r4(z + s)
        arrive(stage.at[zz], s_z.at[zz])

        @pl.when(zz != y)
        def _(zz=zz, n=n):
            to_plane(stage.at[zz], zz, n + 1).start()

    keep.wait()
    for s in peers:
        arrive(nz.at[r4(z + s)], s_nz.at[r4(z + s)])
    nn[c, x, y] = nz[y]
    for s in peers:
        yt = r4(y + s)
        send(nz.at[yt], nn.at[c, x, y], s_my.at[y], dev(x, yt, z, c))
    mine = pltpu.make_async_copy(stage.at[y], bp.at[y, x], s_loc.at[1])
    mine.start()
    for s in (1, 3):
        send(stage.at[y], bp.at[y, x], s_bx.at[y, x], dev(x + s, y, z, c))

    xf, xb, x2 = r4(x - way), r4(x + way), r4(x + 2)
    yf, yb, y2 = r4(y - way), r4(y + way), r4(y + 2)
    for xx in (xf, xb, x2):
        arrive(bq.at[y, xx], s_ax.at[xx])
        if not XDIRECT and xx is xf:
            send(bq.at[y, xx], bq.at[y, xx], s_ax.at[xx], dev(x + way, y, z, c))
        for s in (1, 3):
            send(bq.at[y, xx], bq.at[y, xx], s_ay.at[y, xx], dev(x, y + s, z, c))
    for xx in (xf, xb, x2):
        arrive(nq.at[c, y, xx], s_nx.at[xx])
    for s in peers:
        send(nq.at[c, y], nq.at[c, y], s_ny.at[y], dev(x, y + s, z, c))
    for yy in (yf, yb, y2):
        arrive(bp.at[yy, x], s_by.at[yy])
        for s in (1, 3):
            send(bp.at[yy, x], bp.at[yy, x], s_bx.at[yy, x], dev(x + s, y, z, c))
    for yy in (yf, yb, y2):
        arrive(nn.at[c, x, yy], s_my.at[yy])
    for s in peers:
        send(nn.at[c, x], nn.at[c, x], s_mx.at[x], dev(x + s, y, z, c))
    mine.wait()
    widen(y, x, y, x)
    for xx, yy in ((x, y), (xf, yf), (xb, yb), (x2, y2)):
        arrive(bq.at[yf, xx], s_ay.at[yf, xx])
        send(bq.at[yf, xx], bq.at[yf, xx], s_ay.at[yf, xx], dev(x, y + way, z, c))
        arrive(bp.at[yy, xf], s_bx.at[yy, xf])
        send(bp.at[yy, xf], bp.at[yy, xf], s_bx.at[yy, xf], dev(x + way, y, z, c))
        if xx is not x:
            widen(y, xx, yy, x)
        widen(yf, xx, yy, xf)
    for s in peers:
        arrive(nq.at[c, r4(y + s)], s_ny.at[r4(y + s)])
        arrive(nn.at[c, r4(x + s)], s_mx.at[r4(x + s)])
    send(nq.at[c], nq.at[c], s_ns.at[0], sib)
    send(nn.at[c], nn.at[c], s_ns.at[1], sib)
    first[2].wait()
    parity = lax.rem(m, 2)
    vbuf[0:128] = held[pl.ds(pl.multiple_of(64 * parity, 64), 128), :]
    half = held[pl.ds(pl.multiple_of(128 * (1 - parity), 64), 64), :]
    vbuf[128:192] = half
    vbuf[192:256] = half
    same = (iota((128, 128), 0) == iota((128, 128), 1)).astype(F32).astype(BF16)
    for q in range(12):
        vt_out[q] = lax.dot_general(same, vbuf[:, 128 * q:128 * q + 128], NT, preferred_element_type=F32).astype(BF16)
    for s in peers:
        arrive(dall.at[r4(z + s)], s_d.at[r4(z + s)])
    same = (iota((192, 192), 0) == iota((192, 192), 1)).astype(F32).astype(BF16)
    full = jnp.concatenate([dall[k] for k in range(4)], axis=0)
    turned = lax.dot_general(same, full, NT, preferred_element_type=F32).astype(BF16)
    lam, lane = iota((192, 128), 0), iota((192, 128), 1)
    part = (lane % 64) // 8
    for l in range(32):
        sel = ((lam == 6 * l + part) & (part < 6)).astype(F32).astype(BF16)
        dexp_out[l] = jnp.dot(turned, sel, preferred_element_type=F32)
    arrive(nq.at[o], s_ns.at[0])
    arrive(nn.at[o], s_ns.at[1])
    chip = m // 2
    tables(nq, nn, 3 * chip + 2 * parity, 3 * chip + 1, z * 12, parity, codex, codep, meta, sig)
    for ya, xa in ((yb, xb), (y2, x2)):
        for xx, yy in ((x, y), (xf, yf), (xb, yb), (x2, y2)):
            arrive(bq.at[ya, xx], s_ay.at[ya, xx])
            arrive(bp.at[yy, xa], s_bx.at[yy, xa])
            widen(ya, xx, yy, xa)
    for yy in (y, yf, yb, y2):
        for xx in (x, xf, xb, x2):
            arrive(wide_q.at[o, yy, xx], s_as.at[yy, xx])
            arrive(wide_p.at[o, yy, xx], s_bs.at[yy, xx])
    for n, s in enumerate((0,) + peers):
        zz = r4(z + s)

        @pl.when(zz != y)
        def _(zz=zz, n=n):
            to_plane(own_piece if n == 0 else stage.at[zz], zz, n).wait_send()

    for d in sends:
        d.wait_send()


def gather(own, triples, offsets, dens, v):
    hbm = pl.BlockSpec(memory_space=pltpu.HBM)
    smem = pl.BlockSpec(memory_space=pltpu.SMEM)
    vmem = pl.BlockSpec(memory_space=pltpu.VMEM)
    dma = pltpu.SemaphoreType.DMA
    return pl.pallas_call(
        gather_kernel,
        out_shape=[
            jax.ShapeDtypeStruct((2, 4, 4, 384, 128), BF16),
            jax.ShapeDtypeStruct((2, 4, 4, 384, 128), BF16),
            jax.ShapeDtypeStruct((12, 128, 256), BF16),
            jax.ShapeDtypeStruct((32, 192, 128), F32),
            jax.ShapeDtypeStruct((1, 512), I32),
            jax.ShapeDtypeStruct((1, 256), I32),
            jax.ShapeDtypeStruct((1, 128), I32),
            jax.ShapeDtypeStruct((256, 2048), BF16),
        ],
        in_specs=[hbm, smem, smem, hbm, hbm],
        out_specs=[vmem] * 8,
        scratch_shapes=[
            pltpu.VMEM((4, 4, ROWS, 128), BF16),
            pltpu.VMEM((4, 4, ROWS, 128), BF16),
            pltpu.VMEM((4, ROWS, 128), BF16),
            pltpu.VMEM((4, 48, 192), BF16),
            pltpu.VMEM((192, 1536), BF16),
            pltpu.VMEM((256, 1536), BF16),
            pltpu.VMEM((384, 288), BF16),
            dma((104,)), dma((4,)), dma((4,)), dma((4,)), dma((4, 4)), dma((4, 4)), dma((4,)), dma((4, 4)), dma((4, 4)), dma((4,)),
            pltpu.VMEM((2, 4, 4, 8, 128), F32),
            pltpu.VMEM((2, 4, 4, 8, 128), F32),
            pltpu.VMEM((4, 8, 128), F32),
            dma((4,)), dma((4,)), dma((4,)), dma((4,)), dma((4,)), dma((2,)), dma((4,)),
        ],
        compiler_params=pltpu.CompilerParams(collective_id=0, has_side_effects=True, vmem_limit_bytes=24 << 20),
        name="gather",
    )(own, triples, offsets, dens, v)


def reduce_kernel(part, out, got, cut, got2, send1, recv1, send2, recv2):
    m, x, y, z, c = place()
    g = lax.rem(m, 8)
    near = [(y * 8 + lax.rem(g + d, 8), z) for d in range(1, 8)]
    far = []
    for d in range(1, 16):
        h = lax.rem(y * 4 + z + d, 16)
        far.append((h // 4, lax.rem(h, 4)))
    greet(near + [((yy * 8 + g), zz) for yy, zz in far])
    first = []
    for d in range(1, 8):
        gg = lax.rem(g + d, 8)
        cp = pltpu.make_async_remote_copy(src_ref=part.at[:, gg], dst_ref=got.at[g], send_sem=send1.at[d], recv_sem=recv1.at[g], device_id=near[d - 1], device_id_type=MESH)
        cp.start()
        first.append(cp)
    got[g] = part[:, g]
    cut[...] = jnp.zeros_like(cut)
    for d in range(1, 8):
        gg = lax.rem(g + d, 8)
        pltpu.make_async_remote_copy(src_ref=part.at[:, gg], dst_ref=got.at[gg], send_sem=send1.at[d], recv_sem=recv1.at[gg], device_id=near[0], device_id_type=MESH).wait_recv()
    total = got[0].astype(F32)
    for k in range(1, 8):
        total = total + got[k].astype(F32)
    for zz in range(4):
        cut[:, zz, :, 0:48] = total[:, :, 48 * zz:48 * zz + 48]
    second = []
    for d, (yy, zz) in enumerate(far):
        cp = pltpu.make_async_remote_copy(src_ref=cut.at[yy, zz], dst_ref=got2.at[y, z], send_sem=send2.at[d], recv_sem=recv2.at[y, z], device_id=(yy * 8 + g, zz), device_id_type=MESH)
        cp.start()
        second.append(cp)
    got2[y, z] = cut[y, z]
    for yy, zz in far:
        pltpu.make_async_remote_copy(src_ref=cut.at[yy, zz], dst_ref=got2.at[yy, zz], send_sem=send2.at[0], recv_sem=recv2.at[yy, zz], device_id=(yy * 8 + g, zz), device_id_type=MESH).wait_recv()
    for part_of in range(2):
        result = got2[2 * part_of, 0]
        for k in range(1, 8):
            result = result + got2[2 * part_of + k // 4, k % 4]
        out[part_of] = result
    for cp in first + second:
        cp.wait_send()


def reduce(part):
    vmem = pl.BlockSpec(memory_space=pltpu.VMEM)
    dma = pltpu.SemaphoreType.DMA
    return pl.pallas_call(
        reduce_kernel,
        out_shape=jax.ShapeDtypeStruct((2, 8, 128), F32),
        in_specs=[vmem],
        out_specs=vmem,
        scratch_shapes=[
            pltpu.VMEM((8, 4, 8, 256), BF16),
            pltpu.VMEM((4, 4, 8, 128), F32),
            pltpu.VMEM((4, 4, 8, 128), F32),
            dma((8,)), dma((8,)), dma((16,)), dma((4, 4)),
        ],
        compiler_params=pltpu.CompilerParams(collective_id=1, has_side_effects=True, vmem_limit_bytes=8 << 20),
        name="reduce",
    )(part)


def body(block_list, block_values, atom_offsets, density, metric_inverse):
    own = block_values.transpose(1, 2, 0, 3).reshape(288, 128)
    bq, bp, vt, dexp, codex, codep, meta, sig = gather(*[pltpu.with_memory_space_constraint(t, pltpu.HBM) for t in (own, block_list.T, atom_offsets, density, metric_inverse)])
    part = contract(codex, codep, meta, sig, bq.reshape(256, 48, 128), bp.reshape(256, 48, 128), vt, dexp)
    sums = reduce(part.reshape(4, 8, 8, 256))
    return sums[0, :6, :48] + sums[1, :6, :48]


def solution(mesh):
    placed = (
        P(("map", "row"), None),
        P(("map", "row"), None, None, None),
        P(),
        P("row", None),
        P("map", "row"),
    )
    return jax.shard_map(
        body, mesh=mesh, in_specs=placed, out_specs=P("map", "row"), check_vma=False
    )
```
